32 devices in a mesh: dp: 8 (over y, x, core), seq: 4 (over z).
Axes of the slice: x: 2, y: 2, z: 4, core: 2. Of those that a mesh axis runs over, the one named last changes fastest.
Arguments:
- block_input: float32 [8, 1024, 1536], P('dp', 'seq'), may hold values from -6 to 6
- cotangent: float32 [8, 1024, 1536], P('dp', 'seq'), may hold values from -6 to 6
- norm_gain: float32 [1536], P(('dp', 'seq')), may hold values from 0.5 to 1.5
- in_weight: float32 [1536, 6448], P(('dp', 'seq')), may hold values from -0.15625 to 0.15625
- conv_weight: float32 [4, 3328], P(None, ('dp', 'seq')), may hold values from -3 to 3
- conv_bias: float32 [3328], P(('dp', 'seq')), may hold values from -0.5 to 0.5
- step_bias: float32 [48], replicated, may hold values from -7 to 0.5
- decay_log: float32 [48], replicated, may hold values from -2.5 to -1.5
- skip_gain: float32 [48], replicated, may hold values from 0.5 to 1.5
- gated_gain: float32 [3072], P(('dp', 'seq')), may hold values from 0.5 to 1.5
- out_weight: float32 [1536, 3072], P(('dp', 'seq')), may hold values from -0.109375 to 0.109375
- first_norm_gain: float32 [1536], P(('dp', 'seq')), may hold values from -28 to 28
- second_norm_gain: float32 [1536], P(('dp', 'seq')), may hold values from 16.384 to 163.84
- first_in_weight: float32 [1536, 6448], P(('dp', 'seq')), may hold values from -14 to 14
- second_in_weight: float32 [1536, 6448], P(('dp', 'seq')), may hold values from 4.096 to 40.96
- first_conv_weight: float32 [4, 3328], P(None, ('dp', 'seq')), may hold values from -14 to 14
- second_conv_weight: float32 [4, 3328], P(None, ('dp', 'seq')), may hold values from 4.096 to 40.96
- first_conv_bias: float32 [3328], P(('dp', 'seq')), may hold values from -14 to 14
- second_conv_bias: float32 [3328], P(('dp', 'seq')), may hold values from 4.096 to 40.96
- first_step_bias: float32 [48], replicated, may hold values from -28 to 28
- second_step_bias: float32 [48], replicated, may hold values from 16.384 to 163.84
- first_decay_log: float32 [48], replicated, may hold values from -28 to 28
- second_decay_log: float32 [48], replicated, may hold values from 16.384 to 163.84
- first_skip_gain: float32 [48], replicated, may hold values from -56 to 56
- second_skip_gain: float32 [48], replicated, may hold values from 81.92 to 819.2
- first_gated_gain: float32 [3072], P(('dp', 'seq')), may hold values from -14 to 14
- second_gated_gain: float32 [3072], P(('dp', 'seq')), may hold values from 4.096 to 40.96
- first_out_weight: float32 [1536, 3072], P(('dp', 'seq')), may hold values from -28 to 28
- second_out_weight: float32 [1536, 3072], P(('dp', 'seq')), may hold values from 16.384 to 163.84
Outputs:
- block_output: float32 [8, 1024, 1536], P('dp', 'seq')
- input_grad: float32 [8, 1024, 1536], P('dp', 'seq')
- grad_norm_gain: float32 [1536], P(('dp', 'seq'))
- grad_in_weight: float32 [1536, 6448], P(('dp', 'seq'))
- grad_conv_weight: float32 [4, 3328], P(None, ('dp', 'seq'))
- grad_conv_bias: float32 [3328], P(('dp', 'seq'))
- grad_step_bias: float32 [48], replicated
- grad_decay_log: float32 [48], replicated
- grad_skip_gain: float32 [48], replicated
- grad_gated_gain: float32 [3072], P(('dp', 'seq'))
- grad_out_weight: float32 [1536, 3072], P(('dp', 'seq'))
- new_norm_gain: float32 [1536], P(('dp', 'seq'))
- new_first_norm_gain: float32 [1536], P(('dp', 'seq'))
- new_second_norm_gain: float32 [1536], P(('dp', 'seq'))
- new_in_weight: float32 [1536, 6448], P(('dp', 'seq'))
- new_first_in_weight: float32 [1536, 6448], P(('dp', 'seq'))
- new_second_in_weight: float32 [1536, 6448], P(('dp', 'seq'))
- new_conv_weight: float32 [4, 3328], P(None, ('dp', 'seq'))
- new_first_conv_weight: float32 [4, 3328], P(None, ('dp', 'seq'))
- new_second_conv_weight: float32 [4, 3328], P(None, ('dp', 'seq'))
- new_conv_bias: float32 [3328], P(('dp', 'seq'))
- new_first_conv_bias: float32 [3328], P(('dp', 'seq'))
- new_second_conv_bias: float32 [3328], P(('dp', 'seq'))
- new_step_bias: float32 [48], replicated
- new_first_step_bias: float32 [48], replicated
- new_second_step_bias: float32 [48], replicated
- new_decay_log: float32 [48], replicated
- new_first_decay_log: float32 [48], replicated
- new_second_decay_log: float32 [48], replicated
- new_skip_gain: float32 [48], replicated
- new_first_skip_gain: float32 [48], replicated
- new_second_skip_gain: float32 [48], replicated
- new_gated_gain: float32 [3072], P(('dp', 'seq'))
- new_first_gated_gain: float32 [3072], P(('dp', 'seq'))
- new_second_gated_gain: float32 [3072], P(('dp', 'seq'))
- new_out_weight: float32 [1536, 3072], P(('dp', 'seq'))
- new_first_out_weight: float32 [1536, 3072], P(('dp', 'seq'))
- new_second_out_weight: float32 [1536, 3072], P(('dp', 'seq'))
The draws below stay inside these ranges and needn't reach their ends.
All inputs are finite; a program needn't handle non-finite values.
Results may differ from the reference program's by a relative error of at most 0.00115.
The reference program's roundings to bfloat16 on the way count: a program that leaves them out, or rounds other values in their place, can miss the bound.
Values may be sent and summed in bfloat16 or wider, within the bound.
No kernel may reach another device: no remote copies, remote signals or barrier semaphores. Data moves between devices by JAX's collectives and lax.ppermute only.
A program may use at most 320 MiB of HBM per device.

```python
import math
import jax
import jax.numpy as jnp
from jax import lax

D = 1536
E = 3072
NST = 128
NHEADS = 48
HDIM = 64
CONVW = 4
SPAN = 256
SEQS = 8
LENGTH = 1024
XBC = 3328
PROJ = 6448


def draw_step_bias(key, part):
    slow_key = jax.random.fold_in(key, 11)
    fast_key = jax.random.fold_in(key, 12)
    order_key = jax.random.fold_in(key, 13)
    slow = jax.random.uniform(slow_key, (NHEADS,), jnp.float32, -7.0, -6.0)
    fast = jax.random.uniform(fast_key, (NHEADS,), jnp.float32, -1.0, 0.5)
    order = jax.random.permutation(order_key, NHEADS)
    picked = order < NHEADS // 2
    return jnp.where(picked, fast, slow)


def level_of(own_key, shape, shards, smallest, high):
    level, own = 1.0, jax.random.fold_in(own_key, 6)
    for dim, shards_of in shards:
        steps = jnp.exp(jax.random.uniform(jax.random.fold_in(own, dim), (shards_of,), jnp.float32, smallest / len(shards), high / len(shards)))
        level = level * jnp.repeat(steps, shape[dim] // shards_of).reshape([-1 if axis == dim else 1 for axis in range(len(shape))])
    return level


def bell_draw(rng, dims, scale, limit, cuts=(), kind=jnp.bfloat16):
    result = jax.random.normal(rng, dims, jnp.float32) * scale
    if len(cuts) > 0:
        result = level_of(rng, dims, cuts, -0.22, 0.18) * result
    return jnp.clip(result, min=-limit, max=limit).astype(kind)


def setup_inputs(seed: int = 0) -> dict:
    keys = jax.random.split(jax.random.key(seed), 30)
    return {
        "block_input": bell_draw(keys[0], (SEQS, LENGTH, D), 1.0, 6.0, ((0, 8), (1, 4)), jnp.float32),
        "cotangent": bell_draw(keys[1], (SEQS, LENGTH, D), 1.0, 6.0, ((0, 8), (1, 4)), jnp.float32),
        "norm_gain": jnp.clip(1.0 + 0.1 * jax.random.normal(keys[2], (D,), jnp.float32), 0.5, 1.5),
        "in_weight": bell_draw(keys[3], (D, PROJ), D ** -0.5, 0.15625, ((0, 32),), jnp.float32),
        "conv_weight": bell_draw(keys[4], (CONVW, XBC), CONVW ** -0.5, 3.0, ((1, 32),), jnp.float32),
        "conv_bias": jnp.clip(jax.random.uniform(keys[5], (XBC,), jnp.float32, -0.5, 0.5) * level_of(keys[5], (XBC,), ((0, 32),), -0.4, 0.0), -0.5, 0.5),
        "step_bias": draw_step_bias(jax.random.fold_in(keys[29], 71), 0),
        "decay_log": jnp.clip(jax.random.uniform(keys[7], (NHEADS,), jnp.float32, -2.5, -1.5), -2.5, -1.5),
        "skip_gain": jnp.clip(jax.random.uniform(keys[8], (NHEADS,), jnp.float32, 0.5, 1.5), 0.5, 1.5),
        "gated_gain": jnp.clip(1.0 + 0.1 * jax.random.normal(keys[9], (E,), jnp.float32), 0.5, 1.5),
        "out_weight": bell_draw(keys[10], (D, E), E ** -0.5, 0.109375, ((0, 32),), jnp.float32),
        "first_norm_gain": bell_draw(keys[11], (D,), ((SEQS * LENGTH) ** 0.5 / 20), 28.0, ((0, 32),), jnp.float32),
        "second_norm_gain": jnp.clip(jnp.exp(math.log(163.84) - 2.30258502 * jax.random.uniform(keys[12], (D,), jnp.float32) ** level_of(keys[12], (D,), ((0, 32),), -0.2, 0.2)), 16.384, 163.84),
        "first_in_weight": bell_draw(keys[13], (D, PROJ), ((SEQS * LENGTH) ** 0.5 / 40), 14.0, ((0, 32),), jnp.float32),
        "second_in_weight": jnp.clip(jnp.exp(math.log(40.96) - 2.30258502 * jax.random.uniform(keys[14], (D, PROJ), jnp.float32) ** level_of(keys[14], (D, PROJ), ((0, 32),), -0.2, 0.2)), 4.096, 40.96),
        "first_conv_weight": bell_draw(keys[15], (CONVW, XBC), ((SEQS * LENGTH) ** 0.5 / 40), 14.0, ((1, 32),), jnp.float32),
        "second_conv_weight": jnp.clip(jnp.exp(math.log(40.96) - 2.30258502 * jax.random.uniform(keys[16], (CONVW, XBC), jnp.float32) ** level_of(keys[16], (CONVW, XBC), ((1, 32),), -0.2, 0.2)), 4.096, 40.96),
        "first_conv_bias": bell_draw(keys[17], (XBC,), ((SEQS * LENGTH) ** 0.5 / 40), 14.0, ((0, 32),), jnp.float32),
        "second_conv_bias": jnp.clip(jnp.exp(math.log(40.96) - 2.30258502 * jax.random.uniform(keys[18], (XBC,), jnp.float32) ** level_of(keys[18], (XBC,), ((0, 32),), -0.2, 0.2)), 4.096, 40.96),
        "first_step_bias": bell_draw(keys[19], (NHEADS,), ((SEQS * LENGTH) ** 0.5 / 20), 28.0, (), jnp.float32),
        "second_step_bias": jnp.clip(jnp.exp(jax.random.uniform(keys[20], (NHEADS,), jnp.float32, math.log(16.384), math.log(163.84))), 16.384, 163.84),
        "first_decay_log": bell_draw(keys[21], (NHEADS,), ((SEQS * LENGTH) ** 0.5 / 20), 28.0, (), jnp.float32),
        "second_decay_log": jnp.clip(jnp.exp(jax.random.uniform(keys[22], (NHEADS,), jnp.float32, math.log(16.384), math.log(163.84))), 16.384, 163.84),
        "first_skip_gain": bell_draw(keys[23], (NHEADS,), ((SEQS * LENGTH) ** 0.5 / 10), 56.0, (), jnp.float32),
        "second_skip_gain": jnp.clip(jnp.exp(jax.random.uniform(keys[24], (NHEADS,), jnp.float32, math.log(81.92), math.log(819.2))), 81.92, 819.2),
        "first_gated_gain": bell_draw(keys[25], (E,), ((SEQS * LENGTH) ** 0.5 / 40), 14.0, ((0, 32),), jnp.float32),
        "second_gated_gain": jnp.clip(jnp.exp(math.log(40.96) - 2.30258502 * jax.random.uniform(keys[26], (E,), jnp.float32) ** level_of(keys[26], (E,), ((0, 32),), -0.2, 0.2)), 4.096, 40.96),
        "first_out_weight": bell_draw(keys[27], (D, E), ((SEQS * LENGTH) ** 0.5 / 20), 28.0, ((0, 32),), jnp.float32),
        "second_out_weight": jnp.clip(jnp.exp(math.log(163.84) - 2.30258502 * jax.random.uniform(keys[28], (D, E), jnp.float32) ** level_of(keys[28], (D, E), ((0, 32),), -0.2, 0.2)), 16.384, 163.84),
    }


highest = lax.Precision.HIGHEST
beta_one = 0.9
beta_two = 0.95
adam_step = 10.0
adam_eps = 1e-08
rate_matrix = 0.01
rate_vector = 0.3
weight_decay = 0.1
norm_eps = 1e-05

def rms_scale(values, gain):
    return values * lax.rsqrt(lax.optimization_barrier(jnp.mean(values * values, axis=-1, keepdims=True)) + norm_eps) * gain

def convolve(extended, kernel, offset):
    length = extended.shape[0] - kernel.shape[0] + 1
    total = offset + kernel[0] * extended[0:length]
    for index in range(1, kernel.shape[0]):
        total = total + kernel[index] * extended[index:index + length]
    return jax.nn.silu(total)

def prepare(extended, raw_step, kernel, offset, step_bias, decay_log):
    active = convolve(extended, kernel, offset)
    length = active.shape[0]
    values = active[:, :E].reshape(length, NHEADS, HDIM)
    inject = active[:, E:E + NST]
    readout = active[:, E + NST:]
    delta = jax.nn.softplus(raw_step + step_bias)
    change = -delta * jnp.exp(decay_log)
    return (values, inject, readout, delta, change)

def span_scan(values, inject, readout, delta, change, initial):
    length = values.shape[0]
    blocks = length // SPAN
    causal = jnp.tril(jnp.ones((SPAN, SPAN), dtype=bool))

    def advance(state, block):
        block_values, block_keys, block_queries, block_steps, block_rates = block
        running = jnp.cumsum(block_rates, axis=0).T
        spread = jnp.where(causal[None], running[:, :, None] - running[:, None, :], 0.0)
        decay = jnp.where(causal[None], jnp.exp(spread), 0.0)
        intersection = jnp.dot(block_queries, block_keys.T, precision=highest)
        mixing = decay * intersection[None] * block_steps.T[:, None, :]
        local = jnp.einsum('hts,shp->thp', mixing, block_values, precision=highest)
        carried = jnp.exp(running).T[:, :, None] * jnp.einsum('tn,hpn->thp', block_queries, state, precision=highest)
        tail = jnp.exp(running[:, -1:] - running) * block_steps.T
        fresh = jnp.einsum('hs,shp,sn->hpn', tail, block_values, block_keys, precision=highest)
        state = jnp.exp(running[:, -1])[:, None, None] * state + fresh
        return (state, local + carried)

    def split(array):
        return array.reshape((blocks, SPAN) + array.shape[1:])
    final, outputs = lax.scan(advance, initial, (split(values), split(inject), split(readout), split(delta), split(change)))
    return (outputs.reshape(values.shape), final)

def mixer(projected, kernel, offset, step_bias, decay_log, skip_gain, gated_gain):
    gate = projected[:, :E]
    conv_in = projected[:, E:2 * E + 2 * NST]
    raw_step = projected[:, 2 * E + 2 * NST:]
    extended = jnp.concatenate([jnp.zeros((CONVW - 1, E + 2 * NST), jnp.float32), conv_in], axis=0)
    values, inject, readout, delta, change = prepare(extended, raw_step, kernel, offset, step_bias, decay_log)
    initial = jnp.zeros((NHEADS, HDIM, NST), jnp.float32)
    scanned, final = span_scan(values, inject, readout, delta, change, initial)
    mixed = scanned + skip_gain[None, :, None] * values
    gated = mixed.reshape(values.shape[0], E) * jax.nn.silu(gate)
    return rms_scale(gated, gated_gain)

def adamw_update(param, grad, first, second, rate, decay):
    first_new = beta_one * first + (1.0 - beta_one) * grad
    second_new = beta_two * second + (1.0 - beta_two) * grad * grad
    corrected_first = first_new / (1.0 - beta_one ** adam_step)
    corrected_second = second_new / (1.0 - beta_two ** adam_step)
    param_new = param - rate * (corrected_first / (jnp.sqrt(corrected_second) + adam_eps) + decay * param)
    return (param_new, first_new, second_new)

def lowered(array):
    return lax.optimization_barrier(array.astype(jnp.bfloat16)).astype(jnp.float32)

def reference(block_input, cotangent, norm_gain, in_weight, conv_weight, conv_bias, step_bias, decay_log, skip_gain, gated_gain, out_weight, first_norm_gain, second_norm_gain, first_in_weight, second_in_weight, first_conv_weight, second_conv_weight, first_conv_bias, second_conv_bias, first_step_bias, second_step_bias, first_decay_log, second_decay_log, first_skip_gain, second_skip_gain, first_gated_gain, second_gated_gain, first_out_weight, second_out_weight):
    in_low = in_weight.astype(jnp.bfloat16)
    out_low = out_weight.astype(jnp.bfloat16)
    norm_float = lowered(norm_gain)
    kernel_float = lowered(conv_weight)
    offset_float = lowered(conv_bias)
    gated_float = lowered(gated_gain)

    def one_sequence(totals, pair):
        tokens, upstream = pair
        hidden_float, norm_back = jax.vjp(rms_scale, tokens, norm_float)
        hidden = hidden_float.astype(jnp.bfloat16)
        projected = jnp.dot(hidden, in_low, preferred_element_type=jnp.float32)
        normed, mixer_back = jax.vjp(mixer, projected, kernel_float, offset_float, step_bias, decay_log, skip_gain, gated_float)
        normed_low = normed.astype(jnp.bfloat16)
        output = tokens + jnp.dot(normed_low, out_low.T, preferred_element_type=jnp.float32)
        upstream_low = upstream.astype(jnp.bfloat16)
        out_grad = jnp.dot(upstream_low.T, normed_low, preferred_element_type=jnp.float32)
        normed_grad = jnp.dot(upstream_low, out_low, preferred_element_type=jnp.float32)
        projected_grad, kernel_grad, offset_grad, bias_grad, decay_grad, skip_grad, gated_grad = mixer_back(normed_grad)
        projected_low = projected_grad.astype(jnp.bfloat16)
        in_grad = jnp.dot(hidden.T, projected_low, preferred_element_type=jnp.float32)
        hidden_grad = jnp.dot(projected_low, in_low.T, preferred_element_type=jnp.float32)
        token_grad, gain_grad = norm_back(hidden_grad)
        terms = (gain_grad, in_grad, kernel_grad, offset_grad, bias_grad, decay_grad, skip_grad, gated_grad, out_grad)
        new_totals = tuple((total + term for total, term in zip(totals, terms)))
        return (new_totals, (output, upstream + token_grad))
    start = (jnp.zeros(norm_gain.shape, jnp.float32), jnp.zeros(in_weight.shape, jnp.float32), jnp.zeros(conv_weight.shape, jnp.float32), jnp.zeros(conv_bias.shape, jnp.float32), jnp.zeros(step_bias.shape, jnp.float32), jnp.zeros(decay_log.shape, jnp.float32), jnp.zeros(skip_gain.shape, jnp.float32), jnp.zeros(gated_gain.shape, jnp.float32), jnp.zeros(out_weight.shape, jnp.float32))
    totals, results = lax.scan(one_sequence, start, (block_input, cotangent))
    block_output, input_grad = results
    grad_norm_gain, grad_in_weight, grad_conv_weight, grad_conv_bias, grad_step_bias, grad_decay_log, grad_skip_gain, grad_gated_gain, grad_out_weight = totals
    new_norm_gain, new_first_norm_gain, new_second_norm_gain = adamw_update(norm_gain, grad_norm_gain, first_norm_gain, second_norm_gain, rate_vector, 0.0)
    new_in_weight, new_first_in_weight, new_second_in_weight = adamw_update(in_weight, grad_in_weight, first_in_weight, second_in_weight, rate_matrix, weight_decay)
    new_conv_weight, new_first_conv_weight, new_second_conv_weight = adamw_update(conv_weight, grad_conv_weight, first_conv_weight, second_conv_weight, rate_vector, 0.0)
    new_conv_bias, new_first_conv_bias, new_second_conv_bias = adamw_update(conv_bias, grad_conv_bias, first_conv_bias, second_conv_bias, rate_vector, 0.0)
    new_step_bias, new_first_step_bias, new_second_step_bias = adamw_update(step_bias, grad_step_bias, first_step_bias, second_step_bias, rate_vector, 0.0)
    new_decay_log, new_first_decay_log, new_second_decay_log = adamw_update(decay_log, grad_decay_log, first_decay_log, second_decay_log, rate_vector, 0.0)
    new_skip_gain, new_first_skip_gain, new_second_skip_gain = adamw_update(skip_gain, grad_skip_gain, first_skip_gain, second_skip_gain, rate_vector, 0.0)
    new_gated_gain, new_first_gated_gain, new_second_gated_gain = adamw_update(gated_gain, grad_gated_gain, first_gated_gain, second_gated_gain, rate_vector, 0.0)
    new_out_weight, new_first_out_weight, new_second_out_weight = adamw_update(out_weight, grad_out_weight, first_out_weight, second_out_weight, rate_matrix, weight_decay)
    return (block_output, input_grad, grad_norm_gain, grad_in_weight, grad_conv_weight, grad_conv_bias, grad_step_bias, grad_decay_log, grad_skip_gain, grad_gated_gain, grad_out_weight, new_norm_gain, new_first_norm_gain, new_second_norm_gain, new_in_weight, new_first_in_weight, new_second_in_weight, new_conv_weight, new_first_conv_weight, new_second_conv_weight, new_conv_bias, new_first_conv_bias, new_second_conv_bias, new_step_bias, new_first_step_bias, new_second_step_bias, new_decay_log, new_first_decay_log, new_second_decay_log, new_skip_gain, new_first_skip_gain, new_second_skip_gain, new_gated_gain, new_first_gated_gain, new_second_gated_gain, new_out_weight, new_first_out_weight, new_second_out_weight)
```

```python
import jax
import jax.numpy as jnp
from jax import lax
from jax.experimental import pallas as pl
from jax.experimental.pallas import tpu as pltpu
from jax.sharding import PartitionSpec as P

E = 3072
NST = 128
NHEADS = 48
HDIM = 64
CONVW = 4
SPAN = 256
LANES = 128


low = jnp.bfloat16
highest = lax.Precision.HIGHEST
beta_one = 0.9
beta_two = 0.95
adam_step = 10.0
adam_eps = 1e-08
rate_matrix = 0.01
rate_vector = 0.3
weight_decay = 0.1
norm_eps = 1e-05


def shift(block, axis, distance):
    size = lax.axis_size(axis)
    return lax.ppermute(block, axis, [(i, (i + distance) % size) for i in range(size)])


def step_to(block, axis, distance):
    size = lax.axis_size(axis)
    route = [(i, i + distance) for i in range(size) if 0 <= i + distance < size]
    return lax.ppermute(block, axis, route)


def swap(block, axis, bit):
    return lax.ppermute(block, axis, [(i, i ^ bit) for i in range(lax.axis_size(axis))])


def pick(stacked, index):
    return lax.dynamic_index_in_dim(stacked, index, 0, keepdims=False)


def exchange(stacked, axis):
    size, here = lax.axis_size(axis), lax.axis_index(axis)
    result = stacked
    for turn in range(1, size):
        arrived = shift(pick(stacked, (here + turn) % size), axis, turn)
        result = lax.dynamic_update_index_in_dim(result, arrived, (here + size - turn) % size, 0)
    return result


def exchange_sum(stacked, axis):
    size, here = lax.axis_size(axis), lax.axis_index(axis)
    arrived = [shift(pick(stacked, (here + turn) % size), axis, turn) for turn in range(1, size)]
    total = pick(stacked, here)
    for part in arrived:
        total = total + part
    return total


def gather_line(block, axis):
    size, here = lax.axis_size(axis), lax.axis_index(axis)
    up, down = [block], [block]
    for turn in range(1, size):
        up.append(step_to(up[-1], axis, 1))
        down.append(step_to(down[-1], axis, -1))
    result = jnp.zeros((size,) + block.shape, block.dtype)
    result = lax.dynamic_update_index_in_dim(result, block, here, 0)
    for turn in range(1, size):
        arrived = up[turn] + down[size - turn]
        result = lax.dynamic_update_index_in_dim(result, arrived, (here + size - turn) % size, 0)
    return result


def gather_direct(block, axis):
    size, here = lax.axis_size(axis), lax.axis_index(axis)
    arrived = [block] + [shift(block, axis, turn) for turn in range(1, size)]
    result = jnp.stack(arrived)
    return jnp.take(result, (here + size - jnp.arange(size)) % size, axis=0)


def sum_direct(block, axis):
    arrived = [shift(block, axis, turn) for turn in range(1, lax.axis_size(axis))]
    total = block
    for part in arrived:
        total = total + part
    return total


def gather_bits(block, axis):
    here = lax.axis_index(axis)
    result, bit = block[None], 1
    while bit < lax.axis_size(axis):
        other = swap(result, axis, bit)
        upper = (here & bit) > 0
        result = jnp.concatenate(
            [jnp.where(upper, other, result), jnp.where(upper, result, other)], axis=0
        )
        bit *= 2
    return result


def scatter_bits(stacked, axis):
    here, size = lax.axis_index(axis), lax.axis_size(axis)
    bit = 1
    rest = stacked
    while bit < size:
        pairs = rest.reshape((rest.shape[0] // 2, 2) + rest.shape[1:])
        own = (here & bit) // bit
        keep = lax.dynamic_index_in_dim(pairs, own, 1, keepdims=False)
        send = lax.dynamic_index_in_dim(pairs, 1 - own, 1, keepdims=False)
        rest = keep + swap(send, axis, bit)
        bit *= 2
    return rest[0]


def halves(value):
    high = value.astype(low)
    return high, (value - high.astype(jnp.float32)).astype(low)


def product(left, right, right_dim=0):
    dims = (((1,), (right_dim,)), ((), ()))

    def one(a, b):
        return lax.dot_general(a, b, dims, preferred_element_type=jnp.float32)

    return one(left[0], right[0]) + (one(left[0], right[1]) + one(left[1], right[0]))


def exact_dot(left, right):
    return jnp.dot(left, right, precision=highest, preferred_element_type=jnp.float32)


def softplus(value):
    small = jnp.exp(-jnp.abs(value))
    ratio = small / (2.0 + small)
    square = ratio * ratio
    series = jnp.full_like(square, 1.0 / 17.0)
    for power in (15, 13, 11, 9, 7, 5, 3, 1):
        series = series * square + 1.0 / power
    return jnp.maximum(value, 0.0) + 2.0 * ratio * series


def lane_of_head(pair, transposed=False):
    shape = (LANES, LANES)
    head = lax.broadcasted_iota(jnp.int32, shape, 1 if transposed else 0)
    lane = lax.broadcasted_iota(jnp.int32, shape, 0 if transposed else 1)
    return (head == 2 * pair + lane // HDIM).astype(jnp.float32)


def taps_of(extended, size, kernel, offset):
    total = offset + kernel[0:1] * extended[pl.ds(8 - CONVW + 1, size), :]
    for index in range(1, CONVW):
        total = total + kernel[index : index + 1] * extended[pl.ds(8 - CONVW + 1 + index, size), :]
    return total


def step_sizes(raw, heads):
    delta = softplus(raw + heads[0:1])
    change = -delta * jnp.exp(heads[1:2])
    size = raw.shape[0]
    below = lax.broadcasted_iota(jnp.int32, (size, size), 0) >= lax.broadcasted_iota(jnp.int32, (size, size), 1)
    return delta, change, exact_dot(below.astype(jnp.float32), change)


def forward_kernel(
    z_ref, x_ref, shared_ref, step_ref, chan_ref, shared_chan_ref, head_ref,
    gated_ref, mixed_ref, state_ref, square_ref,
    tails, shared_tail, extended, shared_extended, meet, read_high, read_low, keys_high, keys_low,
    delta_all, run_all, run_rows, states,
):
    chunk, pair = pl.program_id(0), pl.program_id(1)
    size = x_ref.shape[0]

    @pl.when(pair == 0)
    def _():
        @pl.when(chunk == 0)
        def _():
            shared_tail[...] = jnp.zeros_like(shared_tail)
            tails[...] = jnp.zeros_like(tails)
            states[...] = jnp.zeros_like(states)

        shared_extended[0:8, :] = shared_tail[...]
        shared_extended[8:, :] = shared_ref[...]
        shared_tail[...] = shared_ref[size - 8 :, :]
        pre = taps_of(shared_extended, size, shared_chan_ref[...], shared_chan_ref[4:5, :])
        active = pre * jax.nn.sigmoid(pre)
        keys, read = halves(active[:, :NST]), halves(active[:, NST:])
        meet[...] = product(read, keys, 1)
        read_high[...], read_low[...] = read
        keys_high[...], keys_low[...] = halves(active[:, :NST].T)
        delta, _, running = step_sizes(step_ref[...], head_ref[...])
        delta_all[...] = delta
        run_all[...] = running
        run_rows[...] = running.T
        square_ref[...] = jnp.zeros_like(square_ref)

    chan = chan_ref[...]
    extended[0:8, :] = tails[pair]
    extended[8:, :] = x_ref[...]
    tails[pair] = x_ref[size - 8 :, :]
    pre = taps_of(extended, size, chan, chan[4:5])
    values = pre * jax.nn.sigmoid(pre)
    lanes = lane_of_head(pair)
    delta = exact_dot(delta_all[...], lanes)
    running = exact_dot(run_all[...], lanes)
    stepped = delta * values
    causal = lax.broadcasted_iota(jnp.int32, (size, size), 0) >= lax.broadcasted_iota(jnp.int32, (size, size), 1)
    locals_ = []
    for side in range(2):
        column = running[:, side * HDIM : side * HDIM + 1]
        row = run_rows[pl.ds(2 * pair + side, 1), :]
        decay = jnp.exp(jnp.where(causal, column - row, -1e30))
        mixing = halves(decay * meet[...])
        locals_.append(product(mixing, halves(stepped[:, side * HDIM : (side + 1) * HDIM])))
    state = states[pair]
    state_ref[0, 0] = state
    carried = product((read_high[...], read_low[...]), halves(state))
    scanned = jnp.concatenate(locals_, axis=1) + jnp.exp(running) * carried
    last = running[size - 1 :, :]
    tail = halves(stepped * jnp.exp(last - running))
    states[pair] = jnp.exp(last) * state + product((keys_high[...], keys_low[...]), tail)
    mixed = scanned + chan[5:6] * values
    z = z_ref[...]
    gated = mixed * (z * jax.nn.sigmoid(z))
    mixed_ref[...] = mixed
    gated_ref[...] = gated
    square_ref[...] += gated * gated


def backward_kernel(
    z_ref, x_ref, x_before_ref, shared_ref, shared_before_ref, step_ref, chan_ref, shared_chan_ref, head_ref,
    gated_ref, mixed_ref, up_ref, scale_ref, pull_ref, state_ref, state_after_ref,
    z_grad_ref, x_grad_ref, shared_grad_ref, step_grad_ref, chan_grad_ref, shared_chan_grad_ref, head_grad_ref,
    heads_after, shared_after, extended, shared_extended, later, shared_later, shared_pre,
    meet, read_high, read_low, keys_high, keys_low, read_rows_high, read_rows_low,
    delta_all, change_all, run_all, run_rows, meet_grad, keys_grad, read_grad, run_grad, delta_grad, last_grad, state_grads,
):
    turn, pair = pl.program_id(0), pl.program_id(1)
    pairs = pl.num_programs(1)
    chunk = pl.num_programs(0) - 1 - turn
    size = x_ref.shape[0]
    first = chunk == 0

    @pl.when(pair == 0)
    def _():
        @pl.when(turn == 0)
        def _():
            heads_after[...] = jnp.zeros_like(heads_after)
            shared_after[...] = jnp.zeros_like(shared_after)
            state_grads[...] = jnp.zeros_like(state_grads)
            chan_grad_ref[...] = jnp.zeros_like(chan_grad_ref)
            shared_chan_grad_ref[...] = jnp.zeros_like(shared_chan_grad_ref)
            head_grad_ref[...] = jnp.zeros_like(head_grad_ref)

        shared_extended[0:8, :] = jnp.where(first, 0.0, shared_before_ref[...])
        shared_extended[8:, :] = shared_ref[...]
        pre = taps_of(shared_extended, size, shared_chan_ref[...], shared_chan_ref[4:5, :])
        shared_pre[...] = pre
        active = pre * jax.nn.sigmoid(pre)
        keys, read = halves(active[:, :NST]), halves(active[:, NST:])
        meet[...] = product(keys, read, 1)
        read_high[...], read_low[...] = read
        keys_high[...], keys_low[...] = keys
        read_rows_high[...], read_rows_low[...] = halves(active[:, NST:].T)
        delta, change, running = step_sizes(step_ref[...], head_ref[...])
        delta_all[...] = delta
        change_all[...] = change
        run_all[...] = running
        run_rows[...] = running.T
        meet_grad[...] = jnp.zeros_like(meet_grad)
        keys_grad[...] = jnp.zeros_like(keys_grad)
        read_grad[...] = jnp.zeros_like(read_grad)
        run_grad[...] = jnp.zeros_like(run_grad)
        delta_grad[...] = jnp.zeros_like(delta_grad)
        last_grad[...] = jnp.zeros_like(last_grad)

    chan = chan_ref[...]
    extended[0:8, :] = jnp.where(first, 0.0, x_before_ref[...])
    extended[8:, :] = x_ref[...]
    pre = taps_of(extended, size, chan, chan[4:5])
    gain = jax.nn.sigmoid(pre)
    values = pre * gain
    lanes = lane_of_head(pair)
    delta = exact_dot(delta_all[...], lanes)
    running = exact_dot(run_all[...], lanes)
    stepped = delta * values

    z, gated, mixed, up, scale = z_ref[...], gated_ref[...], mixed_ref[...], up_ref[...], scale_ref[...]
    z_gain = jax.nn.sigmoid(z)
    gated_grad = up * chan[6:7] * scale - gated * pull_ref[...]
    mix_grad = gated_grad * (z * z_gain)
    z_grad_ref[...] = (gated_grad * mixed * (z_gain * (1.0 + z * (1.0 - z_gain)))).astype(z_grad_ref.dtype)

    last = running[size - 1 :, :]
    fall = jnp.exp(last - running)
    rise = jnp.exp(running)
    state, state_grad = state_ref[0, 0], state_grads[pair]
    state_halves, state_grad_halves = halves(state), halves(state_grad)
    keys = (keys_high[...], keys_low[...])
    stepped_grad = fall * product(keys, state_grad_halves)
    keys_grad[...] += product(halves(stepped * fall), state_grad_halves, 1)
    risen = halves(mix_grad * rise)
    read_grad[...] += product(risen, state_halves, 1)
    ended = jnp.sum(state_grad * state_after_ref[0, 0], axis=0, keepdims=True)
    state_grads[pair] = jnp.exp(last) * state_grad + product((read_rows_high[...], read_rows_low[...]), risen)

    causal = lax.broadcasted_iota(jnp.int32, (size, size), 0) <= lax.broadcasted_iota(jnp.int32, (size, size), 1)
    parts = []
    for side in range(2):
        own = slice(side * HDIM, (side + 1) * HDIM)
        column = running[:, side * HDIM : side * HDIM + 1]
        row = run_rows[pl.ds(2 * pair + side, 1), :]
        decay = jnp.exp(jnp.where(causal, row - column, -1e30))
        mixing = halves(decay * meet[...])
        grad_halves = halves(mix_grad[:, own])
        parts.append(product(mixing, grad_halves))
        meet_grad[...] += decay * product(halves(stepped[:, own]), grad_halves, 1)
    stepped_grad = stepped_grad + jnp.concatenate(parts, axis=1)
    to_head = lane_of_head(pair, transposed=True)
    scanned = mixed - chan[5:6] * values
    run_grad[...] += exact_dot(mix_grad * scanned - stepped * stepped_grad, to_head)
    delta_grad[...] += exact_dot(values * stepped_grad, to_head)
    last_grad[0:1, :] += exact_dot(jnp.broadcast_to(ended, (8, LANES)), to_head)[0:1]

    values_grad = chan[5:6] * mix_grad + delta * stepped_grad
    pre_grad = values_grad * (gain * (1.0 + pre * (1.0 - gain)))
    later[0:size, :] = pre_grad
    later[size:, :] = heads_after[pair]
    heads_after[pair] = pre_grad[0:8]
    x_grad = chan[0:1] * later[pl.ds(CONVW - 1, size), :]
    for index in range(1, CONVW):
        x_grad = x_grad + chan[index : index + 1] * later[pl.ds(CONVW - 1 - index, size), :]
    x_grad_ref[...] = x_grad.astype(x_grad_ref.dtype)
    for index in range(CONVW):
        seen = extended[pl.ds(8 - CONVW + 1 + index, size), :]
        chan_grad_ref[pair, index : index + 1, :] += jnp.sum(pre_grad * seen, axis=0, keepdims=True)
    chan_grad_ref[pair, 4:5, :] += jnp.sum(pre_grad, axis=0, keepdims=True)
    chan_grad_ref[pair, 5:6, :] += jnp.sum(mix_grad * values, axis=0, keepdims=True)
    chan_grad_ref[pair, 6:7, :] += jnp.sum(up * gated * scale, axis=0, keepdims=True)

    @pl.when(pair == pairs - 1)
    def _():
        meet_halves = halves(meet_grad[...])
        keys_all = keys_grad[...] + product(meet_halves, (read_high[...], read_low[...]))
        read_all = read_grad[...] + product(halves(meet_grad[...].T), (keys_high[...], keys_low[...]))
        pre_s = shared_pre[...]
        gain_s = jax.nn.sigmoid(pre_s)
        chan_s = shared_chan_ref[...]
        grad_s = jnp.concatenate([keys_all, read_all], axis=1) * (gain_s * (1.0 + pre_s * (1.0 - gain_s)))
        shared_later[0:size, :] = grad_s
        shared_later[size:, :] = shared_after[...]
        shared_after[...] = grad_s[0:8]
        out = chan_s[0:1] * shared_later[pl.ds(CONVW - 1, size), :]
        for index in range(1, CONVW):
            out = out + chan_s[index : index + 1] * shared_later[pl.ds(CONVW - 1 - index, size), :]
        shared_grad_ref[...] = out
        for index in range(CONVW):
            seen = shared_extended[pl.ds(8 - CONVW + 1 + index, size), :]
            shared_chan_grad_ref[index : index + 1, :] += jnp.sum(grad_s * seen, axis=0, keepdims=True)
        shared_chan_grad_ref[4:5, :] += jnp.sum(grad_s, axis=0, keepdims=True)

        above = lax.broadcasted_iota(jnp.int32, (size, size), 0) <= lax.broadcasted_iota(jnp.int32, (size, size), 1)
        change_grad = exact_dot(above.astype(jnp.float32), run_grad[...]) + last_grad[0:1, :]
        rate = jnp.exp(head_ref[1:2, :])
        raw = step_ref[...] + head_ref[0:1, :]
        raw_grad = (delta_grad[...] - change_grad * rate) * jax.nn.sigmoid(raw)
        step_grad_ref[...] = raw_grad.astype(step_grad_ref.dtype)
        head_grad_ref[0:1, :] += jnp.sum(raw_grad, axis=0, keepdims=True)
        head_grad_ref[1:2, :] += jnp.sum(change_grad * change_all[...], axis=0, keepdims=True)


def run_forward(projected, chan, shared_chan, head_rows):
    length, wide = projected.shape[0], chan.shape[1]
    chunks, pairs = length // SPAN, wide // LANES
    f32 = jnp.float32
    at = 2 * pairs
    block = pl.BlockSpec((SPAN, LANES), lambda c, p: (c, p))
    return pl.pallas_call(
        forward_kernel,
        grid=(chunks, pairs),
        in_specs=[
            block,
            pl.BlockSpec((SPAN, LANES), lambda c, p: (c, pairs + p)),
            pl.BlockSpec((SPAN, 2 * NST), lambda c, p: (c, at // 2)),
            pl.BlockSpec((SPAN, LANES), lambda c, p: (c, at + 2)),
            pl.BlockSpec((8, LANES), lambda c, p: (0, p)),
            pl.BlockSpec((8, 2 * NST), lambda c, p: (0, 0)),
            pl.BlockSpec((8, LANES), lambda c, p: (0, 0)),
        ],
        out_specs=[
            block,
            block,
            pl.BlockSpec((1, 1, NST, LANES), lambda c, p: (c, p, 0, 0)),
            pl.BlockSpec((SPAN, LANES), lambda c, p: (c, 0)),
        ],
        out_shape=[
            jax.ShapeDtypeStruct((length, wide), f32),
            jax.ShapeDtypeStruct((length, wide), f32),
            jax.ShapeDtypeStruct((chunks, pairs, NST, LANES), f32),
            jax.ShapeDtypeStruct((length, LANES), f32),
        ],
        scratch_shapes=[
            pltpu.VMEM((pairs, 8, LANES), f32),
            pltpu.VMEM((8, 2 * NST), f32),
            pltpu.VMEM((SPAN + 8, LANES), f32),
            pltpu.VMEM((SPAN + 8, 2 * NST), f32),
            pltpu.VMEM((SPAN, SPAN), f32),
            pltpu.VMEM((SPAN, NST), low),
            pltpu.VMEM((SPAN, NST), low),
            pltpu.VMEM((NST, SPAN), low),
            pltpu.VMEM((NST, SPAN), low),
            pltpu.VMEM((SPAN, LANES), f32),
            pltpu.VMEM((SPAN, LANES), f32),
            pltpu.VMEM((LANES, SPAN), f32),
            pltpu.VMEM((pairs, NST, LANES), f32),
        ],
        name="mixer_forward",
    )(projected, projected, projected, projected, chan, shared_chan, head_rows)


def run_backward(projected, chan, shared_chan, head_rows, gated, mixed, up, scale, pull, states):
    length, wide = projected.shape[0], chan.shape[1]
    chunks, pairs = length // SPAN, wide // LANES
    f32 = jnp.float32
    at, lines = 2 * pairs, SPAN // 8
    back = lambda c: chunks - 1 - c
    block = pl.BlockSpec((SPAN, LANES), lambda c, p: (back(c), p))
    column = pl.BlockSpec((SPAN, 1), lambda c, p: (back(c), 0))
    before = lambda c: jnp.maximum(back(c) * lines - 1, 0)
    return pl.pallas_call(
        backward_kernel,
        grid=(chunks, pairs),
        in_specs=[
            block,
            pl.BlockSpec((SPAN, LANES), lambda c, p: (back(c), pairs + p)),
            pl.BlockSpec((8, LANES), lambda c, p: (before(c), pairs + p)),
            pl.BlockSpec((SPAN, 2 * NST), lambda c, p: (back(c), at // 2)),
            pl.BlockSpec((8, 2 * NST), lambda c, p: (before(c), at // 2)),
            pl.BlockSpec((SPAN, LANES), lambda c, p: (back(c), at + 2)),
            pl.BlockSpec((8, LANES), lambda c, p: (0, p)),
            pl.BlockSpec((8, 2 * NST), lambda c, p: (0, 0)),
            pl.BlockSpec((8, LANES), lambda c, p: (0, 0)),
            block,
            block,
            block,
            column,
            column,
            pl.BlockSpec((1, 1, NST, LANES), lambda c, p: (back(c), p, 0, 0)),
            pl.BlockSpec((1, 1, NST, LANES), lambda c, p: (jnp.minimum(back(c) + 1, chunks - 1), p, 0, 0)),
        ],
        out_specs=[
            block,
            block,
            pl.BlockSpec((SPAN, 2 * NST), lambda c, p: (back(c), 0)),
            pl.BlockSpec((SPAN, LANES), lambda c, p: (back(c), 0)),
            pl.BlockSpec((pairs, 8, LANES), lambda c, p: (0, 0, 0)),
            pl.BlockSpec((8, 2 * NST), lambda c, p: (0, 0)),
            pl.BlockSpec((8, LANES), lambda c, p: (0, 0)),
        ],
        out_shape=[
            jax.ShapeDtypeStruct((length, wide), low),
            jax.ShapeDtypeStruct((length, wide), low),
            jax.ShapeDtypeStruct((length, 2 * NST), f32),
            jax.ShapeDtypeStruct((length, LANES), low),
            jax.ShapeDtypeStruct((pairs, 8, LANES), f32),
            jax.ShapeDtypeStruct((8, 2 * NST), f32),
            jax.ShapeDtypeStruct((8, LANES), f32),
        ],
        scratch_shapes=[
            pltpu.VMEM((pairs, 8, LANES), f32),
            pltpu.VMEM((8, 2 * NST), f32),
            pltpu.VMEM((SPAN + 8, LANES), f32),
            pltpu.VMEM((SPAN + 8, 2 * NST), f32),
            pltpu.VMEM((SPAN + 8, LANES), f32),
            pltpu.VMEM((SPAN + 8, 2 * NST), f32),
            pltpu.VMEM((SPAN, 2 * NST), f32),
            pltpu.VMEM((SPAN, SPAN), f32),
            pltpu.VMEM((SPAN, NST), low),
            pltpu.VMEM((SPAN, NST), low),
            pltpu.VMEM((SPAN, NST), low),
            pltpu.VMEM((SPAN, NST), low),
            pltpu.VMEM((NST, SPAN), low),
            pltpu.VMEM((NST, SPAN), low),
            pltpu.VMEM((SPAN, LANES), f32),
            pltpu.VMEM((SPAN, LANES), f32),
            pltpu.VMEM((SPAN, LANES), f32),
            pltpu.VMEM((LANES, SPAN), f32),
            pltpu.VMEM((SPAN, SPAN), f32),
            pltpu.VMEM((SPAN, NST), f32),
            pltpu.VMEM((SPAN, NST), f32),
            pltpu.VMEM((SPAN, LANES), f32),
            pltpu.VMEM((SPAN, LANES), f32),
            pltpu.VMEM((8, LANES), f32),
            pltpu.VMEM((pairs, NST, LANES), f32),
        ],
        name="mixer_backward",
    )(
        projected, projected, projected, projected, projected, projected, chan, shared_chan, head_rows,
        gated, mixed, up, scale, pull, states, states,
    )


def adamw_update(param, grad, first, second, rate, decay):
    first_new = beta_one * first + (1.0 - beta_one) * grad
    second_new = beta_two * second + (1.0 - beta_two) * grad * grad
    corrected_first = first_new / (1.0 - beta_one**adam_step)
    corrected_second = second_new / (1.0 - beta_two**adam_step)
    param_new = param - rate * (
        corrected_first / (jnp.sqrt(corrected_second) + adam_eps) + decay * param
    )
    return (param_new, first_new, second_new)


def dot(left, right):
    return jnp.dot(left, right, preferred_element_type=jnp.float32)


def body(
    block_input,
    cotangent,
    norm_gain,
    in_weight,
    conv_weight,
    conv_bias,
    step_bias,
    decay_log,
    skip_gain,
    gated_gain,
    out_weight,
    first_norm_gain,
    second_norm_gain,
    first_in_weight,
    second_in_weight,
    first_conv_weight,
    second_conv_weight,
    first_conv_bias,
    second_conv_bias,
    first_step_bias,
    second_step_bias,
    first_decay_log,
    second_decay_log,
    first_skip_gain,
    second_skip_gain,
    first_gated_gain,
    second_gated_gain,
    first_out_weight,
    second_out_weight,
):
    ranks, rank = lax.axis_size("seq"), lax.axis_index("seq")
    groups = lax.axis_size("dp")
    devices = ranks * groups
    wide, heads = E // ranks, NHEADS // ranks
    rows = in_weight.shape[0]
    width = rows * devices
    taps = conv_bias.shape[0]
    channels = taps * devices
    tail_pad = LANES - heads
    columns = 2 * wide + 2 * NST + LANES

    in_low = in_weight.astype(low)
    out_low = out_weight.astype(low)

    def of_rank(j):
        return jnp.concatenate(
            [
                in_low[:, j * wide : (j + 1) * wide],
                in_low[:, E + j * wide : E + (j + 1) * wide],
                in_low[:, 2 * E : 2 * E + 2 * NST],
                in_low[:, 2 * E + 2 * NST + j * heads : 2 * E + 2 * NST + (j + 1) * heads],
                jnp.zeros((rows, tail_pad), low),
            ],
            axis=1,
        )

    in_parts = jnp.stack([of_rank(j) for j in range(ranks)])
    in_rows = exchange(in_parts, "seq").reshape(ranks * rows, columns)
    in_full = lax.all_gather(in_rows, "dp", axis=0, tiled=True)
    out_parts = jnp.stack([out_low[:, j * wide : (j + 1) * wide] for j in range(ranks)])
    out_rows = exchange(out_parts, "seq").reshape(ranks * rows, wide)
    out_full = lax.all_gather(out_rows, "dp", axis=0, tiled=True)

    packed = jnp.concatenate(
        [norm_gain, conv_weight.reshape(-1), conv_bias, gated_gain]
    ).astype(low).astype(jnp.float32)
    gains = gated_gain.shape[0]
    filled = packed.shape[0]
    lines = -(-filled // LANES)
    packed = jnp.pad(packed, (0, lines * LANES - filled)).reshape(lines, LANES)
    small = gather_bits(gather_direct(packed, "seq"), "dp")
    small = small.reshape(devices, lines * LANES)
    norm_float = small[:, :rows].reshape(-1)
    kernel_float = small[:, rows : rows + CONVW * taps].reshape(devices, CONVW, taps)
    kernel_float = kernel_float.transpose(1, 0, 2).reshape(CONVW, channels)
    offset_float = small[:, rows + CONVW * taps : rows + (CONVW + 1) * taps].reshape(-1)
    gated_float = small[:, rows + (CONVW + 1) * taps : filled].reshape(-1)
    kernel_own = lax.dynamic_slice_in_dim(kernel_float, rank * wide, wide, 1)
    offset_own = lax.dynamic_slice_in_dim(offset_float, rank * wide, wide, 0)
    gated_own = lax.dynamic_slice_in_dim(gated_float, rank * wide, wide, 0)
    bias_own = lax.dynamic_slice_in_dim(step_bias, rank * heads, heads, 0)
    decay_own = lax.dynamic_slice_in_dim(decay_log, rank * heads, heads, 0)
    skip_own = lax.dynamic_slice_in_dim(skip_gain, rank * heads, heads, 0)

    tokens, upstream = block_input[0], cotangent[0]
    span = tokens.shape[0]
    length = span * ranks
    inverse = lax.rsqrt(jnp.mean(tokens * tokens, axis=-1, keepdims=True) + norm_eps)
    hidden_own = (tokens * inverse * norm_float).astype(low)
    hidden = gather_line(hidden_own, "seq").reshape(length, width)
    upstream_low = gather_line(upstream.astype(low), "seq").reshape(length, width)

    projected = dot(hidden, in_full)
    none = jnp.zeros((1, wide), jnp.float32)
    chan = jnp.concatenate(
        [kernel_own, offset_own[None], jnp.repeat(skip_own, HDIM)[None], gated_own[None], none], axis=0
    )
    shared_chan = jnp.concatenate(
        [kernel_float[:, E:], offset_float[None, E:], jnp.zeros((3, 2 * NST), jnp.float32)], axis=0
    )
    head_rows = jnp.pad(jnp.stack([bias_own, decay_own]), ((0, 6), (0, tail_pad)))
    gated, mixed, states, squares = run_forward(projected, chan, shared_chan, head_rows)
    normed_grad = dot(upstream_low, out_full)
    weighted = normed_grad * gated_own
    sums = jnp.stack([jnp.sum(squares, axis=1), jnp.sum(weighted * gated, axis=1)])
    sums = sum_direct(sums.reshape(2 * length // LANES, LANES), "seq").reshape(2, length)
    scale = lax.rsqrt(sums[0] / E + norm_eps)[:, None]
    normed_low = (gated * scale * gated_own).astype(low)
    out_part = dot(normed_low, out_full.T)
    branch = exchange_sum(out_part.reshape(ranks, span, width), "seq")
    block_output = (tokens + branch)[None]

    out_grad_part = dot(upstream_low.T, normed_low)
    out_grad_rows = lax.psum_scatter(out_grad_part, "dp", scatter_dimension=0, tiled=True)
    out_grad_parts = exchange(out_grad_rows.reshape(ranks, rows, wide), "seq")
    grad_out_weight = jnp.concatenate([out_grad_parts[j] for j in range(ranks)], axis=1)

    pull = scale * scale * scale * (sums[1] / E)[:, None]
    gate_low, conv_low, shared_grad, step_low, chan_grad, shared_chan_grad, head_grad = run_backward(
        projected, chan, shared_chan, head_rows, gated, mixed, normed_grad, scale, pull, states
    )
    chan_grad = chan_grad.transpose(1, 0, 2).reshape(8, wide)
    kernel_grad, offset_grad, gated_grad = chan_grad[:CONVW], chan_grad[4], chan_grad[6]
    skip_grad = jnp.sum(chan_grad[5].reshape(heads, HDIM), axis=1)
    kernel_shared_grad, offset_shared_grad = shared_chan_grad[:CONVW], shared_chan_grad[4]
    bias_grad, decay_grad = head_grad[0, :heads], head_grad[1, :heads]

    shared_own = exchange_sum(shared_grad.reshape(ranks, span, 2 * NST), "seq").astype(low)
    projected_low = jnp.concatenate([gate_low, conv_low], axis=1)
    hidden_part = dot(projected_low, in_full[:, : 2 * wide].T) + dot(step_low, in_full[:, 2 * wide + 2 * NST :].T)
    hidden_grad = exchange_sum(hidden_part.reshape(ranks, span, width), "seq")
    hidden_grad = hidden_grad + dot(shared_own, in_full[:, 2 * wide : 2 * wide + 2 * NST].T)

    in_grad_part = jnp.concatenate(
        [dot(hidden.T, projected_low), dot(hidden_own.T, shared_own), dot(hidden.T, step_low)], axis=1
    )
    in_grad_rows = lax.psum_scatter(in_grad_part, "dp", scatter_dimension=0, tiled=True)
    in_grad_parts = exchange(in_grad_rows.reshape(ranks, rows, columns), "seq")
    shared_sum = in_grad_parts[0, :, 2 * wide : 2 * wide + 2 * NST]
    for j in range(1, ranks):
        shared_sum = shared_sum + in_grad_parts[j, :, 2 * wide : 2 * wide + 2 * NST]
    grad_in_weight = jnp.concatenate(
        [in_grad_parts[j, :, :wide] for j in range(ranks)]
        + [in_grad_parts[j, :, wide : 2 * wide] for j in range(ranks)]
        + [shared_sum]
        + [in_grad_parts[j, :, 2 * wide + 2 * NST : 2 * wide + 2 * NST + heads] for j in range(ranks)],
        axis=1,
    )

    scaled = tokens * inverse
    gain_grad = jnp.sum(hidden_grad * scaled, axis=0)
    inner = hidden_grad * norm_float
    token_grad = inverse * (inner - scaled * jnp.mean(inner * scaled, axis=-1, keepdims=True))
    input_grad = (upstream + token_grad)[None]

    def placed(own, shared):
        full = jnp.zeros(own.shape[:-1] + (E,), jnp.float32)
        full = lax.dynamic_update_slice_in_dim(full, own, rank * wide, own.ndim - 1)
        return jnp.concatenate([full, shared], axis=-1)

    kernel_all = placed(kernel_grad, kernel_shared_grad).reshape(CONVW, devices, taps)
    kernel_all = kernel_all.transpose(1, 0, 2).reshape(devices, CONVW * taps)
    offset_all = placed(offset_grad, offset_shared_grad).reshape(devices, taps)
    gated_all = lax.dynamic_update_slice_in_dim(jnp.zeros((E,), jnp.float32), gated_grad, rank * wide, 0)
    head_all = lax.dynamic_update_slice_in_dim(
        jnp.zeros((3, NHEADS), jnp.float32), jnp.stack([bias_grad, decay_grad, skip_grad]), rank * heads, 1
    )
    terms = jnp.concatenate(
        [
            gain_grad.reshape(devices, rows),
            kernel_all,
            offset_all,
            gated_all.reshape(devices, gains),
            jnp.broadcast_to(head_all.reshape(1, 3 * NHEADS), (devices, 3 * NHEADS)),
        ],
        axis=1,
    )
    used = terms.shape[1]
    term_lines = -(-used // LANES)
    terms = jnp.pad(terms, ((0, 0), (0, term_lines * LANES - used)))
    terms = terms.reshape(groups, ranks * term_lines, LANES)
    summed = scatter_bits(terms, "dp").reshape(ranks, term_lines, LANES)
    summed = exchange_sum(summed, "seq").reshape(-1)
    grad_norm_gain = summed[:rows]
    at = rows
    grad_conv_weight = summed[at : at + CONVW * taps].reshape(CONVW, taps)
    at += CONVW * taps
    grad_conv_bias = summed[at : at + taps]
    at += taps
    grad_gated_gain = summed[at : at + gains]
    at += gains
    grad_step_bias, grad_decay_log, grad_skip_gain = (
        summed[at + k * NHEADS : at + (k + 1) * NHEADS] for k in range(3)
    )
    new_norm_gain, new_first_norm_gain, new_second_norm_gain = adamw_update(
        norm_gain, grad_norm_gain, first_norm_gain, second_norm_gain, rate_vector, 0.0
    )
    new_in_weight, new_first_in_weight, new_second_in_weight = adamw_update(
        in_weight, grad_in_weight, first_in_weight, second_in_weight, rate_matrix, weight_decay
    )
    new_conv_weight, new_first_conv_weight, new_second_conv_weight = adamw_update(
        conv_weight, grad_conv_weight, first_conv_weight, second_conv_weight, rate_vector, 0.0
    )
    new_conv_bias, new_first_conv_bias, new_second_conv_bias = adamw_update(
        conv_bias, grad_conv_bias, first_conv_bias, second_conv_bias, rate_vector, 0.0
    )
    new_step_bias, new_first_step_bias, new_second_step_bias = adamw_update(
        step_bias, grad_step_bias, first_step_bias, second_step_bias, rate_vector, 0.0
    )
    new_decay_log, new_first_decay_log, new_second_decay_log = adamw_update(
        decay_log, grad_decay_log, first_decay_log, second_decay_log, rate_vector, 0.0
    )
    new_skip_gain, new_first_skip_gain, new_second_skip_gain = adamw_update(
        skip_gain, grad_skip_gain, first_skip_gain, second_skip_gain, rate_vector, 0.0
    )
    new_gated_gain, new_first_gated_gain, new_second_gated_gain = adamw_update(
        gated_gain, grad_gated_gain, first_gated_gain, second_gated_gain, rate_vector, 0.0
    )
    new_out_weight, new_first_out_weight, new_second_out_weight = adamw_update(
        out_weight, grad_out_weight, first_out_weight, second_out_weight, rate_matrix, weight_decay
    )
    return (
        block_output,
        input_grad,
        grad_norm_gain,
        grad_in_weight,
        grad_conv_weight,
        grad_conv_bias,
        grad_step_bias,
        grad_decay_log,
        grad_skip_gain,
        grad_gated_gain,
        grad_out_weight,
        new_norm_gain,
        new_first_norm_gain,
        new_second_norm_gain,
        new_in_weight,
        new_first_in_weight,
        new_second_in_weight,
        new_conv_weight,
        new_first_conv_weight,
        new_second_conv_weight,
        new_conv_bias,
        new_first_conv_bias,
        new_second_conv_bias,
        new_step_bias,
        new_first_step_bias,
        new_second_step_bias,
        new_decay_log,
        new_first_decay_log,
        new_second_decay_log,
        new_skip_gain,
        new_first_skip_gain,
        new_second_skip_gain,
        new_gated_gain,
        new_first_gated_gain,
        new_second_gated_gain,
        new_out_weight,
        new_first_out_weight,
        new_second_out_weight,
    )


def solution(mesh):
    in_specs = (
        P("dp", "seq", None),
        P("dp", "seq", None),
        P(("dp", "seq")),
        P(("dp", "seq"), None),
        P(None, ("dp", "seq")),
        P(("dp", "seq")),
        P(),
        P(),
        P(),
        P(("dp", "seq")),
        P(("dp", "seq"), None),
        P(("dp", "seq")),
        P(("dp", "seq")),
        P(("dp", "seq"), None),
        P(("dp", "seq"), None),
        P(None, ("dp", "seq")),
        P(None, ("dp", "seq")),
        P(("dp", "seq")),
        P(("dp", "seq")),
        P(),
        P(),
        P(),
        P(),
        P(),
        P(),
        P(("dp", "seq")),
        P(("dp", "seq")),
        P(("dp", "seq"), None),
        P(("dp", "seq"), None),
    )
    out_specs = (
        P("dp", "seq", None),
        P("dp", "seq", None),
        P(("dp", "seq")),
        P(("dp", "seq"), None),
        P(None, ("dp", "seq")),
        P(("dp", "seq")),
        P(),
        P(),
        P(),
        P(("dp", "seq")),
        P(("dp", "seq"), None),
        P(("dp", "seq")),
        P(("dp", "seq")),
        P(("dp", "seq")),
        P(("dp", "seq"), None),
        P(("dp", "seq"), None),
        P(("dp", "seq"), None),
        P(None, ("dp", "seq")),
        P(None, ("dp", "seq")),
        P(None, ("dp", "seq")),
        P(("dp", "seq")),
        P(("dp", "seq")),
        P(("dp", "seq")),
        P(),
        P(),
        P(),
        P(),
        P(),
        P(),
        P(),
        P(),
        P(),
        P(("dp", "seq")),
        P(("dp", "seq")),
        P(("dp", "seq")),
        P(("dp", "seq"), None),
        P(("dp", "seq"), None),
        P(("dp", "seq"), None),
    )
    return jax.shard_map(body, mesh=mesh, in_specs=in_specs, out_specs=out_specs, check_vma=False)
```

```python
import functools
import math

import jax
import jax.numpy as jnp
from jax import lax
from jax.experimental import pallas as pl
from jax.experimental.pallas import tpu as pltpu
from jax.sharding import PartitionSpec as P


E = 3072
NST = 128
NHEADS = 48
HDIM = 64
CONVW = 4
SPAN = 256
LANES = 128


low = jnp.bfloat16
half = jnp.float16
highest = lax.Precision.HIGHEST
beta_one = 0.9
beta_two = 0.95
adam_step = 10.0
adam_eps = 1e-08
rate_matrix = 0.01
rate_vector = 0.3
weight_decay = 0.1
norm_eps = 1e-05


def shift(block, axis, distance):
    size = lax.axis_size(axis)
    return lax.ppermute(block, axis, [(i, (i + distance) % size) for i in range(size)])


def swap(block, axis, bit):
    return lax.ppermute(block, axis, [(i, i ^ bit) for i in range(lax.axis_size(axis))])


def pick(stacked, index):
    return lax.dynamic_index_in_dim(stacked, index, 0, keepdims=False)


def exchange_sum(stacked, axis):
    size, here = lax.axis_size(axis), lax.axis_index(axis)
    arrived = [shift(pick(stacked, (here + turn) % size), axis, turn) for turn in range(1, size)]
    total = pick(stacked, here)
    for part in arrived:
        total = total + part
    return total


def after(value, *others):
    return lax.optimization_barrier((value,) + others)[0]


def pack_half(parts, bound):
    power = jnp.clip(jnp.ceil(jnp.log2(bound)) - 14.0, -120.0, 120.0)
    scaled = (parts * jnp.exp2(-power)).astype(half)
    return jnp.concatenate([scaled, jnp.broadcast_to(power.astype(half), parts.shape[:-1] + (LANES,))], axis=-1)


def unpack_half(message):
    width = message.shape[-1] - LANES
    return message[..., :width].astype(jnp.float32) * jnp.exp2(message[..., width : width + 1].astype(jnp.float32))


def gather_near(block, axis):
    return jnp.stack([block] + [shift(block, axis, turn) for turn in range(1, lax.axis_size(axis))])


def send_near(stacked, axis):
    return [shift(stacked[turn], axis, lax.axis_size(axis) - turn) for turn in range(1, lax.axis_size(axis))]


def gather_direct(block, axis):
    size, here = lax.axis_size(axis), lax.axis_index(axis)
    arrived = [block] + [shift(block, axis, turn) for turn in range(1, size)]
    result = jnp.stack(arrived)
    return jnp.take(result, (here + size - jnp.arange(size)) % size, axis=0)


def sum_near(stacked, axis):
    total = stacked
    for turn in range(1, lax.axis_size(axis)):
        total = total + jnp.roll(shift(stacked, axis, turn), turn, axis=0)
    return total


def gather_bits(block, axis):
    here = lax.axis_index(axis)
    result, bit = block[None], 1
    while bit < lax.axis_size(axis):
        other = swap(result, axis, bit)
        upper = (here & bit) > 0
        result = jnp.concatenate(
            [jnp.where(upper, other, result), jnp.where(upper, result, other)], axis=0
        )
        bit *= 2
    return result


def scatter_bits(stacked, axis):
    here, size = lax.axis_index(axis), lax.axis_size(axis)
    bit = 1
    rest = stacked
    while bit < size:
        pairs = rest.reshape((rest.shape[0] // 2, 2) + rest.shape[1:])
        own = (here & bit) // bit
        keep = lax.dynamic_index_in_dim(pairs, own, 1, keepdims=False)
        send = lax.dynamic_index_in_dim(pairs, 1 - own, 1, keepdims=False)
        rest = keep + swap(send, axis, bit)
        bit *= 2
    return rest[0]


def halves(value):
    high = value.astype(low)
    return high, (value - high.astype(jnp.float32)).astype(low)


def product(left, right, right_dim=0):
    dims = (((1,), (right_dim,)), ((), ()))

    def one(a, b):
        return lax.dot_general(a, b, dims, preferred_element_type=jnp.float32)

    return one(left[0], right[0]) + (one(left[0], right[1]) + one(left[1], right[0]))


def exact_dot(left, right):
    return jnp.dot(left, right, precision=highest, preferred_element_type=jnp.float32)


def softplus(value):
    small = jnp.exp(-jnp.abs(value))
    ratio = small / (2.0 + small)
    square = ratio * ratio
    series = jnp.full_like(square, 1.0 / 17.0)
    for power in (15, 13, 11, 9, 7, 5, 3, 1):
        series = series * square + 1.0 / power
    return jnp.maximum(value, 0.0) + 2.0 * ratio * series


def lane_of_head(pair, base, transposed=False):
    shape = (LANES, LANES)
    head = lax.broadcasted_iota(jnp.int32, shape, 1 if transposed else 0)
    lane = lax.broadcasted_iota(jnp.int32, shape, 0 if transposed else 1)
    return (head == base + 2 * pair + lane // HDIM).astype(jnp.float32)


def taps_of(extended, size, kernel, offset):
    total = offset + kernel[0:1] * extended[pl.ds(8 - CONVW + 1, size), :]
    for index in range(1, CONVW):
        total = total + kernel[index : index + 1] * extended[pl.ds(8 - CONVW + 1 + index, size), :]
    return total


def step_sizes(raw, heads):
    delta = softplus(raw + heads[0:1])
    change = -delta * jnp.exp(heads[1:2])
    size = raw.shape[0]
    below = lax.broadcasted_iota(jnp.int32, (size, size), 0) >= lax.broadcasted_iota(jnp.int32, (size, size), 1)
    return delta, change, exact_dot(below.astype(jnp.float32), change)


def forward_kernel(
    table_ref, z_ref, x_ref, shared_ref, step_ref, chan_ref, shared_chan_ref, head_ref,
    gated_ref, mixed_ref, state_ref, square_ref,
    tails, shared_tail, states,
    extended, shared_extended, meet, read_high, read_low, keys_high, keys_low,
    delta_all, run_all, run_rows,
):
    chunk, pair = pl.program_id(0), pl.program_id(1)
    size = x_ref.shape[0]
    base = table_ref[pl.num_programs(0)]

    @pl.when(pair == 0)
    def _():
        @pl.when(chunk == 0)
        def _():
            shared_tail[...] = jnp.zeros_like(shared_tail)
            tails[...] = jnp.zeros_like(tails)
            states[...] = jnp.zeros_like(states)

        shared_extended[0:8, :] = shared_tail[...]
        shared_extended[8:, :] = shared_ref[...]
        shared_tail[...] = shared_ref[size - 8 :, :]
        pre = taps_of(shared_extended, size, shared_chan_ref[...], shared_chan_ref[4:5, :])
        active = pre * jax.nn.sigmoid(pre)
        keys, read = halves(active[:, :NST]), halves(active[:, NST:])
        meet[...] = product(read, keys, 1)
        read_high[...], read_low[...] = read
        keys_high[...], keys_low[...] = halves(active[:, :NST].T)
        delta, _, running = step_sizes(step_ref[...], head_ref[...])
        delta_all[...] = delta
        run_all[...] = running
        run_rows[...] = running.T
        square_ref[...] = jnp.zeros_like(square_ref)

    chan = chan_ref[...]
    extended[0:8, :] = tails[pair]
    extended[8:, :] = x_ref[...]
    tails[pair] = x_ref[size - 8 :, :]
    pre = taps_of(extended, size, chan, chan[4:5])
    values = pre * jax.nn.sigmoid(pre)
    lanes = lane_of_head(pair, base)
    delta = exact_dot(delta_all[...], lanes)
    running = exact_dot(run_all[...], lanes)
    stepped = delta * values
    causal = lax.broadcasted_iota(jnp.int32, (size, size), 0) >= lax.broadcasted_iota(jnp.int32, (size, size), 1)
    locals_ = []
    for side in range(2):
        column = running[:, side * HDIM : side * HDIM + 1]
        row = run_rows[pl.ds(base + 2 * pair + side, 1), :]
        decay = jnp.exp(jnp.where(causal, column - row, -1e30))
        mixing = halves(decay * meet[...])
        locals_.append(product(mixing, halves(stepped[:, side * HDIM : (side + 1) * HDIM])))
    state = states[pair]
    state_ref[0, 0] = state
    carried = product((read_high[...], read_low[...]), halves(state))
    scanned = jnp.concatenate(locals_, axis=1) + jnp.exp(running) * carried
    last = running[size - 1 :, :]
    tail = halves(stepped * jnp.exp(last - running))
    states[pair] = jnp.exp(last) * state + product((keys_high[...], keys_low[...]), tail)
    mixed = scanned + chan[5:6] * values
    z = z_ref[...]
    gated = mixed * (z * jax.nn.sigmoid(z))
    mixed_ref[...] = mixed
    gated_ref[...] = gated
    square_ref[...] += gated * gated


def gate_kernel(
    z_ref, gated_ref, mixed_ref, up_ref, chan_ref, stats_ref,
    z_grad_ref, mix_grad_ref, square_ref, gain_grad_ref,
):
    @pl.when(pl.program_id(0) == 0)
    def _():
        gain_grad_ref[...] = jnp.zeros_like(gain_grad_ref)

    stats = stats_ref[...].T
    scale, pull = stats[:, 0:1], stats[:, 1:2]
    z, gated = z_ref[...], gated_ref[...]
    scaled = up_ref[...] * scale
    z_gain = jax.nn.sigmoid(z)
    gated_grad = scaled * chan_ref[6:7, :] - gated * pull
    z_gate = gated_grad * z_gain
    mix_grad_ref[...] = z_gate * z
    z_grad = (z_gate * mixed_ref[...] * (1.0 + z * (1.0 - z_gain))).astype(z_grad_ref.dtype)
    z_grad_ref[...] = z_grad
    wide_grad = z_grad.astype(jnp.float32)
    square_ref[...] = jnp.sum(wide_grad * wide_grad, axis=1, keepdims=True)
    gain_grad_ref[0:1, :] += jnp.sum(scaled * gated, axis=0, keepdims=True)


def backward_kernel(
    first, chunks, table_ref, x_ref, x_before_ref, shared_ref, shared_before_ref, step_ref, chan_ref, shared_chan_ref, head_ref,
    mixed_ref, mix_grad_ref, state_ref, state_after_ref, carried_in, *refs
):
    carried_in = (carried_in,) + refs[:5]
    (
        x_grad_ref, square_ref, shared_grad_ref,
        state_grads, heads_after, shared_after, chan_grad_ref, shared_chan_grad_ref, head_grad_ref,
        extended, shared_extended, later, shared_later, shared_pre,
        meet, read_high, read_low, keys_high, keys_low, read_rows_high, read_rows_low,
        delta_all, change_all, run_all, run_rows, meet_grad, keys_grad, read_grad, run_grad, delta_grad, last_grad,
    ) = refs[-31:]
    carried_out = (state_grads, heads_after, shared_after, chan_grad_ref, shared_chan_grad_ref, head_grad_ref)
    pair, pairs = pl.program_id(0), pl.num_programs(0)
    size = x_ref.shape[0]
    base = table_ref[chunks]

    @pl.when(pair == 0)
    def _():
        for new, old in zip(carried_out, carried_in):
            new[...] = old[...]

        shared_extended[0:8, :] = jnp.zeros(shared_before_ref.shape, jnp.float32) if first else shared_before_ref[...]
        shared_extended[8:, :] = shared_ref[...]
        pre = taps_of(shared_extended, size, shared_chan_ref[...], shared_chan_ref[4:5, :])
        shared_pre[...] = pre
        active = pre * jax.nn.sigmoid(pre)
        keys, read = halves(active[:, :NST]), halves(active[:, NST:])
        meet[...] = product(keys, read, 1)
        read_high[...], read_low[...] = read
        keys_high[...], keys_low[...] = keys
        read_rows_high[...], read_rows_low[...] = halves(active[:, NST:].T)
        delta, change, running = step_sizes(step_ref[...], head_ref[...])
        delta_all[...] = delta
        change_all[...] = change
        run_all[...] = running
        run_rows[...] = running.T
        meet_grad[...] = jnp.zeros_like(meet_grad)
        keys_grad[...] = jnp.zeros_like(keys_grad)
        read_grad[...] = jnp.zeros_like(read_grad)
        run_grad[...] = jnp.zeros_like(run_grad)
        delta_grad[...] = jnp.zeros_like(delta_grad)
        last_grad[...] = jnp.zeros_like(last_grad)
        square_ref[...] = jnp.zeros_like(square_ref)

    chan = chan_ref[...]
    extended[0:8, :] = jnp.zeros(x_before_ref.shape, jnp.float32) if first else x_before_ref[...]
    extended[8:, :] = x_ref[...]
    pre = taps_of(extended, size, chan, chan[4:5])
    gain = jax.nn.sigmoid(pre)
    values = pre * gain
    lanes = lane_of_head(pair, base)
    delta = exact_dot(delta_all[...], lanes)
    running = exact_dot(run_all[...], lanes)
    stepped = delta * values

    mixed, mix_grad = mixed_ref[...], mix_grad_ref[...]
    last = running[size - 1 :, :]
    fall = jnp.exp(last - running)
    rise = jnp.exp(running)
    state, state_grad = state_ref[0, 0], state_grads[pair]
    state_halves, state_grad_halves = halves(state), halves(state_grad)
    keys = (keys_high[...], keys_low[...])
    stepped_grad = fall * product(keys, state_grad_halves)
    keys_grad[...] += product(halves(stepped * fall), state_grad_halves, 1)
    risen = halves(mix_grad * rise)
    read_grad[...] += product(risen, state_halves, 1)
    ended = jnp.sum(state_grad * state_after_ref[0, 0], axis=0, keepdims=True)
    state_grads[pair] = jnp.exp(last) * state_grad + product((read_rows_high[...], read_rows_low[...]), risen)

    causal = lax.broadcasted_iota(jnp.int32, (size, size), 0) <= lax.broadcasted_iota(jnp.int32, (size, size), 1)
    parts = []
    for side in range(2):
        own = slice(side * HDIM, (side + 1) * HDIM)
        column = running[:, side * HDIM : side * HDIM + 1]
        row = run_rows[pl.ds(base + 2 * pair + side, 1), :]
        decay = jnp.exp(jnp.where(causal, row - column, -1e30))
        mixing = halves(decay * meet[...])
        grad_halves = halves(mix_grad[:, own])
        parts.append(product(mixing, grad_halves))
        meet_grad[...] += decay * product(halves(stepped[:, own]), grad_halves, 1)
    stepped_grad = stepped_grad + jnp.concatenate(parts, axis=1)
    to_head = lane_of_head(pair, base, transposed=True)
    scanned = mixed - chan[5:6] * values
    run_grad[...] += exact_dot(mix_grad * scanned - stepped * stepped_grad, to_head)
    delta_grad[...] += exact_dot(values * stepped_grad, to_head)
    last_grad[0:1, :] += exact_dot(jnp.broadcast_to(ended, (8, LANES)), to_head)[0:1]

    values_grad = chan[5:6] * mix_grad + delta * stepped_grad
    pre_grad = values_grad * (gain * (1.0 + pre * (1.0 - gain)))
    later[0:size, :] = pre_grad
    later[size:, :] = heads_after[pair]
    heads_after[pair] = pre_grad[0:8]
    x_grad = chan[0:1] * later[pl.ds(CONVW - 1, size), :]
    for index in range(1, CONVW):
        x_grad = x_grad + chan[index : index + 1] * later[pl.ds(CONVW - 1 - index, size), :]
    x_grad = x_grad.astype(x_grad_ref.dtype)
    x_grad_ref[:, pl.ds(pl.multiple_of(pair * LANES, LANES), LANES)] = x_grad
    wide_grad = x_grad.astype(jnp.float32)
    square_ref[...] += wide_grad * wide_grad
    for index in range(CONVW):
        seen = extended[pl.ds(8 - CONVW + 1 + index, size), :]
        chan_grad_ref[pair, index : index + 1, :] += jnp.sum(pre_grad * seen, axis=0, keepdims=True)
    chan_grad_ref[pair, 4:5, :] += jnp.sum(pre_grad, axis=0, keepdims=True)
    chan_grad_ref[pair, 5:6, :] += jnp.sum(mix_grad * values, axis=0, keepdims=True)

    @pl.when(pair == pairs - 1)
    def _():
        meet_halves = halves(meet_grad[...])
        keys_all = keys_grad[...] + product(meet_halves, (read_high[...], read_low[...]))
        read_all = read_grad[...] + product(halves(meet_grad[...].T), (keys_high[...], keys_low[...]))
        pre_s = shared_pre[...]
        gain_s = jax.nn.sigmoid(pre_s)
        chan_s = shared_chan_ref[...]
        grad_s = jnp.concatenate([keys_all, read_all], axis=1) * (gain_s * (1.0 + pre_s * (1.0 - gain_s)))
        shared_later[0:size, :] = grad_s
        shared_later[size:, :] = shared_after[...]
        shared_after[...] = grad_s[0:8]
        out = chan_s[0:1] * shared_later[pl.ds(CONVW - 1, size), :]
        for index in range(1, CONVW):
            out = out + chan_s[index : index + 1] * shared_later[pl.ds(CONVW - 1 - index, size), :]
        shared_grad_ref[...] = out
        for index in range(CONVW):
            seen = shared_extended[pl.ds(8 - CONVW + 1 + index, size), :]
            shared_chan_grad_ref[index : index + 1, :] += jnp.sum(grad_s * seen, axis=0, keepdims=True)
        shared_chan_grad_ref[4:5, :] += jnp.sum(grad_s, axis=0, keepdims=True)

        above = lax.broadcasted_iota(jnp.int32, (size, size), 0) <= lax.broadcasted_iota(jnp.int32, (size, size), 1)
        change_grad = exact_dot(above.astype(jnp.float32), run_grad[...]) + last_grad[0:1, :]
        rate = jnp.exp(head_ref[1:2, :])
        raw = step_ref[...] + head_ref[0:1, :]
        raw_grad = (delta_grad[...] - change_grad * rate) * jax.nn.sigmoid(raw)
        raw_low = raw_grad.astype(x_grad_ref.dtype)
        x_grad_ref[:, x_grad_ref.shape[1] - LANES :] = raw_low
        wide_raw = raw_low.astype(jnp.float32)
        square_ref[...] += wide_raw * wide_raw
        head_grad_ref[0:1, :] += jnp.sum(raw_grad, axis=0, keepdims=True)
        head_grad_ref[1:2, :] += jnp.sum(change_grad * change_all[...], axis=0, keepdims=True)


def run_forward(table, projected, chan, shared_chan, head_rows):
    length, wide = projected.shape[0], chan.shape[1]
    chunks, pairs = length // SPAN, wide // LANES
    f32 = jnp.float32
    block = pl.BlockSpec((SPAN, LANES), lambda c, p, t: (t[c], p))
    return pl.pallas_call(
        forward_kernel,
        grid_spec=pltpu.PrefetchScalarGridSpec(
            num_scalar_prefetch=1,
            grid=(chunks, pairs),
            in_specs=[
                block,
                pl.BlockSpec((SPAN, LANES), lambda c, p, t: (t[c], pairs + 2 + p)),
                pl.BlockSpec((SPAN, 2 * NST), lambda c, p, t: (t[c], pairs // 2)),
                pl.BlockSpec((SPAN, LANES), lambda c, p, t: (t[c], 2 * pairs + 2)),
                pl.BlockSpec((8, LANES), lambda c, p, t: (0, p)),
                pl.BlockSpec((8, 2 * NST), lambda c, p, t: (0, 0)),
                pl.BlockSpec((8, LANES), lambda c, p, t: (0, 0)),
            ],
            out_specs=[
                block,
                block,
                pl.BlockSpec((1, 1, NST, LANES), lambda c, p, t: (c, p, 0, 0)),
                pl.BlockSpec((SPAN, LANES), lambda c, p, t: (t[c], 0)),
            ],
            scratch_shapes=[
                pltpu.VMEM((pairs, 8, LANES), f32),
                pltpu.VMEM((8, 2 * NST), f32),
                pltpu.VMEM((pairs, NST, LANES), f32),
                pltpu.VMEM((SPAN + 8, LANES), f32),
                pltpu.VMEM((SPAN + 8, 2 * NST), f32),
                pltpu.VMEM((SPAN, SPAN), f32),
                pltpu.VMEM((SPAN, NST), low),
                pltpu.VMEM((SPAN, NST), low),
                pltpu.VMEM((NST, SPAN), low),
                pltpu.VMEM((NST, SPAN), low),
                pltpu.VMEM((SPAN, LANES), f32),
                pltpu.VMEM((SPAN, LANES), f32),
                pltpu.VMEM((LANES, SPAN), f32),
            ],
        ),
        out_shape=[
            jax.ShapeDtypeStruct((length, wide), f32),
            jax.ShapeDtypeStruct((length, wide), f32),
            jax.ShapeDtypeStruct((chunks, pairs, NST, LANES), f32),
            jax.ShapeDtypeStruct((length, LANES), f32),
        ],
        name="mixer_forward",
    )(table, projected, projected, projected, projected, chan, shared_chan, head_rows)


def run_gate(projected, gated, mixed, up, chan, stats):
    length, wide = gated.shape
    f32 = jnp.float32
    size = SPAN // 2
    block = pl.BlockSpec((size, wide), lambda c: (c, 0))
    whole = pl.BlockSpec((8, wide), lambda c: (0, 0))
    return pl.pallas_call(
        gate_kernel,
        grid=(length // size,),
        in_specs=[block, block, block, block, whole, pl.BlockSpec((8, size), lambda c: (0, c))],
        out_specs=[block, block, pl.BlockSpec((size, 1), lambda c: (c, 0)), whole],
        out_shape=[
            jax.ShapeDtypeStruct((length, wide), low),
            jax.ShapeDtypeStruct((length, wide), f32),
            jax.ShapeDtypeStruct((length, 1), f32),
            jax.ShapeDtypeStruct((8, wide), f32),
        ],
        name="gate_backward",
    )(projected, gated, mixed, up, chan, stats)


def run_backward(chunk, table, projected, chan, shared_chan, head_rows, mixed, mix_grad, states, carried, before):
    length, wide = projected.shape[0], chan.shape[1]
    chunks, pairs = length // SPAN, wide // LANES
    f32 = jnp.float32
    lines = SPAN // 8
    earlier, following = max(chunk - 1, 0), min(chunk + 1, chunks - 1)
    block = pl.BlockSpec((SPAN, LANES), lambda p, t: (t[chunk], p))
    flat = pl.BlockSpec((8, 2 * NST), lambda p, t: (0, 0))
    head = pl.BlockSpec((8, LANES), lambda p, t: (0, 0))
    carries = [
        pl.BlockSpec((pairs, NST, LANES), lambda p, t: (0, 0, 0)),
        pl.BlockSpec((pairs, 8, LANES), lambda p, t: (0, 0, 0)),
        flat,
        pl.BlockSpec((pairs, 8, LANES), lambda p, t: (0, 0, 0)),
        flat,
        head,
    ]
    carried_shapes = [jax.ShapeDtypeStruct(c.shape, f32) for c in carried]
    return pl.pallas_call(
        functools.partial(backward_kernel, chunk == 0, chunks),
        grid_spec=pltpu.PrefetchScalarGridSpec(
            num_scalar_prefetch=1,
            grid=(pairs,),
            in_specs=[
                pl.BlockSpec((SPAN, LANES), lambda p, t: (t[chunk], pairs + 2 + p)),
                pl.BlockSpec((8, LANES), lambda p, t: (t[earlier] * lines + lines - 1, pairs + 2 + p)),
                pl.BlockSpec((SPAN, 2 * NST), lambda p, t: (t[chunk], pairs // 2)),
                pl.BlockSpec((8, 2 * NST), lambda p, t: (t[earlier] * lines + lines - 1, pairs // 2)),
                pl.BlockSpec((SPAN, LANES), lambda p, t: (t[chunk], 2 * pairs + 2)),
                pl.BlockSpec((8, LANES), lambda p, t: (0, p)),
                flat,
                head,
                block,
                block,
                pl.BlockSpec((1, 1, NST, LANES), lambda p, t: (chunk, p, 0, 0)),
                pl.BlockSpec((1, 1, NST, LANES), lambda p, t: (following, p, 0, 0)),
            ]
            + carries
            + [pl.BlockSpec(memory_space=pl.ANY)] * len(before),
            out_specs=[
                pl.BlockSpec((SPAN, wide + LANES), lambda p, t: (t[chunk], 0)),
                pl.BlockSpec((SPAN, LANES), lambda p, t: (t[chunk], 0)),
                pl.BlockSpec((SPAN, 2 * NST), lambda p, t: (t[chunk], 0)),
            ]
            + carries,
            scratch_shapes=[
                pltpu.VMEM((SPAN + 8, LANES), f32),
                pltpu.VMEM((SPAN + 8, 2 * NST), f32),
                pltpu.VMEM((SPAN + 8, LANES), f32),
                pltpu.VMEM((SPAN + 8, 2 * NST), f32),
                pltpu.VMEM((SPAN, 2 * NST), f32),
                pltpu.VMEM((SPAN, SPAN), f32),
                pltpu.VMEM((SPAN, NST), low),
                pltpu.VMEM((SPAN, NST), low),
                pltpu.VMEM((SPAN, NST), low),
                pltpu.VMEM((SPAN, NST), low),
                pltpu.VMEM((NST, SPAN), low),
                pltpu.VMEM((NST, SPAN), low),
                pltpu.VMEM((SPAN, LANES), f32),
                pltpu.VMEM((SPAN, LANES), f32),
                pltpu.VMEM((SPAN, LANES), f32),
                pltpu.VMEM((LANES, SPAN), f32),
                pltpu.VMEM((SPAN, SPAN), f32),
                pltpu.VMEM((SPAN, NST), f32),
                pltpu.VMEM((SPAN, NST), f32),
                pltpu.VMEM((SPAN, LANES), f32),
                pltpu.VMEM((SPAN, LANES), f32),
                pltpu.VMEM((8, LANES), f32),
            ],
        ),
        out_shape=[
            jax.ShapeDtypeStruct((length, wide + LANES), low),
            jax.ShapeDtypeStruct((length, LANES), f32),
            jax.ShapeDtypeStruct((length, 2 * NST), f32),
        ]
        + carried_shapes,
        input_output_aliases={19 + k: k for k in range(len(before))},
        name="mixer_backward",
    )(
        table, projected, projected, projected, projected, projected, chan, shared_chan, head_rows,
        mixed, mix_grad, states, states, *carried, *before,
    )


def halve(block, left, bit, axis):
    place = left.index(bit)
    own = (lax.axis_index(axis) & bit) // bit
    keep = lax.dynamic_index_in_dim(block, own, place, keepdims=False)
    send = lax.dynamic_index_in_dim(block, 1 - own, place, keepdims=False)
    return keep + swap(send, axis, bit), [b for b in left if b != bit]


class Scatter:
    def __init__(self, arrays, axis):
        self.axis = axis
        size = lax.axis_size(axis)
        bits = [1 << k for k in range(size.bit_length() - 1)]
        upper = bits[1:]
        turned = upper[len(upper) // 2 :] + upper[: len(upper) // 2]
        self.orders = [bits[:1] + (upper if k % 2 == 0 else turned) for k in range(len(arrays))]
        self.left = [bits[::-1] for _ in arrays]
        self.blocks = [
            a.reshape((2,) * len(bits) + (a.shape[0] // size,) + a.shape[1:]) for a in arrays
        ]
        self.steps = len(bits)
        self.done = 0

    def step(self):
        for k in range(len(self.blocks)):
            self.blocks[k], self.left[k] = halve(
                self.blocks[k], self.left[k], self.orders[k][self.done], self.axis
            )
        self.done += 1

    def finish(self):
        while self.done < self.steps:
            self.step()
        return self.blocks


def adamw_update(param, grad, first, second, rate, decay):
    first_new = beta_one * first + (1.0 - beta_one) * grad
    second_new = beta_two * second + (1.0 - beta_two) * grad * grad
    corrected_first = first_new / (1.0 - beta_one**adam_step)
    corrected_second = second_new / (1.0 - beta_two**adam_step)
    param_new = param - rate * (
        corrected_first / (jnp.sqrt(corrected_second) + adam_eps) + decay * param
    )
    return (param_new, first_new, second_new)


def dot(left, right):
    return jnp.dot(left, right, preferred_element_type=jnp.float32)


def body(
    block_input,
    cotangent,
    norm_gain,
    in_weight,
    conv_weight,
    conv_bias,
    step_bias,
    decay_log,
    skip_gain,
    gated_gain,
    out_weight,
    first_norm_gain,
    second_norm_gain,
    first_in_weight,
    second_in_weight,
    first_conv_weight,
    second_conv_weight,
    first_conv_bias,
    second_conv_bias,
    first_step_bias,
    second_step_bias,
    first_decay_log,
    second_decay_log,
    first_skip_gain,
    second_skip_gain,
    first_gated_gain,
    second_gated_gain,
    first_out_weight,
    second_out_weight,
):
    ranks, rank = lax.axis_size("seq"), lax.axis_index("seq")
    groups = lax.axis_size("dp")
    devices = ranks * groups
    wide, heads = E // ranks, NHEADS // ranks
    rows = in_weight.shape[0]
    width = rows * devices
    taps = conv_bias.shape[0]
    channels = taps * devices
    step_at = 2 * E + 2 * NST
    spare = LANES - (in_weight.shape[1] - step_at)

    packed = jnp.concatenate(
        [norm_gain, conv_weight.reshape(-1), conv_bias, gated_gain]
    ).astype(low).astype(jnp.float32)
    gains = gated_gain.shape[0]
    filled = packed.shape[0]
    lines = -(-filled // LANES)
    packed = jnp.pad(packed, (0, lines * LANES - filled)).reshape(lines, LANES)
    small_line = gather_direct(packed, "seq")
    small = gather_bits(small_line, "dp")
    small = small.reshape(devices, lines * LANES)
    norm_float = small[:, :rows].reshape(-1)
    kernel_float = small[:, rows : rows + CONVW * taps].reshape(devices, CONVW, taps)
    kernel_float = kernel_float.transpose(1, 0, 2).reshape(CONVW, channels)
    offset_float = small[:, rows + CONVW * taps : rows + (CONVW + 1) * taps].reshape(-1)
    gated_float = small[:, rows + (CONVW + 1) * taps : filled].reshape(-1)
    kernel_own = lax.dynamic_slice_in_dim(kernel_float, rank * wide, wide, 1)
    offset_own = lax.dynamic_slice_in_dim(offset_float, rank * wide, wide, 0)
    gated_own = lax.dynamic_slice_in_dim(gated_float, rank * wide, wide, 0)
    skip_own = lax.dynamic_slice_in_dim(skip_gain, rank * heads, heads, 0)

    in_low = after(in_weight.astype(low), small_line)
    out_low = after(out_weight.astype(low), small_line)

    def for_rank(j):
        return jnp.concatenate(
            [
                lax.dynamic_slice_in_dim(in_low, j * wide, wide, 1),
                in_low[:, 2 * E : step_at],
                lax.dynamic_slice_in_dim(in_low, E + j * wide, wide, 1),
                jnp.pad(in_low[:, step_at:], ((0, 0), (0, spare))),
                lax.dynamic_slice_in_dim(out_low, j * wide, wide, 1),
            ],
            axis=1,
        )

    columns = 2 * NST + 2 * wide + LANES
    weights_arrived = []
    for turn in range(1, ranks):
        weights_arrived.append(shift(for_rank((rank + turn) % ranks), "seq", turn))

    tokens, upstream = block_input[0], cotangent[0]
    span = tokens.shape[0]
    length = span * ranks
    inverse = lax.rsqrt(jnp.mean(tokens * tokens, axis=-1, keepdims=True) + norm_eps)
    hidden_own = (tokens * inverse * norm_float).astype(low)
    weights_arrived = [after(part, hidden_own) for part in weights_arrived]
    weight_rows = jnp.zeros((ranks, rows, columns + wide), low)
    weight_rows = lax.dynamic_update_index_in_dim(weight_rows, for_rank(rank), rank, 0)
    for turn in range(1, ranks):
        weight_rows = lax.dynamic_update_index_in_dim(
            weight_rows, weights_arrived[turn - 1], (rank + ranks - turn) % ranks, 0
        )
    weight_rows = weight_rows.reshape(ranks * rows, columns + wide)
    in_full = lax.all_gather(weight_rows[:, :columns], "dp", axis=0, tiled=True)
    out_full = lax.all_gather(weight_rows[:, columns:], "dp", axis=0, tiled=True)

    hidden = gather_near(hidden_own, "seq").reshape(length, width)
    upstream_low = gather_near(after(upstream.astype(low), hidden), "seq").reshape(length, width)

    projected = dot(hidden, in_full)
    none = jnp.zeros((1, wide), jnp.float32)
    chan = jnp.concatenate(
        [kernel_own, offset_own[None], jnp.repeat(skip_own, HDIM)[None], gated_own[None], none], axis=0
    )
    shared_chan = jnp.concatenate(
        [kernel_float[:, E:], offset_float[None, E:], jnp.zeros((3, 2 * NST), jnp.float32)], axis=0
    )
    head_rows = jnp.pad(jnp.stack([step_bias, decay_log]), ((0, 6), (0, LANES - NHEADS)))
    pairs, chunks = wide // LANES, length // SPAN
    per_rank = span // SPAN
    order = jnp.arange(chunks, dtype=jnp.int32)
    order = (rank + ranks - order // per_rank) % ranks * per_rank + order % per_rank
    table = jnp.concatenate([order, jnp.reshape(rank * heads, (1,))]).astype(jnp.int32)
    zeros = functools.partial(jnp.zeros, dtype=jnp.float32)
    gated, mixed, states, squares = run_forward(table, projected, chan, shared_chan, head_rows)
    packed_length = (ranks, span // LANES, LANES)
    square_sum = sum_near(jnp.sum(squares, axis=1).reshape(packed_length), "seq").reshape(length)
    scale = lax.rsqrt(square_sum / E + norm_eps)
    normed_low = (gated * scale[:, None] * gated_own).astype(low)
    branch_factor = 2.0 ** (14 - math.ceil(math.log2(0.17 * math.sqrt(E * wide))))
    out_half = (dot(normed_low, out_full.T) * branch_factor).astype(half).reshape(ranks, span, width)
    branch = tokens + dot(normed_low[:span], out_full.T)

    normed_grad = dot(upstream_low, out_full)
    pull_sum = jnp.sum(normed_grad * gated_own * gated, axis=1).reshape(packed_length)
    pull_sum = sum_near(pull_sum, "seq").reshape(length)
    stats = jnp.stack([scale, scale * scale * scale * (pull_sum / E)])
    stats = jnp.pad(stats, ((0, 6), (0, 0)))
    gate_low, mix_grad, gate_square, gain_rows = run_gate(projected, gated, mixed, normed_grad, chan, stats)
    gated_grad = gain_rows[0]

    branch_parts = send_near(after(out_half, pull_sum), "seq")

    early = Scatter([dot(upstream_low.T, normed_low), dot(hidden.T, gate_low)], "dp")
    carried = (
        zeros((pairs, NST, LANES)), zeros((pairs, 8, LANES)), zeros((8, 2 * NST)),
        zeros((pairs, 8, LANES)), zeros((8, 2 * NST)), zeros((8, LANES)),
    )
    outputs = ()
    ready = (branch,)
    for turn in range(chunks):
        if early.done < early.steps and turn != 2:
            early.step()
        mix_grad = after(mix_grad, *ready)
        result = run_backward(
            chunks - 1 - turn, table, projected, chan, shared_chan, head_rows, mixed, mix_grad, states, carried, outputs
        )
        outputs, carried = tuple(result[:3]), tuple(result[3:])
        ready = tuple(early.blocks) if turn != 1 else ()
    conv_low, conv_square, shared_grad = outputs
    _, _, _, chan_grad, shared_chan_grad, head_grad = carried
    early.finish()

    shared_parts = shared_grad.reshape(ranks, span, 2 * NST)
    shared_sent = send_near(shared_parts, "seq")

    hidden_part = dot(gate_low, in_full[:, :wide].T) + dot(conv_low, in_full[:, wide + 2 * NST :].T)
    row_bound = 0.1565 * math.sqrt(2 * wide + NHEADS) * jnp.sqrt(gate_square + jnp.sum(conv_square, axis=1, keepdims=True))
    hidden_part = hidden_part.reshape(ranks, span, width)
    hidden_half = pack_half(hidden_part, row_bound.reshape(ranks, span, 1))
    hidden_parts = send_near(hidden_half, "seq")

    split = 4 * LANES
    conv_parts = [dot(hidden.T, conv_low[:, :split]), dot(hidden.T, conv_low[:, split:])]
    for part in branch_parts:
        branch = branch + part.astype(jnp.float32) * (1.0 / branch_factor)
    block_output = branch[None]

    shared_own = shared_parts[0]
    for part in shared_sent:
        shared_own = shared_own + part
    shared_own = shared_own.astype(low)
    late = Scatter(conv_parts + [dot(hidden_own.T, shared_own)], "dp")
    late.finish()

    chan_grad = chan_grad.transpose(1, 0, 2).reshape(8, wide)
    kernel_grad, offset_grad = chan_grad[:CONVW], chan_grad[4]
    skip_grad = jnp.sum(chan_grad[5].reshape(heads, HDIM), axis=1)
    kernel_shared_grad, offset_shared_grad = shared_chan_grad[:CONVW], shared_chan_grad[4]

    sums_all = jnp.concatenate(
        [block.reshape(ranks, rows, -1) for block in (late.blocks + early.blocks)], axis=2
    )
    conv_wide = wide + LANES
    packed_sums = pack_half(sums_all, jnp.max(jnp.abs(sums_all), axis=-1, keepdims=True))
    hidden_parts = [after(part, packed_sums) for part in hidden_parts]
    collected = sums_all
    for turn in range(1, ranks):
        arrived = shift(pick(packed_sums, (rank + turn) % ranks), "seq", turn)
        collected = lax.dynamic_update_index_in_dim(
            collected, unpack_half(arrived), (rank + ranks - turn) % ranks, 0
        )
    at = conv_wide + 2 * NST
    shared_sum = sum(collected[j, :, wide:at] for j in range(ranks))
    grad_in_weight = jnp.concatenate(
        [collected[j, :, at + wide :] for j in range(ranks)]
        + [collected[j, :, :wide] for j in range(ranks)]
        + [shared_sum[:, LANES:], shared_sum[:, : LANES - spare]],
        axis=1,
    )
    grad_out_weight = jnp.concatenate([collected[j, :, at : at + wide] for j in range(ranks)], axis=1)

    hidden_grad = hidden_part[0] + dot(shared_own, in_full[:, wide : wide + 2 * NST].T)
    for part in hidden_parts:
        hidden_grad = hidden_grad + unpack_half(part)
    scaled = tokens * inverse
    gain_grad = jnp.sum(hidden_grad * scaled, axis=0)
    inner = hidden_grad * norm_float
    token_grad = inverse * (inner - scaled * jnp.mean(inner * scaled, axis=-1, keepdims=True))
    input_grad = (upstream + token_grad)[None]

    def placed(own, shared):
        full = jnp.zeros(own.shape[:-1] + (E,), jnp.float32)
        full = lax.dynamic_update_slice_in_dim(full, own, rank * wide, own.ndim - 1)
        return jnp.concatenate([full, shared], axis=-1)

    kernel_all = placed(kernel_grad, kernel_shared_grad).reshape(CONVW, devices, taps)
    kernel_all = kernel_all.transpose(1, 0, 2).reshape(devices, CONVW * taps)
    offset_all = placed(offset_grad, offset_shared_grad).reshape(devices, taps)
    gated_all = lax.dynamic_update_slice_in_dim(jnp.zeros((E,), jnp.float32), gated_grad, rank * wide, 0)
    skip_all = lax.dynamic_update_slice_in_dim(jnp.zeros((NHEADS,), jnp.float32), skip_grad, rank * heads, 0)
    head_all = jnp.concatenate([head_grad[0, :NHEADS], head_grad[1, :NHEADS], skip_all])
    terms = jnp.concatenate(
        [
            gain_grad.reshape(devices, rows),
            kernel_all,
            offset_all,
            gated_all.reshape(devices, gains),
            jnp.broadcast_to(head_all[None], (devices, 3 * NHEADS)),
        ],
        axis=1,
    )
    used = terms.shape[1]
    term_lines = -(-used // LANES)
    terms = jnp.pad(terms, ((0, 0), (0, term_lines * LANES - used)))
    terms = terms.reshape(groups, ranks * term_lines, LANES)
    summed = scatter_bits(terms, "dp").reshape(ranks, term_lines, LANES)
    summed = exchange_sum(summed, "seq").reshape(-1)
    grad_norm_gain = summed[:rows]
    at = rows
    grad_conv_weight = summed[at : at + CONVW * taps].reshape(CONVW, taps)
    at += CONVW * taps
    grad_conv_bias = summed[at : at + taps]
    at += taps
    grad_gated_gain = summed[at : at + gains]
    at += gains
    grad_step_bias, grad_decay_log, grad_skip_gain = (
        summed[at + k * NHEADS : at + (k + 1) * NHEADS] for k in range(3)
    )
    new_norm_gain, new_first_norm_gain, new_second_norm_gain = adamw_update(
        norm_gain, grad_norm_gain, first_norm_gain, second_norm_gain, rate_vector, 0.0
    )
    new_in_weight, new_first_in_weight, new_second_in_weight = adamw_update(
        in_weight, grad_in_weight, first_in_weight, second_in_weight, rate_matrix, weight_decay
    )
    new_conv_weight, new_first_conv_weight, new_second_conv_weight = adamw_update(
        conv_weight, grad_conv_weight, first_conv_weight, second_conv_weight, rate_vector, 0.0
    )
    new_conv_bias, new_first_conv_bias, new_second_conv_bias = adamw_update(
        conv_bias, grad_conv_bias, first_conv_bias, second_conv_bias, rate_vector, 0.0
    )
    new_step_bias, new_first_step_bias, new_second_step_bias = adamw_update(
        step_bias, grad_step_bias, first_step_bias, second_step_bias, rate_vector, 0.0
    )
    new_decay_log, new_first_decay_log, new_second_decay_log = adamw_update(
        decay_log, grad_decay_log, first_decay_log, second_decay_log, rate_vector, 0.0
    )
    new_skip_gain, new_first_skip_gain, new_second_skip_gain = adamw_update(
        skip_gain, grad_skip_gain, first_skip_gain, second_skip_gain, rate_vector, 0.0
    )
    new_gated_gain, new_first_gated_gain, new_second_gated_gain = adamw_update(
        gated_gain, grad_gated_gain, first_gated_gain, second_gated_gain, rate_vector, 0.0
    )
    new_out_weight, new_first_out_weight, new_second_out_weight = adamw_update(
        out_weight, grad_out_weight, first_out_weight, second_out_weight, rate_matrix, weight_decay
    )
    return (
        block_output,
        input_grad,
        grad_norm_gain,
        grad_in_weight,
        grad_conv_weight,
        grad_conv_bias,
        grad_step_bias,
        grad_decay_log,
        grad_skip_gain,
        grad_gated_gain,
        grad_out_weight,
        new_norm_gain,
        new_first_norm_gain,
        new_second_norm_gain,
        new_in_weight,
        new_first_in_weight,
        new_second_in_weight,
        new_conv_weight,
        new_first_conv_weight,
        new_second_conv_weight,
        new_conv_bias,
        new_first_conv_bias,
        new_second_conv_bias,
        new_step_bias,
        new_first_step_bias,
        new_second_step_bias,
        new_decay_log,
        new_first_decay_log,
        new_second_decay_log,
        new_skip_gain,
        new_first_skip_gain,
        new_second_skip_gain,
        new_gated_gain,
        new_first_gated_gain,
        new_second_gated_gain,
        new_out_weight,
        new_first_out_weight,
        new_second_out_weight,
    )


def solution(mesh):
    in_specs = (
        P("dp", "seq", None),
        P("dp", "seq", None),
        P(("dp", "seq")),
        P(("dp", "seq"), None),
        P(None, ("dp", "seq")),
        P(("dp", "seq")),
        P(),
        P(),
        P(),
        P(("dp", "seq")),
        P(("dp", "seq"), None),
        P(("dp", "seq")),
        P(("dp", "seq")),
        P(("dp", "seq"), None),
        P(("dp", "seq"), None),
        P(None, ("dp", "seq")),
        P(None, ("dp", "seq")),
        P(("dp", "seq")),
        P(("dp", "seq")),
        P(),
        P(),
        P(),
        P(),
        P(),
        P(),
        P(("dp", "seq")),
        P(("dp", "seq")),
        P(("dp", "seq"), None),
        P(("dp", "seq"), None),
    )
    out_specs = (
        P("dp", "seq", None),
        P("dp", "seq", None),
        P(("dp", "seq")),
        P(("dp", "seq"), None),
        P(None, ("dp", "seq")),
        P(("dp", "seq")),
        P(),
        P(),
        P(),
        P(("dp", "seq")),
        P(("dp", "seq"), None),
        P(("dp", "seq")),
        P(("dp", "seq")),
        P(("dp", "seq")),
        P(("dp", "seq"), None),
        P(("dp", "seq"), None),
        P(("dp", "seq"), None),
        P(None, ("dp", "seq")),
        P(None, ("dp", "seq")),
        P(None, ("dp", "seq")),
        P(("dp", "seq")),
        P(("dp", "seq")),
        P(("dp", "seq")),
        P(),
        P(),
        P(),
        P(),
        P(),
        P(),
        P(),
        P(),
        P(),
        P(("dp", "seq")),
        P(("dp", "seq")),
        P(("dp", "seq")),
        P(("dp", "seq"), None),
        P(("dp", "seq"), None),
        P(("dp", "seq"), None),
    )

    return jax.shard_map(body, mesh=mesh, in_specs=in_specs, out_specs=out_specs, check_vma=False)
```

```python
import functools
import math

import jax
import jax.numpy as jnp
from jax import lax
from jax.experimental import pallas as pl
from jax.experimental.pallas import tpu as pltpu
from jax.sharding import PartitionSpec as P


E = 3072
NST = 128
NHEADS = 48
HDIM = 64
CONVW = 4
SPAN = 256
LANES = 128


low = jnp.bfloat16
half = jnp.float16
highest = lax.Precision.HIGHEST
beta_one = 0.9
beta_two = 0.95
adam_step = 10.0
adam_eps = 1e-08
rate_matrix = 0.01
rate_vector = 0.3
weight_decay = 0.1
norm_eps = 1e-05


def shift(block, axis, distance):
    size = lax.axis_size(axis)
    return lax.ppermute(block, axis, [(i, (i + distance) % size) for i in range(size)])


def step_to(block, axis, distance):
    size = lax.axis_size(axis)
    route = [(i, i + distance) for i in range(size) if 0 <= i + distance < size]
    return lax.ppermute(block, axis, route)


def swap(block, axis, bit):
    return lax.ppermute(block, axis, [(i, i ^ bit) for i in range(lax.axis_size(axis))])


def pick(stacked, index):
    return lax.dynamic_index_in_dim(stacked, index, 0, keepdims=False)


def exchange_sum(stacked, axis):
    size, here = lax.axis_size(axis), lax.axis_index(axis)
    arrived = [shift(pick(stacked, (here + turn) % size), axis, turn) for turn in range(1, size)]
    total = pick(stacked, here)
    for part in arrived:
        total = total + part
    return total


def after(value, *others):
    return lax.optimization_barrier((value,) + others)[0]


def pack_half(parts, bound):
    power = jnp.clip(jnp.ceil(jnp.log2(bound)) - 14.0, -120.0, 120.0)
    scaled = (parts * jnp.exp2(-power)).astype(half)
    return jnp.concatenate([scaled, jnp.broadcast_to(power.astype(half), parts.shape[:-1] + (LANES,))], axis=-1)


def unpack_half(message):
    width = message.shape[-1] - LANES
    return message[..., :width].astype(jnp.float32) * jnp.exp2(message[..., width : width + 1].astype(jnp.float32))


def near_parts(block, axis):
    size, here = lax.axis_size(axis), lax.axis_index(axis)
    if size != 4:
        return [block] + [shift(block, axis, turn) for turn in range(1, size)]
    below, above = step_to(block, axis, 1), step_to(block, axis, -1)
    across = shift(block, axis, 2)
    far = lax.ppermute(across, axis, [(2, 3), (1, 0)])
    return [block, jnp.where(here == 0, far, below), across, jnp.where(here == size - 1, far, above)]


def send_near(stacked, axis):
    return [shift(stacked[turn], axis, lax.axis_size(axis) - turn) for turn in range(1, lax.axis_size(axis))]


def gather_direct(block, axis):
    size, here = lax.axis_size(axis), lax.axis_index(axis)
    arrived = [block] + [shift(block, axis, turn) for turn in range(1, size)]
    result = jnp.stack(arrived)
    return jnp.take(result, (here + size - jnp.arange(size)) % size, axis=0)


def sum_near(stacked, axis):
    total = stacked
    for turn in range(1, lax.axis_size(axis)):
        total = total + jnp.roll(shift(stacked, axis, turn), turn, axis=0)
    return total


def gather_bits(block, axis):
    here = lax.axis_index(axis)
    result, bit = block[None], 1
    while bit < lax.axis_size(axis):
        other = swap(result, axis, bit)
        upper = (here & bit) > 0
        result = jnp.concatenate(
            [jnp.where(upper, other, result), jnp.where(upper, result, other)], axis=0
        )
        bit *= 2
    return result


def gather_rows(blocks, axis):
    size, here = lax.axis_size(axis), lax.axis_index(axis)
    bits = [1 << k for k in range(size.bit_length() - 1)]
    upper = bits[1:]
    turned = upper[len(upper) // 2 :] + upper[: len(upper) // 2]
    parts, paths = [], []
    for block in blocks:
        rows = block.shape[0] // 2
        parts += [p.reshape((1,) * len(bits) + p.shape) for p in (block[:rows], block[rows:])]
        paths += [upper + bits[:1], turned + bits[:1]]
    for step in range(len(bits)):
        arrived = [swap(p, axis, path[step]) for p, path in zip(parts, paths)]
        for k, path in enumerate(paths):
            place = bits[::-1].index(path[step])
            up = (here & path[step]) > 0
            parts[k] = jnp.concatenate(
                [jnp.where(up, arrived[k], parts[k]), jnp.where(up, parts[k], arrived[k])], axis=place
            )
    return [
        jnp.concatenate(parts[2 * k : 2 * k + 2], axis=len(bits)).reshape(-1, block.shape[1])
        for k, block in enumerate(blocks)
    ]


def scatter_bits(stacked, axis):
    here, size = lax.axis_index(axis), lax.axis_size(axis)
    bit = 1
    rest = stacked
    while bit < size:
        pairs = rest.reshape((rest.shape[0] // 2, 2) + rest.shape[1:])
        own = (here & bit) // bit
        keep = lax.dynamic_index_in_dim(pairs, own, 1, keepdims=False)
        send = lax.dynamic_index_in_dim(pairs, 1 - own, 1, keepdims=False)
        rest = keep + swap(send, axis, bit)
        bit *= 2
    return rest[0]


def halves(value):
    high = value.astype(low)
    return high, (value - high.astype(jnp.float32)).astype(low)


def product(left, right, right_dim=0):
    joined_left = jnp.concatenate([left[0], left[0], left[1]], axis=1)
    joined_right = jnp.concatenate([right[0], right[1], right[0]], axis=right_dim)
    dims = (((1,), (right_dim,)), ((), ()))
    return lax.dot_general(joined_left, joined_right, dims, preferred_element_type=jnp.float32)


def thirds(value):
    high, rest = value.astype(low), value
    rest = value - high.astype(jnp.float32)
    middle = rest.astype(low)
    return high, middle, (rest - middle.astype(jnp.float32)).astype(low)


def spread(parts, chosen):
    return jnp.dot(
        jnp.concatenate(parts, axis=1), jnp.concatenate([chosen] * len(parts), axis=0), preferred_element_type=jnp.float32
    )


def exact_dot(left, right):
    return jnp.dot(left, right, precision=highest, preferred_element_type=jnp.float32)


def softplus(value):
    small = jnp.exp(-jnp.abs(value))
    ratio = small / (2.0 + small)
    square = ratio * ratio
    series = jnp.full_like(square, 1.0 / 17.0)
    for power in (15, 13, 11, 9, 7, 5, 3, 1):
        series = series * square + 1.0 / power
    return jnp.maximum(value, 0.0) + 2.0 * ratio * series


def lane_of_head(pair, base, transposed=False):
    shape = (LANES, LANES)
    head = lax.broadcasted_iota(jnp.int32, shape, 1 if transposed else 0)
    lane = lax.broadcasted_iota(jnp.int32, shape, 0 if transposed else 1)
    return jnp.where(head == base + 2 * pair + lane // HDIM, 1.0, 0.0).astype(low)


def own_lanes(parts, side):
    lane = lax.broadcasted_iota(jnp.int32, parts[0].shape, 1)
    return tuple(jnp.where(lane // HDIM == side, p, jnp.zeros_like(p)) for p in parts)


def decays(column, row, after_row):
    mid = column.shape[0] // 2
    shape = (mid, mid)
    down = lax.broadcasted_iota(jnp.int32, shape, 0)
    across = lax.broadcasted_iota(jnp.int32, shape, 1)
    keep = (down <= across) if after_row else (down >= across)

    def block(rows, cols, masked):
        gap = column[rows] - row[:, cols]
        gap = -gap if after_row else gap
        return jnp.exp(jnp.where(keep, gap, -1e30)) if masked else jnp.exp(gap)

    early, late = slice(0, mid), slice(mid, 2 * mid)
    side = block(early, late, False) if after_row else block(late, early, False)
    return block(early, early, True), side, block(late, late, True)


def taps_of(extended, size, kernel, offset):
    total = offset + kernel[0:1] * extended[pl.ds(8 - CONVW + 1, size), :]
    for index in range(1, CONVW):
        total = total + kernel[index : index + 1] * extended[pl.ds(8 - CONVW + 1 + index, size), :]
    return total


def step_sizes(raw, heads):
    delta = softplus(raw + heads[0:1])
    change = -delta * jnp.exp(heads[1:2])
    size = raw.shape[0]
    below = lax.broadcasted_iota(jnp.int32, (size, size), 0) >= lax.broadcasted_iota(jnp.int32, (size, size), 1)
    return delta, change, exact_dot(below.astype(jnp.float32), change)


def forward_kernel(
    table_ref, z_ref, x_ref, shared_ref, step_ref, chan_ref, shared_chan_ref, head_ref,
    gated_ref, mixed_ref, state_ref, square_ref,
    tails, shared_tail, states,
    extended, shared_extended, meet, read_high, read_low, keys_high, keys_low,
    delta_all, run_all, run_rows,
):
    chunk, pair = pl.program_id(0), pl.program_id(1)
    size = x_ref.shape[0]
    base = table_ref[pl.num_programs(0)]

    @pl.when(pair == 0)
    def _():
        @pl.when(chunk == 0)
        def _():
            shared_tail[...] = jnp.zeros_like(shared_tail)
            tails[...] = jnp.zeros_like(tails)
            states[...] = jnp.zeros_like(states)

        shared_extended[0:8, :] = shared_tail[...]
        shared_extended[8:, :] = shared_ref[...]
        shared_tail[...] = shared_ref[size - 8 :, :]
        pre = taps_of(shared_extended, size, shared_chan_ref[...], shared_chan_ref[4:5, :])
        active = pre * jax.nn.sigmoid(pre)
        keys, read = halves(active[:, :NST]), halves(active[:, NST:])
        meet[...] = product(read, keys, 1)
        read_high[...], read_low[...] = read
        keys_high[...], keys_low[...] = halves(active[:, :NST].T)
        delta, _, running = step_sizes(step_ref[...], head_ref[...])
        for k, (d, r) in enumerate(zip(thirds(delta), thirds(running))):
            delta_all[k] = d
            run_all[k] = r
        run_rows[...] = running.T
        square_ref[...] = jnp.zeros_like(square_ref)

    chan = chan_ref[...]
    extended[0:8, :] = tails[pair]
    extended[8:, :] = x_ref[...]
    tails[pair] = x_ref[size - 8 :, :]
    pre = taps_of(extended, size, chan, chan[4:5])
    values = pre * jax.nn.sigmoid(pre)
    lanes = lane_of_head(pair, base)
    delta = spread([delta_all[k] for k in range(3)], lanes)
    running = spread([run_all[k] for k in range(3)], lanes)
    stepped = delta * values
    stepped_halves = halves(stepped)
    mid = size // 2
    top, bottom, sources = [], [], []
    for side in range(2):
        column = running[:, side * HDIM : side * HDIM + 1]
        row = run_rows[pl.ds(base + 2 * pair + side, 1), :]
        first, below, second = decays(column, row, False)
        top.append(halves(first * meet[:mid, :mid]))
        bottom.append(
            (halves(below * meet[mid:, :mid]), halves(second * meet[mid:, mid:]))
        )
        sources.append(own_lanes(stepped_halves, side))
    joined = lambda parts, axis: tuple(jnp.concatenate(p, axis=axis) for p in zip(*parts))
    upper = product(joined(top, 1), joined([tuple(p[:mid] for p in x) for x in sources], 0))
    lower = product(joined([joined(b, 1) for b in bottom], 1), joined(sources, 0))
    local = jnp.concatenate([upper, lower], axis=0)
    state = states[pair]
    state_ref[0, 0] = state
    carried = product((read_high[...], read_low[...]), halves(state))
    scanned = local + jnp.exp(running) * carried
    last = running[size - 1 :, :]
    tail = halves(stepped * jnp.exp(last - running))
    states[pair] = jnp.exp(last) * state + product((keys_high[...], keys_low[...]), tail)
    mixed = scanned + chan[5:6] * values
    z = z_ref[...]
    gated = mixed * (z * jax.nn.sigmoid(z))
    mixed_ref[...] = mixed
    gated_ref[...] = gated
    square_ref[...] += gated * gated


def gate_kernel(
    z_ref, gated_ref, mixed_ref, up_ref, chan_ref, stats_ref,
    z_grad_ref, mix_grad_ref, square_ref, gain_grad_ref,
):
    @pl.when(pl.program_id(0) == 0)
    def _():
        gain_grad_ref[...] = jnp.zeros_like(gain_grad_ref)

    stats = stats_ref[...].T
    scale, pull = stats[:, 0:1], stats[:, 1:2]
    z, gated = z_ref[...], gated_ref[...]
    scaled = up_ref[...] * scale
    z_gain = jax.nn.sigmoid(z)
    gated_grad = scaled * chan_ref[6:7, :] - gated * pull
    z_gate = gated_grad * z_gain
    mix_grad_ref[...] = z_gate * z
    z_grad = (z_gate * mixed_ref[...] * (1.0 + z * (1.0 - z_gain))).astype(z_grad_ref.dtype)
    z_grad_ref[...] = z_grad
    wide_grad = z_grad.astype(jnp.float32)
    square_ref[...] = jnp.sum(wide_grad * wide_grad, axis=1, keepdims=True)
    gain_grad_ref[0:1, :] += jnp.sum(scaled * gated, axis=0, keepdims=True)


def backward_kernel(
    first, chunks, table_ref, x_ref, x_before_ref, shared_ref, shared_before_ref, step_ref, chan_ref, shared_chan_ref, head_ref,
    mixed_ref, mix_grad_ref, state_ref, state_after_ref, carried_in, *refs
):
    carried_in = (carried_in,) + refs[:5]
    (
        x_grad_ref, square_ref, shared_grad_ref,
        state_grads, heads_after, shared_after, chan_grad_ref, shared_chan_grad_ref, head_grad_ref,
        extended, shared_extended, later, shared_later, shared_pre,
        meet, read_high, read_low, keys_high, keys_low, read_rows_high, read_rows_low,
        delta_all, change_all, run_all, run_rows, meet_grad, keys_grad, read_grad, run_grad, delta_grad, last_grad,
    ) = refs[-31:]
    carried_out = (state_grads, heads_after, shared_after, chan_grad_ref, shared_chan_grad_ref, head_grad_ref)
    pair, pairs = pl.program_id(0), pl.num_programs(0)
    size = x_ref.shape[0]
    base = table_ref[chunks]

    @pl.when(pair == 0)
    def _():
        for new, old in zip(carried_out, carried_in):
            new[...] = old[...]

        shared_extended[0:8, :] = jnp.zeros(shared_before_ref.shape, jnp.float32) if first else shared_before_ref[...]
        shared_extended[8:, :] = shared_ref[...]
        pre = taps_of(shared_extended, size, shared_chan_ref[...], shared_chan_ref[4:5, :])
        shared_pre[...] = pre
        active = pre * jax.nn.sigmoid(pre)
        keys, read = halves(active[:, :NST]), halves(active[:, NST:])
        meet[...] = product(keys, read, 1)
        read_high[...], read_low[...] = read
        keys_high[...], keys_low[...] = keys
        read_rows_high[...], read_rows_low[...] = halves(active[:, NST:].T)
        delta, change, running = step_sizes(step_ref[...], head_ref[...])
        for k, (d, r) in enumerate(zip(thirds(delta), thirds(running))):
            delta_all[k] = d
            run_all[k] = r
        change_all[...] = change
        run_rows[...] = running.T
        meet_grad[...] = jnp.zeros_like(meet_grad)
        keys_grad[...] = jnp.zeros_like(keys_grad)
        read_grad[...] = jnp.zeros_like(read_grad)
        run_grad[...] = jnp.zeros_like(run_grad)
        delta_grad[...] = jnp.zeros_like(delta_grad)
        last_grad[...] = jnp.zeros_like(last_grad)
        square_ref[...] = jnp.zeros_like(square_ref)

    chan = chan_ref[...]
    extended[0:8, :] = jnp.zeros(x_before_ref.shape, jnp.float32) if first else x_before_ref[...]
    extended[8:, :] = x_ref[...]
    pre = taps_of(extended, size, chan, chan[4:5])
    gain = jax.nn.sigmoid(pre)
    values = pre * gain
    lanes = lane_of_head(pair, base)
    delta = spread([delta_all[k] for k in range(3)], lanes)
    running = spread([run_all[k] for k in range(3)], lanes)
    stepped = delta * values

    mixed, mix_grad = mixed_ref[...], mix_grad_ref[...]
    last = running[size - 1 :, :]
    fall = jnp.exp(last - running)
    rise = jnp.exp(running)
    state, state_grad = state_ref[0, 0], state_grads[pair]
    state_halves, state_grad_halves = halves(state), halves(state_grad)
    keys = (keys_high[...], keys_low[...])
    stepped_grad = fall * product(keys, state_grad_halves)
    keys_grad[...] += product(halves(stepped * fall), state_grad_halves, 1)
    risen = halves(mix_grad * rise)
    read_grad[...] += product(risen, state_halves, 1)
    ended = jnp.sum(state_grad * state_after_ref[0, 0], axis=0, keepdims=True)
    state_grads[pair] = jnp.exp(last) * state_grad + product((read_rows_high[...], read_rows_low[...]), risen)

    mid = size // 2
    grad_halves, stepped_halves = halves(mix_grad), halves(stepped)
    early, late = slice(0, mid), slice(mid, size)
    joined = lambda parts, axis: tuple(jnp.concatenate(p, axis=axis) for p in zip(*parts))
    top, bottom, sources = [], [], []
    first_grad = side_grad = second_grad = 0.0
    for side in range(2):
        column = running[:, side * HDIM : side * HDIM + 1]
        row = run_rows[pl.ds(base + 2 * pair + side, 1), :]
        first, beside, second = decays(column, row, True)
        top.append((halves(first * meet[early, early]), halves(beside * meet[early, late])))
        bottom.append(halves(second * meet[late, late]))
        sources.append(own_lanes(grad_halves, side))
        mine = own_lanes(stepped_halves, side)
        wide_grad = product(tuple(p[early] for p in mine), grad_halves, 1)
        first_grad += first * wide_grad[:, early]
        side_grad += beside * wide_grad[:, late]
        second_grad += second * product(tuple(p[late] for p in mine), tuple(p[late] for p in grad_halves), 1)
    meet_grad[early, early] += first_grad
    meet_grad[early, late] += side_grad
    meet_grad[late, late] += second_grad
    upper = product(joined([joined(t, 1) for t in top], 1), joined(sources, 0))
    lower = product(joined(bottom, 1), joined([tuple(p[late] for p in x) for x in sources], 0))
    stepped_grad = stepped_grad + jnp.concatenate([upper, lower], axis=0)
    to_head = lane_of_head(pair, base, transposed=True)
    scanned = mixed - chan[5:6] * values
    run_grad[...] += spread(halves(mix_grad * scanned - stepped * stepped_grad), to_head)
    delta_grad[...] += spread(halves(values * stepped_grad), to_head)
    last_grad[...] += spread(thirds(jnp.broadcast_to(ended, (8, LANES))), to_head)

    values_grad = chan[5:6] * mix_grad + delta * stepped_grad
    pre_grad = values_grad * (gain * (1.0 + pre * (1.0 - gain)))
    later[0:size, :] = pre_grad
    later[size:, :] = heads_after[pair]
    heads_after[pair] = pre_grad[0:8]
    x_grad = chan[0:1] * later[pl.ds(CONVW - 1, size), :]
    for index in range(1, CONVW):
        x_grad = x_grad + chan[index : index + 1] * later[pl.ds(CONVW - 1 - index, size), :]
    x_grad = x_grad.astype(x_grad_ref.dtype)
    x_grad_ref[:, pl.ds(pl.multiple_of(pair * LANES, LANES), LANES)] = x_grad
    wide_grad = x_grad.astype(jnp.float32)
    square_ref[...] += wide_grad * wide_grad
    for index in range(CONVW):
        seen = extended[pl.ds(8 - CONVW + 1 + index, size), :]
        chan_grad_ref[pair, index : index + 1, :] += jnp.sum(pre_grad * seen, axis=0, keepdims=True)
    chan_grad_ref[pair, 4:5, :] += jnp.sum(pre_grad, axis=0, keepdims=True)
    chan_grad_ref[pair, 5:6, :] += jnp.sum(mix_grad * values, axis=0, keepdims=True)

    @pl.when(pair == pairs - 1)
    def _():
        meet_halves = halves(meet_grad[...])
        keys_all = keys_grad[...] + product(meet_halves, (read_high[...], read_low[...]))
        read_all = read_grad[...] + product(halves(meet_grad[...].T), (keys_high[...], keys_low[...]))
        pre_s = shared_pre[...]
        gain_s = jax.nn.sigmoid(pre_s)
        chan_s = shared_chan_ref[...]
        grad_s = jnp.concatenate([keys_all, read_all], axis=1) * (gain_s * (1.0 + pre_s * (1.0 - gain_s)))
        shared_later[0:size, :] = grad_s
        shared_later[size:, :] = shared_after[...]
        shared_after[...] = grad_s[0:8]
        out = chan_s[0:1] * shared_later[pl.ds(CONVW - 1, size), :]
        for index in range(1, CONVW):
            out = out + chan_s[index : index + 1] * shared_later[pl.ds(CONVW - 1 - index, size), :]
        shared_grad_ref[...] = out
        for index in range(CONVW):
            seen = shared_extended[pl.ds(8 - CONVW + 1 + index, size), :]
            shared_chan_grad_ref[index : index + 1, :] += jnp.sum(grad_s * seen, axis=0, keepdims=True)
        shared_chan_grad_ref[4:5, :] += jnp.sum(grad_s, axis=0, keepdims=True)

        above = lax.broadcasted_iota(jnp.int32, (size, size), 0) <= lax.broadcasted_iota(jnp.int32, (size, size), 1)
        change_grad = exact_dot(above.astype(jnp.float32), run_grad[...]) + last_grad[0:1, :]
        rate = jnp.exp(head_ref[1:2, :])
        raw = step_ref[...] + head_ref[0:1, :]
        raw_grad = (delta_grad[...] - change_grad * rate) * jax.nn.sigmoid(raw)
        raw_low = raw_grad.astype(x_grad_ref.dtype)
        x_grad_ref[:, x_grad_ref.shape[1] - LANES :] = raw_low
        wide_raw = raw_low.astype(jnp.float32)
        square_ref[...] += wide_raw * wide_raw
        head_grad_ref[0:1, :] += jnp.sum(raw_grad, axis=0, keepdims=True)
        head_grad_ref[1:2, :] += jnp.sum(change_grad * change_all[...], axis=0, keepdims=True)


def run_forward(table, projected, chan, shared_chan, head_rows):
    length, wide = projected.shape[0], chan.shape[1]
    chunks, pairs = length // SPAN, wide // LANES
    f32 = jnp.float32
    block = pl.BlockSpec((SPAN, LANES), lambda c, p, t: (t[c], p))
    return pl.pallas_call(
        forward_kernel,
        grid_spec=pltpu.PrefetchScalarGridSpec(
            num_scalar_prefetch=1,
            grid=(chunks, pairs),
            in_specs=[
                block,
                pl.BlockSpec((SPAN, LANES), lambda c, p, t: (t[c], pairs + 2 + p)),
                pl.BlockSpec((SPAN, 2 * NST), lambda c, p, t: (t[c], pairs // 2)),
                pl.BlockSpec((SPAN, LANES), lambda c, p, t: (t[c], 2 * pairs + 2)),
                pl.BlockSpec((8, LANES), lambda c, p, t: (0, p)),
                pl.BlockSpec((8, 2 * NST), lambda c, p, t: (0, 0)),
                pl.BlockSpec((8, LANES), lambda c, p, t: (0, 0)),
            ],
            out_specs=[
                block,
                block,
                pl.BlockSpec((1, 1, NST, LANES), lambda c, p, t: (c, p, 0, 0)),
                pl.BlockSpec((SPAN, LANES), lambda c, p, t: (t[c], 0)),
            ],
            scratch_shapes=[
                pltpu.VMEM((pairs, 8, LANES), f32),
                pltpu.VMEM((8, 2 * NST), f32),
                pltpu.VMEM((pairs, NST, LANES), f32),
                pltpu.VMEM((SPAN + 8, LANES), f32),
                pltpu.VMEM((SPAN + 8, 2 * NST), f32),
                pltpu.VMEM((SPAN, SPAN), f32),
                pltpu.VMEM((SPAN, NST), low),
                pltpu.VMEM((SPAN, NST), low),
                pltpu.VMEM((NST, SPAN), low),
                pltpu.VMEM((NST, SPAN), low),
                pltpu.VMEM((3, SPAN, LANES), low),
                pltpu.VMEM((3, SPAN, LANES), low),
                pltpu.VMEM((LANES, SPAN), f32),
            ],
        ),
        out_shape=[
            jax.ShapeDtypeStruct((length, wide), f32),
            jax.ShapeDtypeStruct((length, wide), f32),
            jax.ShapeDtypeStruct((chunks, pairs, NST, LANES), f32),
            jax.ShapeDtypeStruct((length, LANES), f32),
        ],
        name="mixer_forward",
    )(table, projected, projected, projected, projected, chan, shared_chan, head_rows)


def run_gate(projected, gated, mixed, up, chan, stats):
    length, wide = gated.shape
    f32 = jnp.float32
    size = SPAN // 2
    block = pl.BlockSpec((size, wide), lambda c: (c, 0))
    whole = pl.BlockSpec((8, wide), lambda c: (0, 0))
    return pl.pallas_call(
        gate_kernel,
        grid=(length // size,),
        in_specs=[block, block, block, block, whole, pl.BlockSpec((8, size), lambda c: (0, c))],
        out_specs=[block, block, pl.BlockSpec((size, 1), lambda c: (c, 0)), whole],
        out_shape=[
            jax.ShapeDtypeStruct((length, wide), low),
            jax.ShapeDtypeStruct((length, wide), f32),
            jax.ShapeDtypeStruct((length, 1), f32),
            jax.ShapeDtypeStruct((8, wide), f32),
        ],
        name="gate_backward",
    )(projected, gated, mixed, up, chan, stats)


def run_backward(chunk, table, projected, chan, shared_chan, head_rows, mixed, mix_grad, states, carried, before):
    length, wide = projected.shape[0], chan.shape[1]
    chunks, pairs = length // SPAN, wide // LANES
    f32 = jnp.float32
    lines = SPAN // 8
    earlier, following = max(chunk - 1, 0), min(chunk + 1, chunks - 1)
    block = pl.BlockSpec((SPAN, LANES), lambda p, t: (t[chunk], p))
    flat = pl.BlockSpec((8, 2 * NST), lambda p, t: (0, 0))
    head = pl.BlockSpec((8, LANES), lambda p, t: (0, 0))
    carries = [
        pl.BlockSpec((pairs, NST, LANES), lambda p, t: (0, 0, 0)),
        pl.BlockSpec((pairs, 8, LANES), lambda p, t: (0, 0, 0)),
        flat,
        pl.BlockSpec((pairs, 8, LANES), lambda p, t: (0, 0, 0)),
        flat,
        head,
    ]
    carried_shapes = [jax.ShapeDtypeStruct(c.shape, f32) for c in carried]
    return pl.pallas_call(
        functools.partial(backward_kernel, chunk == 0, chunks),
        grid_spec=pltpu.PrefetchScalarGridSpec(
            num_scalar_prefetch=1,
            grid=(pairs,),
            in_specs=[
                pl.BlockSpec((SPAN, LANES), lambda p, t: (t[chunk], pairs + 2 + p)),
                pl.BlockSpec((8, LANES), lambda p, t: (t[earlier] * lines + lines - 1, pairs + 2 + p)),
                pl.BlockSpec((SPAN, 2 * NST), lambda p, t: (t[chunk], pairs // 2)),
                pl.BlockSpec((8, 2 * NST), lambda p, t: (t[earlier] * lines + lines - 1, pairs // 2)),
                pl.BlockSpec((SPAN, LANES), lambda p, t: (t[chunk], 2 * pairs + 2)),
                pl.BlockSpec((8, LANES), lambda p, t: (0, p)),
                flat,
                head,
                block,
                block,
                pl.BlockSpec((1, 1, NST, LANES), lambda p, t: (chunk, p, 0, 0)),
                pl.BlockSpec((1, 1, NST, LANES), lambda p, t: (following, p, 0, 0)),
            ]
            + carries
            + [pl.BlockSpec(memory_space=pl.ANY)] * len(before),
            out_specs=[
                pl.BlockSpec((SPAN, wide + LANES), lambda p, t: (t[chunk], 0)),
                pl.BlockSpec((SPAN, LANES), lambda p, t: (t[chunk], 0)),
                pl.BlockSpec((SPAN, 2 * NST), lambda p, t: (t[chunk], 0)),
            ]
            + carries,
            scratch_shapes=[
                pltpu.VMEM((SPAN + 8, LANES), f32),
                pltpu.VMEM((SPAN + 8, 2 * NST), f32),
                pltpu.VMEM((SPAN + 8, LANES), f32),
                pltpu.VMEM((SPAN + 8, 2 * NST), f32),
                pltpu.VMEM((SPAN, 2 * NST), f32),
                pltpu.VMEM((SPAN, SPAN), f32),
                pltpu.VMEM((SPAN, NST), low),
                pltpu.VMEM((SPAN, NST), low),
                pltpu.VMEM((SPAN, NST), low),
                pltpu.VMEM((SPAN, NST), low),
                pltpu.VMEM((NST, SPAN), low),
                pltpu.VMEM((NST, SPAN), low),
                pltpu.VMEM((3, SPAN, LANES), low),
                pltpu.VMEM((SPAN, LANES), f32),
                pltpu.VMEM((3, SPAN, LANES), low),
                pltpu.VMEM((LANES, SPAN), f32),
                pltpu.VMEM((SPAN, SPAN), f32),
                pltpu.VMEM((SPAN, NST), f32),
                pltpu.VMEM((SPAN, NST), f32),
                pltpu.VMEM((SPAN, LANES), f32),
                pltpu.VMEM((SPAN, LANES), f32),
                pltpu.VMEM((8, LANES), f32),
            ],
        ),
        out_shape=[
            jax.ShapeDtypeStruct((length, wide + LANES), low),
            jax.ShapeDtypeStruct((length, LANES), f32),
            jax.ShapeDtypeStruct((length, 2 * NST), f32),
        ]
        + carried_shapes,
        input_output_aliases={19 + k: k for k in range(len(before))},
        name="mixer_backward",
    )(
        table, projected, projected, projected, projected, projected, chan, shared_chan, head_rows,
        mixed, mix_grad, states, states, *carried, *before,
    )


def halve(block, left, bit, axis):
    place = left.index(bit)
    own = (lax.axis_index(axis) & bit) // bit
    keep = lax.dynamic_index_in_dim(block, own, place, keepdims=False)
    send = lax.dynamic_index_in_dim(block, 1 - own, place, keepdims=False)
    return keep + swap(send, axis, bit), [b for b in left if b != bit]


class Scatter:
    def __init__(self, arrays, axis):
        self.axis = axis
        size = lax.axis_size(axis)
        bits = [1 << k for k in range(size.bit_length() - 1)]
        upper = bits[1:]
        turned = upper[len(upper) // 2 :] + upper[: len(upper) // 2]
        self.orders = [bits[:1] + (upper if k % 2 == 0 else turned) for k in range(len(arrays))]
        self.left = [bits[::-1] for _ in arrays]
        self.blocks = [
            a.reshape((2,) * len(bits) + (a.shape[0] // size,) + a.shape[1:]) for a in arrays
        ]
        self.steps = len(bits)
        self.done = 0

    def step(self):
        for k in range(len(self.blocks)):
            self.blocks[k], self.left[k] = halve(
                self.blocks[k], self.left[k], self.orders[k][self.done], self.axis
            )
        self.done += 1

    def finish(self):
        while self.done < self.steps:
            self.step()
        return self.blocks


def adamw_update(param, grad, first, second, rate, decay):
    first_new = beta_one * first + (1.0 - beta_one) * grad
    second_new = beta_two * second + (1.0 - beta_two) * grad * grad
    corrected_first = first_new / (1.0 - beta_one**adam_step)
    corrected_second = second_new / (1.0 - beta_two**adam_step)
    param_new = param - rate * (
        corrected_first / (jnp.sqrt(corrected_second) + adam_eps) + decay * param
    )
    return (param_new, first_new, second_new)


def dot(left, right):
    return jnp.dot(left, right, preferred_element_type=jnp.float32)


def body(
    block_input,
    cotangent,
    norm_gain,
    in_weight,
    conv_weight,
    conv_bias,
    step_bias,
    decay_log,
    skip_gain,
    gated_gain,
    out_weight,
    first_norm_gain,
    second_norm_gain,
    first_in_weight,
    second_in_weight,
    first_conv_weight,
    second_conv_weight,
    first_conv_bias,
    second_conv_bias,
    first_step_bias,
    second_step_bias,
    first_decay_log,
    second_decay_log,
    first_skip_gain,
    second_skip_gain,
    first_gated_gain,
    second_gated_gain,
    first_out_weight,
    second_out_weight,
):
    ranks, rank = lax.axis_size("seq"), lax.axis_index("seq")
    groups = lax.axis_size("dp")
    devices = ranks * groups
    wide, heads = E // ranks, NHEADS // ranks
    rows = in_weight.shape[0]
    width = rows * devices
    taps = conv_bias.shape[0]
    channels = taps * devices
    step_at = 2 * E + 2 * NST
    spare = LANES - (in_weight.shape[1] - step_at)

    packed = jnp.concatenate(
        [norm_gain, conv_weight.reshape(-1), conv_bias, gated_gain]
    ).astype(low).astype(jnp.float32)
    gains = gated_gain.shape[0]
    filled = packed.shape[0]
    lines = -(-filled // LANES)
    packed = jnp.pad(packed, (0, lines * LANES - filled)).reshape(lines, LANES)
    small_line = gather_direct(packed, "seq")
    small = gather_bits(small_line, "dp")
    small = small.reshape(devices, lines * LANES)
    norm_float = small[:, :rows].reshape(-1)
    kernel_float = small[:, rows : rows + CONVW * taps].reshape(devices, CONVW, taps)
    kernel_float = kernel_float.transpose(1, 0, 2).reshape(CONVW, channels)
    offset_float = small[:, rows + CONVW * taps : rows + (CONVW + 1) * taps].reshape(-1)
    gated_float = small[:, rows + (CONVW + 1) * taps : filled].reshape(-1)
    kernel_own = lax.dynamic_slice_in_dim(kernel_float, rank * wide, wide, 1)
    offset_own = lax.dynamic_slice_in_dim(offset_float, rank * wide, wide, 0)
    gated_own = lax.dynamic_slice_in_dim(gated_float, rank * wide, wide, 0)
    skip_own = lax.dynamic_slice_in_dim(skip_gain, rank * heads, heads, 0)

    in_low = in_weight.astype(low)
    out_low = out_weight.astype(low)

    def for_rank(j):
        return jnp.concatenate(
            [
                lax.dynamic_slice_in_dim(in_low, j * wide, wide, 1),
                in_low[:, 2 * E : step_at],
                lax.dynamic_slice_in_dim(in_low, E + j * wide, wide, 1),
                jnp.pad(in_low[:, step_at:], ((0, 0), (0, spare))),
                lax.dynamic_slice_in_dim(out_low, j * wide, wide, 1),
            ],
            axis=1,
        )

    columns = 2 * NST + 2 * wide + LANES
    weights_arrived = []
    for turn in range(1, ranks):
        weights_arrived.append(shift(for_rank((rank + turn) % ranks), "seq", turn))

    tokens, upstream = block_input[0], cotangent[0]
    span = tokens.shape[0]
    length = span * ranks
    inverse = lax.rsqrt(jnp.mean(tokens * tokens, axis=-1, keepdims=True) + norm_eps)
    hidden_own = (tokens * inverse * norm_float).astype(low)
    weights_arrived = [after(part, hidden_own) for part in weights_arrived]
    weight_rows = jnp.zeros((ranks, rows, columns + wide), low)
    weight_rows = lax.dynamic_update_index_in_dim(weight_rows, for_rank(rank), rank, 0)
    for turn in range(1, ranks):
        weight_rows = lax.dynamic_update_index_in_dim(
            weight_rows, weights_arrived[turn - 1], (rank + ranks - turn) % ranks, 0
        )
    weight_rows = weight_rows.reshape(ranks * rows, columns + wide)
    in_full, out_full = gather_rows([weight_rows[:, :columns], weight_rows[:, columns:]], "dp")

    line_parts = near_parts(hidden_own, "seq")
    line_parts = [after(part, in_full, out_full) for part in line_parts]
    up_parts = near_parts(after(upstream.astype(low), *line_parts), "seq")
    hidden = jnp.stack(line_parts).reshape(length, width)

    projected = dot(hidden, in_full)
    none = jnp.zeros((1, wide), jnp.float32)
    chan = jnp.concatenate(
        [kernel_own, offset_own[None], jnp.repeat(skip_own, HDIM)[None], gated_own[None], none], axis=0
    )
    shared_chan = jnp.concatenate(
        [kernel_float[:, E:], offset_float[None, E:], jnp.zeros((3, 2 * NST), jnp.float32)], axis=0
    )
    head_rows = jnp.pad(jnp.stack([step_bias, decay_log]), ((0, 6), (0, LANES - NHEADS)))
    pairs, chunks = wide // LANES, length // SPAN
    per_rank = span // SPAN
    order = jnp.arange(chunks, dtype=jnp.int32)
    order = (rank + ranks - order // per_rank) % ranks * per_rank + order % per_rank
    table = jnp.concatenate([order, jnp.reshape(rank * heads, (1,))]).astype(jnp.int32)
    zeros = functools.partial(jnp.zeros, dtype=jnp.float32)
    gated, mixed, states, squares = run_forward(table, projected, chan, shared_chan, head_rows)
    packed_length = (ranks, span // LANES, LANES)
    square_sum = sum_near(jnp.sum(squares, axis=1).reshape(packed_length), "seq").reshape(length)
    scale = lax.rsqrt(square_sum / E + norm_eps)
    normed_low = (gated * scale[:, None] * gated_own).astype(low)
    branch_factor = 2.0 ** (14 - math.ceil(math.log2(0.17 * math.sqrt(E * wide))))
    out_half = (dot(normed_low, out_full.T) * branch_factor).astype(half).reshape(ranks, span, width)

    upstream_low = jnp.stack([after(part, out_half) for part in up_parts]).reshape(length, width)
    normed_grad = dot(upstream_low, out_full)
    pull_sum = jnp.sum(normed_grad * gated_own * gated, axis=1).reshape(packed_length)
    pull_sum = sum_near(pull_sum, "seq").reshape(length)
    stats = jnp.stack([scale, scale * scale * scale * (pull_sum / E)])
    stats = jnp.pad(stats, ((0, 6), (0, 0)))
    gate_low, mix_grad, gate_square, gain_rows = run_gate(projected, gated, mixed, normed_grad, chan, stats)
    gated_grad = gain_rows[0]

    branch_parts = send_near(out_half, "seq")

    out_grad_part = dot(upstream_low.T, normed_low)
    early = Scatter([out_grad_part, dot(hidden.T, gate_low)], "dp")
    carried = (
        zeros((pairs, NST, LANES)), zeros((pairs, 8, LANES)), zeros((8, 2 * NST)),
        zeros((pairs, 8, LANES)), zeros((8, 2 * NST)), zeros((8, LANES)),
    )
    outputs = ()
    ready = (gate_low,)
    for turn in range(chunks):
        if early.done < early.steps and turn != 2:
            early.step()
        mix_grad = after(mix_grad, *ready)
        result = run_backward(
            chunks - 1 - turn, table, projected, chan, shared_chan, head_rows, mixed, mix_grad, states, carried, outputs
        )
        outputs, carried = tuple(result[:3]), tuple(result[3:])
        ready = tuple(early.blocks) if turn != 1 else ()
    conv_low, conv_square, shared_grad = outputs
    _, _, _, chan_grad, shared_chan_grad, head_grad = carried
    early.finish()

    largest = jnp.max(gate_square.reshape(ranks, span) + jnp.sum(conv_square.reshape(ranks, span, LANES), axis=2), axis=1)
    bound = 0.1565 * math.sqrt(2 * wide + NHEADS) * jnp.sqrt(largest)
    power = jnp.clip(jnp.ceil(jnp.log2(bound)) - 14.0, -120.0, 120.0)
    shared_parts = shared_grad.reshape(ranks, span, 2 * NST)
    lines_of_power = jnp.broadcast_to(power[:, None, None], (ranks, 8, 2 * NST))
    shared_sent = send_near(jnp.concatenate([shared_parts, lines_of_power], axis=1), "seq")

    def hidden_rows(turn):
        own = slice(turn * span, (turn + 1) * span)
        return dot(gate_low[own], in_full[:, :wide].T) + dot(conv_low[own], in_full[:, wide + 2 * NST :].T)

    hidden_parts, hidden_halves = [], []
    for turn in range(1, ranks):
        hidden_halves.append((hidden_rows(turn) * jnp.exp2(-power[turn])).astype(half))
        hidden_parts.append(shift(hidden_halves[-1], "seq", ranks - turn))
    split = 4 * LANES
    conv_parts = [dot(hidden.T, conv_low[:, :split]), dot(hidden.T, conv_low[:, split:])]
    late = Scatter(conv_parts, "dp")
    conv_own, normed_own = conv_low[:span], normed_low[:span]
    for turn in range(late.steps):
        if turn == 1:
            conv_own, normed_own = after(conv_own, *late.blocks), after(normed_own, *late.blocks)
        late.step()
    shared_own = shared_parts[0]
    for part in shared_sent:
        shared_own = shared_own + part[:span]
    shared_own = shared_own.astype(low)
    hidden_grad = dot(gate_low[:span], in_full[:, :wide].T) + dot(conv_own, in_full[:, wide + 2 * NST :].T)
    branch = tokens + dot(normed_own, out_full.T)
    for part in branch_parts:
        branch = branch + part.astype(jnp.float32) * (1.0 / branch_factor)
    block_output = branch[None]
    last = Scatter([dot(hidden_own.T, shared_own)], "dp")
    last.finish()

    chan_grad = chan_grad.transpose(1, 0, 2).reshape(8, wide)
    kernel_grad, offset_grad = chan_grad[:CONVW], chan_grad[4]
    skip_grad = jnp.sum(chan_grad[5].reshape(heads, HDIM), axis=1)
    kernel_shared_grad, offset_shared_grad = shared_chan_grad[:CONVW], shared_chan_grad[4]

    sums_all = jnp.concatenate(
        [block.reshape(ranks, rows, -1) for block in (late.blocks + last.blocks + early.blocks)], axis=2
    )
    conv_wide = wide + LANES
    packed_sums = pack_half(sums_all, jnp.max(jnp.abs(sums_all), axis=-1, keepdims=True))
    hidden_parts = [after(part, packed_sums, block_output) for part in hidden_parts]
    power_parts = [after(part, packed_sums)[span, 0] for part in shared_sent]
    collected = sums_all
    for turn in range(1, ranks):
        arrived = shift(pick(packed_sums, (rank + turn) % ranks), "seq", turn)
        collected = lax.dynamic_update_index_in_dim(
            collected, unpack_half(arrived), (rank + ranks - turn) % ranks, 0
        )
    at = conv_wide + 2 * NST
    shared_sum = sum(collected[j, :, wide:at] for j in range(ranks))
    grad_in_weight = jnp.concatenate(
        [collected[j, :, at + wide :] for j in range(ranks)]
        + [collected[j, :, :wide] for j in range(ranks)]
        + [shared_sum[:, LANES:], shared_sum[:, : LANES - spare]],
        axis=1,
    )
    grad_out_weight = jnp.concatenate([collected[j, :, at : at + wide] for j in range(ranks)], axis=1)

    hidden_grad = hidden_grad + dot(shared_own, in_full[:, wide : wide + 2 * NST].T)
    for part, exponent in zip(hidden_parts, power_parts):
        hidden_grad = hidden_grad + part.astype(jnp.float32) * jnp.exp2(exponent)
    scaled = tokens * inverse
    gain_grad = jnp.sum(hidden_grad * scaled, axis=0)
    inner = hidden_grad * norm_float
    token_grad = inverse * (inner - scaled * jnp.mean(inner * scaled, axis=-1, keepdims=True))
    input_grad = (upstream + token_grad)[None]

    def placed(own, shared):
        full = jnp.zeros(own.shape[:-1] + (E,), jnp.float32)
        full = lax.dynamic_update_slice_in_dim(full, own, rank * wide, own.ndim - 1)
        return jnp.concatenate([full, shared], axis=-1)

    kernel_all = placed(kernel_grad, kernel_shared_grad).reshape(CONVW, devices, taps)
    kernel_all = kernel_all.transpose(1, 0, 2).reshape(devices, CONVW * taps)
    offset_all = placed(offset_grad, offset_shared_grad).reshape(devices, taps)
    gated_all = lax.dynamic_update_slice_in_dim(jnp.zeros((E,), jnp.float32), gated_grad, rank * wide, 0)
    skip_all = lax.dynamic_update_slice_in_dim(jnp.zeros((NHEADS,), jnp.float32), skip_grad, rank * heads, 0)
    head_all = jnp.concatenate([head_grad[0, :NHEADS], head_grad[1, :NHEADS], skip_all])
    terms = jnp.concatenate(
        [
            kernel_all,
            offset_all,
            gated_all.reshape(devices, gains),
            jnp.broadcast_to(head_all[None], (devices, 3 * NHEADS)),
        ],
        axis=1,
    )
    used = terms.shape[1]
    term_lines = -(-used // LANES)
    terms = jnp.pad(terms, ((0, 0), (0, term_lines * LANES - used)))
    terms = terms.reshape(groups, ranks, term_lines, LANES)
    norm_lines = -(-rows // LANES)
    norm_terms = jnp.pad(gain_grad.reshape(devices, rows), ((0, 0), (0, norm_lines * LANES - rows)))
    norm_terms = norm_terms.reshape(groups, ranks, norm_lines, LANES)
    term_lines += norm_lines
    terms = jnp.concatenate([norm_terms, terms], axis=2).reshape(groups, ranks * term_lines, LANES)
    summed = scatter_bits(terms, "dp").reshape(ranks, term_lines, LANES)
    summed = exchange_sum(summed, "seq").reshape(-1)
    grad_norm_gain = summed[:rows]
    at = norm_lines * LANES
    grad_conv_weight = summed[at : at + CONVW * taps].reshape(CONVW, taps)
    at += CONVW * taps
    grad_conv_bias = summed[at : at + taps]
    at += taps
    grad_gated_gain = summed[at : at + gains]
    at += gains
    grad_step_bias, grad_decay_log, grad_skip_gain = (
        summed[at + k * NHEADS : at + (k + 1) * NHEADS] for k in range(3)
    )
    new_norm_gain, new_first_norm_gain, new_second_norm_gain = adamw_update(
        norm_gain, grad_norm_gain, first_norm_gain, second_norm_gain, rate_vector, 0.0
    )
    new_in_weight, new_first_in_weight, new_second_in_weight = adamw_update(
        in_weight, grad_in_weight, first_in_weight, second_in_weight, rate_matrix, weight_decay
    )
    new_conv_weight, new_first_conv_weight, new_second_conv_weight = adamw_update(
        conv_weight, grad_conv_weight, first_conv_weight, second_conv_weight, rate_vector, 0.0
    )
    new_conv_bias, new_first_conv_bias, new_second_conv_bias = adamw_update(
        conv_bias, grad_conv_bias, first_conv_bias, second_conv_bias, rate_vector, 0.0
    )
    new_step_bias, new_first_step_bias, new_second_step_bias = adamw_update(
        step_bias, grad_step_bias, first_step_bias, second_step_bias, rate_vector, 0.0
    )
    new_decay_log, new_first_decay_log, new_second_decay_log = adamw_update(
        decay_log, grad_decay_log, first_decay_log, second_decay_log, rate_vector, 0.0
    )
    new_skip_gain, new_first_skip_gain, new_second_skip_gain = adamw_update(
        skip_gain, grad_skip_gain, first_skip_gain, second_skip_gain, rate_vector, 0.0
    )
    new_gated_gain, new_first_gated_gain, new_second_gated_gain = adamw_update(
        gated_gain, grad_gated_gain, first_gated_gain, second_gated_gain, rate_vector, 0.0
    )
    new_out_weight, new_first_out_weight, new_second_out_weight = adamw_update(
        out_weight, grad_out_weight, first_out_weight, second_out_weight, rate_matrix, weight_decay
    )
    return (
        block_output,
        input_grad,
        grad_norm_gain,
        grad_in_weight,
        grad_conv_weight,
        grad_conv_bias,
        grad_step_bias,
        grad_decay_log,
        grad_skip_gain,
        grad_gated_gain,
        grad_out_weight,
        new_norm_gain,
        new_first_norm_gain,
        new_second_norm_gain,
        new_in_weight,
        new_first_in_weight,
        new_second_in_weight,
        new_conv_weight,
        new_first_conv_weight,
        new_second_conv_weight,
        new_conv_bias,
        new_first_conv_bias,
        new_second_conv_bias,
        new_step_bias,
        new_first_step_bias,
        new_second_step_bias,
        new_decay_log,
        new_first_decay_log,
        new_second_decay_log,
        new_skip_gain,
        new_first_skip_gain,
        new_second_skip_gain,
        new_gated_gain,
        new_first_gated_gain,
        new_second_gated_gain,
        new_out_weight,
        new_first_out_weight,
        new_second_out_weight,
    )


def solution(mesh):
    in_specs = (
        P("dp", "seq", None),
        P("dp", "seq", None),
        P(("dp", "seq")),
        P(("dp", "seq"), None),
        P(None, ("dp", "seq")),
        P(("dp", "seq")),
        P(),
        P(),
        P(),
        P(("dp", "seq")),
        P(("dp", "seq"), None),
        P(("dp", "seq")),
        P(("dp", "seq")),
        P(("dp", "seq"), None),
        P(("dp", "seq"), None),
        P(None, ("dp", "seq")),
        P(None, ("dp", "seq")),
        P(("dp", "seq")),
        P(("dp", "seq")),
        P(),
        P(),
        P(),
        P(),
        P(),
        P(),
        P(("dp", "seq")),
        P(("dp", "seq")),
        P(("dp", "seq"), None),
        P(("dp", "seq"), None),
    )
    out_specs = (
        P("dp", "seq", None),
        P("dp", "seq", None),
        P(("dp", "seq")),
        P(("dp", "seq"), None),
        P(None, ("dp", "seq")),
        P(("dp", "seq")),
        P(),
        P(),
        P(),
        P(("dp", "seq")),
        P(("dp", "seq"), None),
        P(("dp", "seq")),
        P(("dp", "seq")),
        P(("dp", "seq")),
        P(("dp", "seq"), None),
        P(("dp", "seq"), None),
        P(("dp", "seq"), None),
        P(None, ("dp", "seq")),
        P(None, ("dp", "seq")),
        P(None, ("dp", "seq")),
        P(("dp", "seq")),
        P(("dp", "seq")),
        P(("dp", "seq")),
        P(),
        P(),
        P(),
        P(),
        P(),
        P(),
        P(),
        P(),
        P(),
        P(("dp", "seq")),
        P(("dp", "seq")),
        P(("dp", "seq")),
        P(("dp", "seq"), None),
        P(("dp", "seq"), None),
        P(("dp", "seq"), None),
    )

    return jax.shard_map(body, mesh=mesh, in_specs=in_specs, out_specs=out_specs, check_vma=False)
```

```python
import functools
import math

import jax
import jax.numpy as jnp
from jax import lax
from jax.experimental import pallas as pl
from jax.experimental.pallas import tpu as pltpu
from jax.sharding import PartitionSpec as P


E = 3072
NST = 128
NHEADS = 48
HDIM = 64
CONVW = 4
SPAN = 256
LANES = 128


low = jnp.bfloat16
half = jnp.float16
highest = lax.Precision.HIGHEST
beta_one = 0.9
beta_two = 0.95
adam_step = 10.0
adam_eps = 1e-08
rate_matrix = 0.01
rate_vector = 0.3
weight_decay = 0.1
norm_eps = 1e-05


def shift(block, axis, distance):
    size = lax.axis_size(axis)
    return lax.ppermute(block, axis, [(i, (i + distance) % size) for i in range(size)])


def step_to(block, axis, distance):
    size = lax.axis_size(axis)
    route = [(i, i + distance) for i in range(size) if 0 <= i + distance < size]
    return lax.ppermute(block, axis, route)


def swap(block, axis, bit):
    return lax.ppermute(block, axis, [(i, i ^ bit) for i in range(lax.axis_size(axis))])


def pick(stacked, index):
    return lax.dynamic_index_in_dim(stacked, index, 0, keepdims=False)


def exchange_sum(stacked, axis):
    size, here = lax.axis_size(axis), lax.axis_index(axis)
    arrived = [shift(pick(stacked, (here + turn) % size), axis, turn) for turn in range(1, size)]
    total = pick(stacked, here)
    for part in arrived:
        total = total + part
    return total


def after(value, *others):
    return lax.optimization_barrier((value,) + others)[0]


def pack_half(parts, bound):
    power = jnp.clip(jnp.ceil(jnp.log2(bound)) - 14.0, -120.0, 120.0)
    scaled = (parts * jnp.exp2(-power)).astype(half)
    return jnp.concatenate([scaled, jnp.broadcast_to(power.astype(half), parts.shape[:-1] + (LANES,))], axis=-1)


def unpack_half(message):
    width = message.shape[-1] - LANES
    return message[..., :width].astype(jnp.float32) * jnp.exp2(message[..., width : width + 1].astype(jnp.float32))


def near_parts(block, axis):
    size, here = lax.axis_size(axis), lax.axis_index(axis)
    if size != 4:
        return [block] + [shift(block, axis, turn) for turn in range(1, size)]
    below, above = step_to(block, axis, 1), step_to(block, axis, -1)
    across = shift(block, axis, 2)
    far = lax.ppermute(across, axis, [(2, 3), (1, 0)])
    return [block, jnp.where(here == 0, far, below), across, jnp.where(here == size - 1, far, above)]


def send_near(stacked, axis):
    return [shift(stacked[turn], axis, lax.axis_size(axis) - turn) for turn in range(1, lax.axis_size(axis))]


def slots_of(own_blocks, packed, axis):
    size, here = lax.axis_size(axis), lax.axis_index(axis)
    arrived = [shift(pick(packed, (here + turn) % size), axis, turn) for turn in range(1, size)]
    return [pick(own_blocks, here)] + arrived


def gather_direct(block, axis):
    size, here = lax.axis_size(axis), lax.axis_index(axis)
    arrived = [block] + [shift(block, axis, turn) for turn in range(1, size)]
    result = jnp.stack(arrived)
    return jnp.take(result, (here + size - jnp.arange(size)) % size, axis=0)


def sum_near(stacked, axis):
    total = stacked
    for turn in range(1, lax.axis_size(axis)):
        total = total + jnp.roll(shift(stacked, axis, turn), turn, axis=0)
    return total


def gather_bits(block, axis):
    here = lax.axis_index(axis)
    result, bit = block[None], 1
    while bit < lax.axis_size(axis):
        other = swap(result, axis, bit)
        upper = (here & bit) > 0
        result = jnp.concatenate(
            [jnp.where(upper, other, result), jnp.where(upper, result, other)], axis=0
        )
        bit *= 2
    return result


def gather_rows(blocks, axis):
    size, here = lax.axis_size(axis), lax.axis_index(axis)
    bits = [1 << k for k in range(size.bit_length() - 1)]
    upper = bits[1:]
    turned = upper[len(upper) // 2 :] + upper[: len(upper) // 2]
    parts, paths = [], []
    for block in blocks:
        rows = block.shape[0] // 2
        parts += [p.reshape((1,) * len(bits) + p.shape) for p in (block[:rows], block[rows:])]
        paths += [upper + bits[:1], turned + bits[:1]]
    for step in range(len(bits)):
        arrived = [swap(p, axis, path[step]) for p, path in zip(parts, paths)]
        for k, path in enumerate(paths):
            place = bits[::-1].index(path[step])
            up = (here & path[step]) > 0
            parts[k] = jnp.concatenate(
                [jnp.where(up, arrived[k], parts[k]), jnp.where(up, parts[k], arrived[k])], axis=place
            )
    return [
        jnp.concatenate(parts[2 * k : 2 * k + 2], axis=len(bits)).reshape(-1, block.shape[1])
        for k, block in enumerate(blocks)
    ]


def scatter_bits(stacked, axis):
    here, size = lax.axis_index(axis), lax.axis_size(axis)
    bit = 1
    rest = stacked
    while bit < size:
        pairs = rest.reshape((rest.shape[0] // 2, 2) + rest.shape[1:])
        own = (here & bit) // bit
        keep = lax.dynamic_index_in_dim(pairs, own, 1, keepdims=False)
        send = lax.dynamic_index_in_dim(pairs, 1 - own, 1, keepdims=False)
        rest = keep + swap(send, axis, bit)
        bit *= 2
    return rest[0]


def halves(value):
    high = value.astype(low)
    return high, (value - high.astype(jnp.float32)).astype(low)


def product(left, right, right_dim=0):
    joined_left = jnp.concatenate([left[0], left[0], left[1]], axis=1)
    joined_right = jnp.concatenate([right[0], right[1], right[0]], axis=right_dim)
    dims = (((1,), (right_dim,)), ((), ()))
    return lax.dot_general(joined_left, joined_right, dims, preferred_element_type=jnp.float32)


def thirds(value):
    high, rest = value.astype(low), value
    rest = value - high.astype(jnp.float32)
    middle = rest.astype(low)
    return high, middle, (rest - middle.astype(jnp.float32)).astype(low)


def spread(parts, chosen):
    return jnp.dot(
        jnp.concatenate(parts, axis=1), jnp.concatenate([chosen] * len(parts), axis=0), preferred_element_type=jnp.float32
    )


def exact_dot(left, right):
    return jnp.dot(left, right, precision=highest, preferred_element_type=jnp.float32)


def softplus(value):
    small = jnp.exp(-jnp.abs(value))
    ratio = small / (2.0 + small)
    square = ratio * ratio
    series = jnp.full_like(square, 1.0 / 17.0)
    for power in (15, 13, 11, 9, 7, 5, 3, 1):
        series = series * square + 1.0 / power
    return jnp.maximum(value, 0.0) + 2.0 * ratio * series


def lane_of_head(pair, base, transposed=False):
    shape = (LANES, LANES)
    head = lax.broadcasted_iota(jnp.int32, shape, 1 if transposed else 0)
    lane = lax.broadcasted_iota(jnp.int32, shape, 0 if transposed else 1)
    return jnp.where(head == base + 2 * pair + lane // HDIM, 1.0, 0.0).astype(low)


def own_lanes(parts, side):
    lane = lax.broadcasted_iota(jnp.int32, parts[0].shape, 1)
    return tuple(jnp.where(lane // HDIM == side, p, jnp.zeros_like(p)) for p in parts)


def decays(column, row, after_row):
    mid = column.shape[0] // 2
    shape = (mid, mid)
    down = lax.broadcasted_iota(jnp.int32, shape, 0)
    across = lax.broadcasted_iota(jnp.int32, shape, 1)
    keep = (down <= across) if after_row else (down >= across)

    def block(rows, cols, masked):
        gap = column[rows] - row[:, cols]
        gap = -gap if after_row else gap
        return jnp.exp(jnp.where(keep, gap, -1e30)) if masked else jnp.exp(gap)

    early, late = slice(0, mid), slice(mid, 2 * mid)
    side = block(early, late, False) if after_row else block(late, early, False)
    return block(early, early, True), side, block(late, late, True)


def taps_of(extended, size, kernel, offset):
    total = offset + kernel[0:1] * extended[pl.ds(8 - CONVW + 1, size), :]
    for index in range(1, CONVW):
        total = total + kernel[index : index + 1] * extended[pl.ds(8 - CONVW + 1 + index, size), :]
    return total


def step_sizes(raw, heads):
    delta = softplus(raw + heads[0:1])
    change = -delta * jnp.exp(heads[1:2])
    size = raw.shape[0]
    below = lax.broadcasted_iota(jnp.int32, (size, size), 0) >= lax.broadcasted_iota(jnp.int32, (size, size), 1)
    return delta, change, exact_dot(below.astype(jnp.float32), change)


def forward_kernel(
    table_ref, z_ref, x_ref, shared_ref, step_ref, chan_ref, shared_chan_ref, head_ref,
    gated_ref, mixed_ref, state_ref, square_ref,
    tails, shared_tail, states,
    extended, shared_extended, meet, read_high, read_low, keys_high, keys_low,
    delta_all, run_all, run_rows,
):
    chunk, pair = pl.program_id(0), pl.program_id(1)
    size = x_ref.shape[0]
    base = table_ref[pl.num_programs(0)]

    @pl.when(pair == 0)
    def _():
        @pl.when(chunk == 0)
        def _():
            shared_tail[...] = jnp.zeros_like(shared_tail)
            tails[...] = jnp.zeros_like(tails)
            states[...] = jnp.zeros_like(states)

        shared_extended[0:8, :] = shared_tail[...]
        shared_extended[8:, :] = shared_ref[...]
        shared_tail[...] = shared_ref[size - 8 :, :]
        pre = taps_of(shared_extended, size, shared_chan_ref[...], shared_chan_ref[4:5, :])
        active = pre * jax.nn.sigmoid(pre)
        keys, read = halves(active[:, :NST]), halves(active[:, NST:])
        meet[...] = product(read, keys, 1)
        read_high[...], read_low[...] = read
        keys_high[...], keys_low[...] = halves(active[:, :NST].T)
        delta, _, running = step_sizes(step_ref[...], head_ref[...])
        for k, (d, r) in enumerate(zip(thirds(delta), thirds(running))):
            delta_all[k] = d
            run_all[k] = r
        run_rows[...] = running.T
        square_ref[...] = jnp.zeros_like(square_ref)

    chan = chan_ref[...]
    extended[0:8, :] = tails[pair]
    extended[8:, :] = x_ref[...]
    tails[pair] = x_ref[size - 8 :, :]
    pre = taps_of(extended, size, chan, chan[4:5])
    values = pre * jax.nn.sigmoid(pre)
    lanes = lane_of_head(pair, base)
    delta = spread([delta_all[k] for k in range(3)], lanes)
    running = spread([run_all[k] for k in range(3)], lanes)
    stepped = delta * values
    stepped_halves = halves(stepped)
    mid = size // 2
    top, bottom, sources = [], [], []
    for side in range(2):
        column = running[:, side * HDIM : side * HDIM + 1]
        row = run_rows[pl.ds(base + 2 * pair + side, 1), :]
        first, below, second = decays(column, row, False)
        top.append(halves(first * meet[:mid, :mid]))
        bottom.append(
            (halves(below * meet[mid:, :mid]), halves(second * meet[mid:, mid:]))
        )
        sources.append(own_lanes(stepped_halves, side))
    joined = lambda parts, axis: tuple(jnp.concatenate(p, axis=axis) for p in zip(*parts))
    upper = product(joined(top, 1), joined([tuple(p[:mid] for p in x) for x in sources], 0))
    lower = product(joined([joined(b, 1) for b in bottom], 1), joined(sources, 0))
    local = jnp.concatenate([upper, lower], axis=0)
    state = states[pair]
    state_ref[0, 0] = state
    carried = product((read_high[...], read_low[...]), halves(state))
    scanned = local + jnp.exp(running) * carried
    last = running[size - 1 :, :]
    tail = halves(stepped * jnp.exp(last - running))
    states[pair] = jnp.exp(last) * state + product((keys_high[...], keys_low[...]), tail)
    mixed = scanned + chan[5:6] * values
    z = z_ref[...]
    gated = mixed * (z * jax.nn.sigmoid(z))
    mixed_ref[...] = mixed
    gated_ref[...] = gated
    square_ref[...] += gated * gated


def gate_kernel(
    z_ref, gated_ref, mixed_ref, up_ref, chan_ref, stats_ref,
    z_grad_ref, mix_grad_ref, square_ref, gain_grad_ref,
):
    @pl.when(pl.program_id(0) == 0)
    def _():
        gain_grad_ref[...] = jnp.zeros_like(gain_grad_ref)

    stats = stats_ref[...].T
    scale, pull = stats[:, 0:1], stats[:, 1:2]
    z, gated = z_ref[...], gated_ref[...]
    scaled = up_ref[...] * scale
    z_gain = jax.nn.sigmoid(z)
    gated_grad = scaled * chan_ref[6:7, :] - gated * pull
    z_gate = gated_grad * z_gain
    mix_grad_ref[...] = z_gate * z
    z_grad = (z_gate * mixed_ref[...] * (1.0 + z * (1.0 - z_gain))).astype(z_grad_ref.dtype)
    z_grad_ref[...] = z_grad
    wide_grad = z_grad.astype(jnp.float32)
    square_ref[...] = jnp.sum(wide_grad * wide_grad, axis=1, keepdims=True)
    gain_grad_ref[0:1, :] += jnp.sum(scaled * gated, axis=0, keepdims=True)


def backward_kernel(
    start, chunks, table_ref, x_ref, x_before_ref, shared_ref, shared_before_ref, step_ref, chan_ref, shared_chan_ref, head_ref,
    mixed_ref, mix_grad_ref, state_ref, state_after_ref, carried_in, *refs
):
    carried_in = (carried_in,) + refs[:5]
    (
        x_grad_ref, square_ref, shared_grad_ref,
        state_grads, heads_after, shared_after, chan_grad_ref, shared_chan_grad_ref, head_grad_ref,
        extended, shared_extended, later, shared_later, shared_pre,
        meet, read_high, read_low, keys_high, keys_low, read_rows_high, read_rows_low,
        delta_all, change_all, run_all, run_rows, meet_grad, keys_grad, read_grad, run_grad, delta_grad, last_grad,
    ) = refs[-31:]
    carried_out = (state_grads, heads_after, shared_after, chan_grad_ref, shared_chan_grad_ref, head_grad_ref)
    turn, pair, pairs = pl.program_id(0), pl.program_id(1), pl.num_programs(1)
    first = turn == start
    size = x_ref.shape[0]
    base = table_ref[chunks]

    @pl.when(pair == 0)
    def _():
        @pl.when(turn == 0)
        def _():
            for new, old in zip(carried_out, carried_in):
                new[...] = old[...]

        shared_extended[0:8, :] = jnp.where(first, 0.0, shared_before_ref[...])
        shared_extended[8:, :] = shared_ref[...]
        pre = taps_of(shared_extended, size, shared_chan_ref[...], shared_chan_ref[4:5, :])
        shared_pre[...] = pre
        active = pre * jax.nn.sigmoid(pre)
        keys, read = halves(active[:, :NST]), halves(active[:, NST:])
        meet[...] = product(keys, read, 1)
        read_high[...], read_low[...] = read
        keys_high[...], keys_low[...] = keys
        read_rows_high[...], read_rows_low[...] = halves(active[:, NST:].T)
        delta, change, running = step_sizes(step_ref[...], head_ref[...])
        for k, (d, r) in enumerate(zip(thirds(delta), thirds(running))):
            delta_all[k] = d
            run_all[k] = r
        change_all[...] = change
        run_rows[...] = running.T
        meet_grad[...] = jnp.zeros_like(meet_grad)
        keys_grad[...] = jnp.zeros_like(keys_grad)
        read_grad[...] = jnp.zeros_like(read_grad)
        run_grad[...] = jnp.zeros_like(run_grad)
        delta_grad[...] = jnp.zeros_like(delta_grad)
        last_grad[...] = jnp.zeros_like(last_grad)
        square_ref[...] = jnp.zeros_like(square_ref)

    chan = chan_ref[...]
    extended[0:8, :] = jnp.where(first, 0.0, x_before_ref[...])
    extended[8:, :] = x_ref[...]
    pre = taps_of(extended, size, chan, chan[4:5])
    gain = jax.nn.sigmoid(pre)
    values = pre * gain
    lanes = lane_of_head(pair, base)
    delta = spread([delta_all[k] for k in range(3)], lanes)
    running = spread([run_all[k] for k in range(3)], lanes)
    stepped = delta * values

    mixed, mix_grad = mixed_ref[...], mix_grad_ref[...]
    last = running[size - 1 :, :]
    fall = jnp.exp(last - running)
    rise = jnp.exp(running)
    state, state_grad = state_ref[0, 0], state_grads[pair]
    state_halves, state_grad_halves = halves(state), halves(state_grad)
    keys = (keys_high[...], keys_low[...])
    stepped_grad = fall * product(keys, state_grad_halves)
    keys_grad[...] += product(halves(stepped * fall), state_grad_halves, 1)
    risen = halves(mix_grad * rise)
    read_grad[...] += product(risen, state_halves, 1)
    ended = jnp.sum(state_grad * state_after_ref[0, 0], axis=0, keepdims=True)
    state_grads[pair] = jnp.exp(last) * state_grad + product((read_rows_high[...], read_rows_low[...]), risen)

    mid = size // 2
    grad_halves, stepped_halves = halves(mix_grad), halves(stepped)
    early, late = slice(0, mid), slice(mid, size)
    joined = lambda parts, axis: tuple(jnp.concatenate(p, axis=axis) for p in zip(*parts))
    top, bottom, sources = [], [], []
    first_grad = side_grad = second_grad = 0.0
    for side in range(2):
        column = running[:, side * HDIM : side * HDIM + 1]
        row = run_rows[pl.ds(base + 2 * pair + side, 1), :]
        first, beside, second = decays(column, row, True)
        top.append((halves(first * meet[early, early]), halves(beside * meet[early, late])))
        bottom.append(halves(second * meet[late, late]))
        sources.append(own_lanes(grad_halves, side))
        mine = own_lanes(stepped_halves, side)
        wide_grad = product(tuple(p[early] for p in mine), grad_halves, 1)
        first_grad += first * wide_grad[:, early]
        side_grad += beside * wide_grad[:, late]
        second_grad += second * product(tuple(p[late] for p in mine), tuple(p[late] for p in grad_halves), 1)
    meet_grad[early, early] += first_grad
    meet_grad[early, late] += side_grad
    meet_grad[late, late] += second_grad
    upper = product(joined([joined(t, 1) for t in top], 1), joined(sources, 0))
    lower = product(joined(bottom, 1), joined([tuple(p[late] for p in x) for x in sources], 0))
    stepped_grad = stepped_grad + jnp.concatenate([upper, lower], axis=0)
    to_head = lane_of_head(pair, base, transposed=True)
    scanned = mixed - chan[5:6] * values
    run_grad[...] += spread(halves(mix_grad * scanned - stepped * stepped_grad), to_head)
    delta_grad[...] += spread(halves(values * stepped_grad), to_head)
    last_grad[...] += spread(thirds(jnp.broadcast_to(ended, (8, LANES))), to_head)

    values_grad = chan[5:6] * mix_grad + delta * stepped_grad
    pre_grad = values_grad * (gain * (1.0 + pre * (1.0 - gain)))
    later[0:size, :] = pre_grad
    later[size:, :] = heads_after[pair]
    heads_after[pair] = pre_grad[0:8]
    x_grad = chan[0:1] * later[pl.ds(CONVW - 1, size), :]
    for index in range(1, CONVW):
        x_grad = x_grad + chan[index : index + 1] * later[pl.ds(CONVW - 1 - index, size), :]
    x_grad = x_grad.astype(x_grad_ref.dtype)
    x_grad_ref[:, pl.ds(pl.multiple_of(pair * LANES, LANES), LANES)] = x_grad
    wide_grad = x_grad.astype(jnp.float32)
    square_ref[...] += wide_grad * wide_grad
    for index in range(CONVW):
        seen = extended[pl.ds(8 - CONVW + 1 + index, size), :]
        chan_grad_ref[pair, index : index + 1, :] += jnp.sum(pre_grad * seen, axis=0, keepdims=True)
    chan_grad_ref[pair, 4:5, :] += jnp.sum(pre_grad, axis=0, keepdims=True)
    chan_grad_ref[pair, 5:6, :] += jnp.sum(mix_grad * values, axis=0, keepdims=True)

    @pl.when(pair == pairs - 1)
    def _():
        meet_halves = halves(meet_grad[...])
        keys_all = keys_grad[...] + product(meet_halves, (read_high[...], read_low[...]))
        read_all = read_grad[...] + product(halves(meet_grad[...].T), (keys_high[...], keys_low[...]))
        pre_s = shared_pre[...]
        gain_s = jax.nn.sigmoid(pre_s)
        chan_s = shared_chan_ref[...]
        grad_s = jnp.concatenate([keys_all, read_all], axis=1) * (gain_s * (1.0 + pre_s * (1.0 - gain_s)))
        shared_later[0:size, :] = grad_s
        shared_later[size:, :] = shared_after[...]
        shared_after[...] = grad_s[0:8]
        out = chan_s[0:1] * shared_later[pl.ds(CONVW - 1, size), :]
        for index in range(1, CONVW):
            out = out + chan_s[index : index + 1] * shared_later[pl.ds(CONVW - 1 - index, size), :]
        shared_grad_ref[...] = out
        for index in range(CONVW):
            seen = shared_extended[pl.ds(8 - CONVW + 1 + index, size), :]
            shared_chan_grad_ref[index : index + 1, :] += jnp.sum(grad_s * seen, axis=0, keepdims=True)
        shared_chan_grad_ref[4:5, :] += jnp.sum(grad_s, axis=0, keepdims=True)

        above = lax.broadcasted_iota(jnp.int32, (size, size), 0) <= lax.broadcasted_iota(jnp.int32, (size, size), 1)
        change_grad = exact_dot(above.astype(jnp.float32), run_grad[...]) + last_grad[0:1, :]
        rate = jnp.exp(head_ref[1:2, :])
        raw = step_ref[...] + head_ref[0:1, :]
        raw_grad = (delta_grad[...] - change_grad * rate) * jax.nn.sigmoid(raw)
        raw_low = raw_grad.astype(x_grad_ref.dtype)
        x_grad_ref[:, x_grad_ref.shape[1] - LANES :] = raw_low
        wide_raw = raw_low.astype(jnp.float32)
        square_ref[...] += wide_raw * wide_raw
        head_grad_ref[0:1, :] += jnp.sum(raw_grad, axis=0, keepdims=True)
        head_grad_ref[1:2, :] += jnp.sum(change_grad * change_all[...], axis=0, keepdims=True)


def run_forward(table, projected, chan, shared_chan, head_rows):
    length, wide = projected.shape[0], chan.shape[1]
    chunks, pairs = length // SPAN, wide // LANES
    f32 = jnp.float32
    block = pl.BlockSpec((SPAN, LANES), lambda c, p, t: (t[c], p))
    return pl.pallas_call(
        forward_kernel,
        grid_spec=pltpu.PrefetchScalarGridSpec(
            num_scalar_prefetch=1,
            grid=(chunks, pairs),
            in_specs=[
                block,
                pl.BlockSpec((SPAN, LANES), lambda c, p, t: (t[c], pairs + 2 + p)),
                pl.BlockSpec((SPAN, 2 * NST), lambda c, p, t: (t[c], pairs // 2)),
                pl.BlockSpec((SPAN, LANES), lambda c, p, t: (t[c], 2 * pairs + 2)),
                pl.BlockSpec((8, LANES), lambda c, p, t: (0, p)),
                pl.BlockSpec((8, 2 * NST), lambda c, p, t: (0, 0)),
                pl.BlockSpec((8, LANES), lambda c, p, t: (0, 0)),
            ],
            out_specs=[
                block,
                block,
                pl.BlockSpec((1, 1, NST, LANES), lambda c, p, t: (c, p, 0, 0)),
                pl.BlockSpec((SPAN, LANES), lambda c, p, t: (t[c], 0)),
            ],
            scratch_shapes=[
                pltpu.VMEM((pairs, 8, LANES), f32),
                pltpu.VMEM((8, 2 * NST), f32),
                pltpu.VMEM((pairs, NST, LANES), f32),
                pltpu.VMEM((SPAN + 8, LANES), f32),
                pltpu.VMEM((SPAN + 8, 2 * NST), f32),
                pltpu.VMEM((SPAN, SPAN), f32),
                pltpu.VMEM((SPAN, NST), low),
                pltpu.VMEM((SPAN, NST), low),
                pltpu.VMEM((NST, SPAN), low),
                pltpu.VMEM((NST, SPAN), low),
                pltpu.VMEM((3, SPAN, LANES), low),
                pltpu.VMEM((3, SPAN, LANES), low),
                pltpu.VMEM((LANES, SPAN), f32),
            ],
        ),
        out_shape=[
            jax.ShapeDtypeStruct((length, wide), f32),
            jax.ShapeDtypeStruct((length, wide), f32),
            jax.ShapeDtypeStruct((chunks, pairs, NST, LANES), f32),
            jax.ShapeDtypeStruct((length, LANES), f32),
        ],
        name="mixer_forward",
    )(table, projected, projected, projected, projected, chan, shared_chan, head_rows)


def run_gate(projected, gated, mixed, up, chan, stats):
    length, wide = gated.shape
    f32 = jnp.float32
    size = SPAN
    block = pl.BlockSpec((size, wide), lambda c: (c, 0))
    whole = pl.BlockSpec((8, wide), lambda c: (0, 0))
    return pl.pallas_call(
        gate_kernel,
        grid=(length // size,),
        in_specs=[block, block, block, block, whole, pl.BlockSpec((8, size), lambda c: (0, c))],
        out_specs=[block, block, pl.BlockSpec((size, 1), lambda c: (c, 0)), whole],
        out_shape=[
            jax.ShapeDtypeStruct((length, wide), low),
            jax.ShapeDtypeStruct((length, wide), f32),
            jax.ShapeDtypeStruct((length, 1), f32),
            jax.ShapeDtypeStruct((8, wide), f32),
        ],
        name="gate_backward",
    )(projected, gated, mixed, up, chan, stats)


def run_backward(start, count, table, projected, chan, shared_chan, head_rows, mixed, mix_grad, states, carried, before):
    length, wide = projected.shape[0], chan.shape[1]
    chunks, pairs = length // SPAN, wide // LANES
    f32 = jnp.float32
    lines = SPAN // 8
    earlier = lambda c: jnp.maximum(start - c - 1, 0)
    following = lambda c: jnp.minimum(start - c + 1, chunks - 1)
    block = pl.BlockSpec((SPAN, LANES), lambda c, p, t: (t[start - c], p))
    flat = pl.BlockSpec((8, 2 * NST), lambda c, p, t: (0, 0))
    head = pl.BlockSpec((8, LANES), lambda c, p, t: (0, 0))
    carries = [
        pl.BlockSpec((pairs, NST, LANES), lambda c, p, t: (0, 0, 0)),
        pl.BlockSpec((pairs, 8, LANES), lambda c, p, t: (0, 0, 0)),
        flat,
        pl.BlockSpec((pairs, 8, LANES), lambda c, p, t: (0, 0, 0)),
        flat,
        head,
    ]
    carried_shapes = [jax.ShapeDtypeStruct(c.shape, f32) for c in carried]
    return pl.pallas_call(
        functools.partial(backward_kernel, start, chunks),
        grid_spec=pltpu.PrefetchScalarGridSpec(
            num_scalar_prefetch=1,
            grid=(count, pairs),
            in_specs=[
                pl.BlockSpec((SPAN, LANES), lambda c, p, t: (t[start - c], pairs + 2 + p)),
                pl.BlockSpec((8, LANES), lambda c, p, t: (t[earlier(c)] * lines + lines - 1, pairs + 2 + p)),
                pl.BlockSpec((SPAN, 2 * NST), lambda c, p, t: (t[start - c], pairs // 2)),
                pl.BlockSpec((8, 2 * NST), lambda c, p, t: (t[earlier(c)] * lines + lines - 1, pairs // 2)),
                pl.BlockSpec((SPAN, LANES), lambda c, p, t: (t[start - c], 2 * pairs + 2)),
                pl.BlockSpec((8, LANES), lambda c, p, t: (0, p)),
                flat,
                head,
                block,
                block,
                pl.BlockSpec((1, 1, NST, LANES), lambda c, p, t: (start - c, p, 0, 0)),
                pl.BlockSpec((1, 1, NST, LANES), lambda c, p, t: (following(c), p, 0, 0)),
            ]
            + carries
            + [pl.BlockSpec(memory_space=pl.ANY)] * len(before),
            out_specs=[
                pl.BlockSpec((SPAN, wide + LANES), lambda c, p, t: (t[start - c], 0)),
                pl.BlockSpec((SPAN, LANES), lambda c, p, t: (t[start - c], 0)),
                pl.BlockSpec((SPAN, 2 * NST), lambda c, p, t: (t[start - c], 0)),
            ]
            + carries,
            scratch_shapes=[
                pltpu.VMEM((SPAN + 8, LANES), f32),
                pltpu.VMEM((SPAN + 8, 2 * NST), f32),
                pltpu.VMEM((SPAN + 8, LANES), f32),
                pltpu.VMEM((SPAN + 8, 2 * NST), f32),
                pltpu.VMEM((SPAN, 2 * NST), f32),
                pltpu.VMEM((SPAN, SPAN), f32),
                pltpu.VMEM((SPAN, NST), low),
                pltpu.VMEM((SPAN, NST), low),
                pltpu.VMEM((SPAN, NST), low),
                pltpu.VMEM((SPAN, NST), low),
                pltpu.VMEM((NST, SPAN), low),
                pltpu.VMEM((NST, SPAN), low),
                pltpu.VMEM((3, SPAN, LANES), low),
                pltpu.VMEM((SPAN, LANES), f32),
                pltpu.VMEM((3, SPAN, LANES), low),
                pltpu.VMEM((LANES, SPAN), f32),
                pltpu.VMEM((SPAN, SPAN), f32),
                pltpu.VMEM((SPAN, NST), f32),
                pltpu.VMEM((SPAN, NST), f32),
                pltpu.VMEM((SPAN, LANES), f32),
                pltpu.VMEM((SPAN, LANES), f32),
                pltpu.VMEM((8, LANES), f32),
            ],
        ),
        out_shape=[
            jax.ShapeDtypeStruct((length, wide + LANES), low),
            jax.ShapeDtypeStruct((length, LANES), f32),
            jax.ShapeDtypeStruct((length, 2 * NST), f32),
        ]
        + carried_shapes,
        input_output_aliases={19 + k: k for k in range(len(before))},
        name="mixer_backward",
    )(
        table, projected, projected, projected, projected, projected, chan, shared_chan, head_rows,
        mixed, mix_grad, states, states, *carried, *before,
    )


def halve(block, left, bit, axis):
    place = left.index(bit)
    own = (lax.axis_index(axis) & bit) // bit
    keep = lax.dynamic_index_in_dim(block, own, place, keepdims=False)
    send = lax.dynamic_index_in_dim(block, 1 - own, place, keepdims=False)
    return keep + swap(send, axis, bit), [b for b in left if b != bit]


class Scatter:
    def __init__(self, arrays, axis, phase=0):
        self.axis = axis
        size = lax.axis_size(axis)
        bits = [1 << k for k in range(size.bit_length() - 1)]
        upper = bits[1:]
        turned = upper[len(upper) // 2 :] + upper[: len(upper) // 2]
        self.orders = [bits[:1] + (upper if (k + phase) % 2 == 0 else turned) for k in range(len(arrays))]
        self.left = [bits[::-1] for _ in arrays]
        self.blocks = [
            a.reshape((2,) * len(bits) + (a.shape[0] // size,) + a.shape[1:]) for a in arrays
        ]
        self.steps = len(bits)
        self.done = 0

    def step(self):
        for k in range(len(self.blocks)):
            self.blocks[k], self.left[k] = halve(
                self.blocks[k], self.left[k], self.orders[k][self.done], self.axis
            )
        self.done += 1

    def finish(self):
        while self.done < self.steps:
            self.step()
        return self.blocks


def update_kernel(
    pieces, widths, rate, decay, slot_ref, source_ref, param_ref, first_ref, second_ref,
    grad_ref, param_out, first_out, second_out,
):
    for piece, width in zip(range(pieces), widths):
        at = sum(widths[:piece])
        own = slice(at, at + width)
        grad = source_ref[slot_ref[piece], :, :width]
        new = adamw_update(param_ref[:, own], grad, first_ref[:, own], second_ref[:, own], rate, decay)
        grad_ref[:, own] = grad
        param_out[:, own], first_out[:, own], second_out[:, own] = new


def run_update(slots, sources, widths, param, first, second, rate, decay):
    rows, total = param.shape
    size = 16 if rows % 16 == 0 else rows
    block = pl.BlockSpec((size, total), lambda r, t: (r, 0))
    return pl.pallas_call(
        functools.partial(update_kernel, len(widths), widths, rate, decay),
        grid_spec=pltpu.PrefetchScalarGridSpec(
            num_scalar_prefetch=1,
            grid=(rows // size,),
            in_specs=[pl.BlockSpec((sources.shape[0], size, sources.shape[2]), lambda r, t: (0, r, 0))] + [block] * 3,
            out_specs=[block] * 4,
        ),
        out_shape=[jax.ShapeDtypeStruct(param.shape, jnp.float32)] * 4,
        name="weight_update",
    )(slots, sources, param, first, second)


def adamw_update(param, grad, first, second, rate, decay):
    first_new = beta_one * first + (1.0 - beta_one) * grad
    second_new = beta_two * second + (1.0 - beta_two) * grad * grad
    corrected_first = first_new / (1.0 - beta_one**adam_step)
    corrected_second = second_new / (1.0 - beta_two**adam_step)
    param_new = param - rate * (
        corrected_first / (jnp.sqrt(corrected_second) + adam_eps) + decay * param
    )
    return (param_new, first_new, second_new)


def dot(left, right):
    return jnp.dot(left, right, preferred_element_type=jnp.float32)


def body(
    block_input,
    cotangent,
    norm_gain,
    in_weight,
    conv_weight,
    conv_bias,
    step_bias,
    decay_log,
    skip_gain,
    gated_gain,
    out_weight,
    first_norm_gain,
    second_norm_gain,
    first_in_weight,
    second_in_weight,
    first_conv_weight,
    second_conv_weight,
    first_conv_bias,
    second_conv_bias,
    first_step_bias,
    second_step_bias,
    first_decay_log,
    second_decay_log,
    first_skip_gain,
    second_skip_gain,
    first_gated_gain,
    second_gated_gain,
    first_out_weight,
    second_out_weight,
):
    ranks, rank = lax.axis_size("seq"), lax.axis_index("seq")
    groups = lax.axis_size("dp")
    devices = ranks * groups
    wide, heads = E // ranks, NHEADS // ranks
    rows = in_weight.shape[0]
    width = rows * devices
    taps = conv_bias.shape[0]
    channels = taps * devices
    step_at = 2 * E + 2 * NST
    spare = LANES - (in_weight.shape[1] - step_at)

    packed = jnp.concatenate(
        [norm_gain, conv_weight.reshape(-1), conv_bias, gated_gain]
    ).astype(low).astype(jnp.float32)
    gains = gated_gain.shape[0]
    filled = packed.shape[0]
    lines = -(-filled // LANES)
    packed = jnp.pad(packed, (0, lines * LANES - filled)).reshape(lines, LANES)
    small_line = gather_direct(packed, "seq")
    small = gather_bits(small_line, "dp")
    small = small.reshape(devices, lines * LANES)
    norm_float = small[:, :rows].reshape(-1)
    kernel_float = small[:, rows : rows + CONVW * taps].reshape(devices, CONVW, taps)
    kernel_float = kernel_float.transpose(1, 0, 2).reshape(CONVW, channels)
    offset_float = small[:, rows + CONVW * taps : rows + (CONVW + 1) * taps].reshape(-1)
    gated_float = small[:, rows + (CONVW + 1) * taps : filled].reshape(-1)
    kernel_own = lax.dynamic_slice_in_dim(kernel_float, rank * wide, wide, 1)
    offset_own = lax.dynamic_slice_in_dim(offset_float, rank * wide, wide, 0)
    gated_own = lax.dynamic_slice_in_dim(gated_float, rank * wide, wide, 0)
    skip_own = lax.dynamic_slice_in_dim(skip_gain, rank * heads, heads, 0)

    in_low = in_weight.astype(low)
    out_low = out_weight.astype(low)

    def for_rank(j):
        return jnp.concatenate(
            [
                lax.dynamic_slice_in_dim(in_low, j * wide, wide, 1),
                in_low[:, 2 * E : step_at],
                lax.dynamic_slice_in_dim(in_low, E + j * wide, wide, 1),
                jnp.pad(in_low[:, step_at:], ((0, 0), (0, spare))),
                lax.dynamic_slice_in_dim(out_low, j * wide, wide, 1),
            ],
            axis=1,
        )

    columns = 2 * NST + 2 * wide + LANES
    weights_arrived = []
    for turn in range(1, ranks):
        weights_arrived.append(shift(for_rank((rank + turn) % ranks), "seq", turn))

    tokens, upstream = block_input[0], cotangent[0]
    span = tokens.shape[0]
    length = span * ranks
    inverse = lax.rsqrt(jnp.mean(tokens * tokens, axis=-1, keepdims=True) + norm_eps)
    hidden_own = (tokens * inverse * norm_float).astype(low)
    weights_arrived = [after(part, hidden_own) for part in weights_arrived]
    weight_rows = jnp.zeros((ranks, rows, columns + wide), low)
    weight_rows = lax.dynamic_update_index_in_dim(weight_rows, for_rank(rank), rank, 0)
    for turn in range(1, ranks):
        weight_rows = lax.dynamic_update_index_in_dim(
            weight_rows, weights_arrived[turn - 1], (rank + ranks - turn) % ranks, 0
        )
    weight_rows = weight_rows.reshape(ranks * rows, columns + wide)
    in_full, out_full = gather_rows([weight_rows[:, :columns], weight_rows[:, columns:]], "dp")

    line_parts = near_parts(hidden_own, "seq")
    line_parts = [after(part, in_full, out_full) for part in line_parts]
    up_parts = near_parts(after(upstream.astype(low), *line_parts), "seq")
    hidden = jnp.stack(line_parts).reshape(length, width)

    projected = dot(hidden, in_full)
    none = jnp.zeros((1, wide), jnp.float32)
    chan = jnp.concatenate(
        [kernel_own, offset_own[None], jnp.repeat(skip_own, HDIM)[None], gated_own[None], none], axis=0
    )
    shared_chan = jnp.concatenate(
        [kernel_float[:, E:], offset_float[None, E:], jnp.zeros((3, 2 * NST), jnp.float32)], axis=0
    )
    head_rows = jnp.pad(jnp.stack([step_bias, decay_log]), ((0, 6), (0, LANES - NHEADS)))
    pairs, chunks = wide // LANES, length // SPAN
    per_rank = span // SPAN
    order = jnp.arange(chunks, dtype=jnp.int32)
    order = (rank + ranks - order // per_rank) % ranks * per_rank + order % per_rank
    table = jnp.concatenate([order, jnp.reshape(rank * heads, (1,))]).astype(jnp.int32)
    zeros = functools.partial(jnp.zeros, dtype=jnp.float32)
    gated, mixed, states, squares = run_forward(table, projected, chan, shared_chan, head_rows)
    packed_length = (ranks, span // LANES, LANES)
    square_sum = sum_near(jnp.sum(squares, axis=1).reshape(packed_length), "seq").reshape(length)
    scale = lax.rsqrt(square_sum / E + norm_eps)
    normed_low = (gated * scale[:, None] * gated_own).astype(low)
    branch_factor = 2.0 ** (14 - math.ceil(math.log2(0.17 * math.sqrt(E * wide))))
    out_half = (dot(normed_low, out_full.T) * branch_factor).astype(half).reshape(ranks, span, width)

    upstream_low = jnp.stack([after(part, out_half) for part in up_parts]).reshape(length, width)
    normed_grad = dot(upstream_low, out_full)
    pull_sum = jnp.sum(normed_grad * gated_own * gated, axis=1).reshape(packed_length)
    pull_sum = sum_near(pull_sum, "seq").reshape(length)
    stats = jnp.stack([scale, scale * scale * scale * (pull_sum / E)])
    stats = jnp.pad(stats, ((0, 6), (0, 0)))
    out_grad_part = dot(upstream_low.T, normed_low)
    out_scatter = Scatter([out_grad_part], "dp")
    out_scatter.step()
    gate_low, mix_grad, gate_square, gain_rows = run_gate(projected, gated, mixed, normed_grad, chan, stats)
    gated_grad = gain_rows[0]

    branch_parts = send_near(out_half, "seq")

    gate_scatter = Scatter([dot(hidden.T, gate_low)], "dp", 1)
    gate_scatter.step()
    carried = (
        zeros((pairs, NST, LANES)), zeros((pairs, 8, LANES)), zeros((8, 2 * NST)),
        zeros((pairs, 8, LANES)), zeros((8, 2 * NST)), zeros((8, LANES)),
    )
    outputs, early = (), (out_scatter, gate_scatter)
    calls = [(chunks - 1, chunks - 2 * (chunks // 4)), (2 * (chunks // 4) - 1, chunks // 4), (chunks // 4 - 1, chunks // 4)]
    for turn, (start, count) in enumerate(calls):
        ready = tuple(scatter.blocks[0] for scatter in early)
        if turn < len(calls) - 1:
            for scatter in early:
                if scatter.done < scatter.steps:
                    scatter.step()
        else:
            early_sums = jnp.concatenate(
                [block.reshape(ranks, rows, wide) for scatter in early for block in scatter.finish()], axis=2
            )
            early_packed = pack_half(early_sums, jnp.max(jnp.abs(early_sums), axis=-1, keepdims=True))
            early_slots = slots_of(early_sums, early_packed, "seq")
            ready = (early_packed,)
        mix_grad = after(mix_grad, *ready)
        result = run_backward(
            start, count, table, projected, chan, shared_chan, head_rows, mixed, mix_grad, states, carried, outputs
        )
        outputs, carried = tuple(result[:3]), tuple(result[3:])
    conv_low, conv_square, shared_grad = outputs
    _, _, _, chan_grad, shared_chan_grad, head_grad = carried

    largest = jnp.max(gate_square.reshape(ranks, span) + jnp.sum(conv_square.reshape(ranks, span, LANES), axis=2), axis=1)
    bound = 0.1565 * math.sqrt(2 * wide + NHEADS) * jnp.sqrt(largest)
    power = jnp.clip(jnp.ceil(jnp.log2(bound)) - 14.0, -120.0, 120.0)
    shared_parts = shared_grad.reshape(ranks, span, 2 * NST)
    lines_of_power = jnp.broadcast_to(power[:, None, None], (ranks, 8, 2 * NST))
    shared_sent = send_near(jnp.concatenate([shared_parts, lines_of_power], axis=1), "seq")

    factors = jnp.exp2(-power)[:, None, None]
    hidden_part = dot(gate_low, in_full[:, :wide].T) + dot(conv_low, in_full[:, wide + 2 * NST :].T)
    hidden_part = hidden_part.reshape(ranks, span, width)
    hidden_half = (hidden_part * factors).astype(half)
    hidden_parts = send_near(hidden_half, "seq")

    split = 4 * LANES
    conv_parts = [dot(hidden.T, conv_low[:, :split]), dot(hidden.T, conv_low[:, split:])]
    late = Scatter(conv_parts, "dp")
    normed_own = normed_low[:span]
    for turn in range(late.steps):
        if turn == 1:
            normed_own = after(normed_own, *late.blocks)
            early_slots = [after(part, *late.blocks) for part in early_slots]
            chan_grad, shared_chan_grad, head_grad = (
                after(part, *late.blocks) for part in (chan_grad, shared_chan_grad, head_grad)
            )
        late.step()
    shared_own = shared_parts[0]
    for part in shared_sent:
        shared_own = shared_own + part[:span]
    shared_own = shared_own.astype(low)
    shared_grad_part = dot(hidden_own.T, shared_own)
    last = Scatter([shared_grad_part], "dp", 1)
    for turn in range(last.steps):
        if turn == last.steps - 1:
            hidden_parts = [after(part, *last.blocks) for part in hidden_parts]
            power_parts = [after(part, *last.blocks)[span, 0] for part in shared_sent]
        last.step()
    hidden_grad = hidden_part[0] + dot(shared_own, in_full[:, wide : wide + 2 * NST].T)
    branch = tokens + dot(normed_own, out_full.T)
    for part in branch_parts:
        branch = branch + part.astype(jnp.float32) * (1.0 / branch_factor)
    block_output = branch[None]

    chan_grad = chan_grad.transpose(1, 0, 2).reshape(8, wide)
    kernel_grad, offset_grad = chan_grad[:CONVW], chan_grad[4]
    skip_grad = jnp.sum(chan_grad[5].reshape(heads, HDIM), axis=1)
    kernel_shared_grad, offset_shared_grad = shared_chan_grad[:CONVW], shared_chan_grad[4]

    late_sums = jnp.concatenate([block.reshape(ranks, rows, -1) for block in late.blocks + last.blocks], axis=2)
    late_packed = pack_half(late_sums, jnp.max(jnp.abs(late_sums), axis=-1, keepdims=True))
    late_slots = slots_of(late_sums, late_packed, "seq")

    for part, exponent in zip(hidden_parts, power_parts):
        hidden_grad = hidden_grad + part.astype(jnp.float32) * jnp.exp2(exponent)
    scaled = tokens * inverse
    gain_grad = jnp.sum(hidden_grad * scaled, axis=0)
    inner = hidden_grad * norm_float
    token_grad = inverse * (inner - scaled * jnp.mean(inner * scaled, axis=-1, keepdims=True))
    input_grad = (upstream + token_grad)[None]

    def placed(own, shared):
        full = jnp.zeros(own.shape[:-1] + (E,), jnp.float32)
        full = lax.dynamic_update_slice_in_dim(full, own, rank * wide, own.ndim - 1)
        return jnp.concatenate([full, shared], axis=-1)

    kernel_all = placed(kernel_grad, kernel_shared_grad).reshape(CONVW, devices, taps)
    kernel_all = kernel_all.transpose(1, 0, 2).reshape(devices, CONVW * taps)
    offset_all = placed(offset_grad, offset_shared_grad).reshape(devices, taps)
    gated_all = lax.dynamic_update_slice_in_dim(jnp.zeros((E,), jnp.float32), gated_grad, rank * wide, 0)
    skip_all = lax.dynamic_update_slice_in_dim(jnp.zeros((NHEADS,), jnp.float32), skip_grad, rank * heads, 0)
    head_all = jnp.concatenate([head_grad[0, :NHEADS], head_grad[1, :NHEADS], skip_all])
    terms = jnp.concatenate(
        [
            kernel_all,
            offset_all,
            gated_all.reshape(devices, gains),
            jnp.broadcast_to(head_all[None], (devices, 3 * NHEADS)),
        ],
        axis=1,
    )
    used = terms.shape[1]
    term_lines = -(-used // LANES)
    terms = jnp.pad(terms, ((0, 0), (0, term_lines * LANES - used)))
    terms = terms.reshape(groups, ranks, term_lines, LANES)
    norm_lines = -(-rows // LANES)
    norm_terms = jnp.pad(gain_grad.reshape(devices, rows), ((0, 0), (0, norm_lines * LANES - rows)))
    norm_terms = norm_terms.reshape(groups, ranks, norm_lines, LANES)
    term_lines += norm_lines
    terms = jnp.concatenate([norm_terms, terms], axis=2).reshape(groups, ranks * term_lines, LANES)
    summed = scatter_bits(terms, "dp").reshape(ranks, term_lines, LANES)
    summed = exchange_sum(summed, "seq").reshape(-1)
    grad_norm_gain = summed[:rows]
    at = norm_lines * LANES
    grad_conv_weight = summed[at : at + CONVW * taps].reshape(CONVW, taps)
    at += CONVW * taps
    grad_conv_bias = summed[at : at + taps]
    at += taps
    grad_gated_gain = summed[at : at + gains]
    at += gains
    grad_step_bias, grad_decay_log, grad_skip_gain = (
        summed[at + k * NHEADS : at + (k + 1) * NHEADS] for k in range(3)
    )
    new_norm_gain, new_first_norm_gain, new_second_norm_gain = adamw_update(
        norm_gain, grad_norm_gain, first_norm_gain, second_norm_gain, rate_vector, 0.0
    )
    place = (rank + ranks - jnp.arange(ranks, dtype=jnp.int32)) % ranks
    early_f32 = early_slots[:1] + list(unpack_half(jnp.stack(early_slots[1:])))
    late_f32 = late_slots[:1] + list(unpack_half(jnp.stack(late_slots[1:])))
    shared_sum = late_f32[0][:, wide:]
    for part in late_f32[1:]:
        shared_sum = shared_sum + part[:, wide:]
    shared_sum = jnp.concatenate([shared_sum[:, LANES:], shared_sum[:, :LANES]], axis=1)
    sources = jnp.stack(
        [part[:, wide:] for part in early_f32]
        + [part[:, :wide] for part in late_f32]
        + [jnp.pad(shared_sum, ((0, 0), (0, wide - shared_sum.shape[1])))]
    )
    slots = jnp.concatenate([place, place + ranks, jnp.full((1,), 2 * ranks)]).astype(jnp.int32)
    widths = (wide,) * (2 * ranks) + (in_weight.shape[1] - 2 * E,)
    grad_in_weight, new_in_weight, new_first_in_weight, new_second_in_weight = run_update(
        slots, sources, widths, in_weight, first_in_weight, second_in_weight, rate_matrix, weight_decay
    )
    new_conv_weight, new_first_conv_weight, new_second_conv_weight = adamw_update(
        conv_weight, grad_conv_weight, first_conv_weight, second_conv_weight, rate_vector, 0.0
    )
    new_conv_bias, new_first_conv_bias, new_second_conv_bias = adamw_update(
        conv_bias, grad_conv_bias, first_conv_bias, second_conv_bias, rate_vector, 0.0
    )
    new_step_bias, new_first_step_bias, new_second_step_bias = adamw_update(
        step_bias, grad_step_bias, first_step_bias, second_step_bias, rate_vector, 0.0
    )
    new_decay_log, new_first_decay_log, new_second_decay_log = adamw_update(
        decay_log, grad_decay_log, first_decay_log, second_decay_log, rate_vector, 0.0
    )
    new_skip_gain, new_first_skip_gain, new_second_skip_gain = adamw_update(
        skip_gain, grad_skip_gain, first_skip_gain, second_skip_gain, rate_vector, 0.0
    )
    new_gated_gain, new_first_gated_gain, new_second_gated_gain = adamw_update(
        gated_gain, grad_gated_gain, first_gated_gain, second_gated_gain, rate_vector, 0.0
    )
    grad_out_weight, new_out_weight, new_first_out_weight, new_second_out_weight = run_update(
        place,
        jnp.stack([part[:, :wide] for part in early_f32]),
        (wide,) * ranks,
        out_weight,
        first_out_weight,
        second_out_weight,
        rate_matrix,
        weight_decay,
    )

    return (
        block_output,
        input_grad,
        grad_norm_gain,
        grad_in_weight,
        grad_conv_weight,
        grad_conv_bias,
        grad_step_bias,
        grad_decay_log,
        grad_skip_gain,
        grad_gated_gain,
        grad_out_weight,
        new_norm_gain,
        new_first_norm_gain,
        new_second_norm_gain,
        new_in_weight,
        new_first_in_weight,
        new_second_in_weight,
        new_conv_weight,
        new_first_conv_weight,
        new_second_conv_weight,
        new_conv_bias,
        new_first_conv_bias,
        new_second_conv_bias,
        new_step_bias,
        new_first_step_bias,
        new_second_step_bias,
        new_decay_log,
        new_first_decay_log,
        new_second_decay_log,
        new_skip_gain,
        new_first_skip_gain,
        new_second_skip_gain,
        new_gated_gain,
        new_first_gated_gain,
        new_second_gated_gain,
        new_out_weight,
        new_first_out_weight,
        new_second_out_weight,
    )


def solution(mesh):
    in_specs = (
        P("dp", "seq", None),
        P("dp", "seq", None),
        P(("dp", "seq")),
        P(("dp", "seq"), None),
        P(None, ("dp", "seq")),
        P(("dp", "seq")),
        P(),
        P(),
        P(),
        P(("dp", "seq")),
        P(("dp", "seq"), None),
        P(("dp", "seq")),
        P(("dp", "seq")),
        P(("dp", "seq"), None),
        P(("dp", "seq"), None),
        P(None, ("dp", "seq")),
        P(None, ("dp", "seq")),
        P(("dp", "seq")),
        P(("dp", "seq")),
        P(),
        P(),
        P(),
        P(),
        P(),
        P(),
        P(("dp", "seq")),
        P(("dp", "seq")),
        P(("dp", "seq"), None),
        P(("dp", "seq"), None),
    )
    out_specs = (
        P("dp", "seq", None),
        P("dp", "seq", None),
        P(("dp", "seq")),
        P(("dp", "seq"), None),
        P(None, ("dp", "seq")),
        P(("dp", "seq")),
        P(),
        P(),
        P(),
        P(("dp", "seq")),
        P(("dp", "seq"), None),
        P(("dp", "seq")),
        P(("dp", "seq")),
        P(("dp", "seq")),
        P(("dp", "seq"), None),
        P(("dp", "seq"), None),
        P(("dp", "seq"), None),
        P(None, ("dp", "seq")),
        P(None, ("dp", "seq")),
        P(None, ("dp", "seq")),
        P(("dp", "seq")),
        P(("dp", "seq")),
        P(("dp", "seq")),
        P(),
        P(),
        P(),
        P(),
        P(),
        P(),
        P(),
        P(),
        P(),
        P(("dp", "seq")),
        P(("dp", "seq")),
        P(("dp", "seq")),
        P(("dp", "seq"), None),
        P(("dp", "seq"), None),
        P(("dp", "seq"), None),
    )

    return jax.shard_map(body, mesh=mesh, in_specs=in_specs, out_specs=out_specs, check_vma=False)
```

```python
import functools
import math

import jax
import jax.numpy as jnp
from jax import lax
from jax.experimental import pallas as pl
from jax.experimental.pallas import tpu as pltpu
from jax.sharding import PartitionSpec as P


E = 3072
NST = 128
NHEADS = 48
HDIM = 64
CONVW = 4
SPAN = 256
LANES = 128
MIB = 2**20
SEQ, DP = "seq", "dp"


low = jnp.bfloat16
half = jnp.float16
highest = lax.Precision.HIGHEST
beta_one = 0.9
beta_two = 0.95
adam_step = 10.0
adam_eps = 1e-08
rate_matrix = 0.01
rate_vector = 0.3
weight_decay = 0.1
norm_eps = 1e-05


def shift(block, axis, distance):
    size = lax.axis_size(axis)
    return lax.ppermute(block, axis, [(i, (i + distance) % size) for i in range(size)])


def step_to(block, axis, distance):
    size = lax.axis_size(axis)
    route = [(i, i + distance) for i in range(size) if 0 <= i + distance < size]
    return lax.ppermute(block, axis, route)


def swap(block, axis, bit):
    return lax.ppermute(block, axis, [(i, i ^ bit) for i in range(lax.axis_size(axis))])


def pick(stacked, index):
    return lax.dynamic_index_in_dim(stacked, index, 0, keepdims=False)


def exchange_sum(stacked, axis):
    size, here = lax.axis_size(axis), lax.axis_index(axis)
    arrived = [shift(pick(stacked, (here + turn) % size), axis, turn) for turn in range(1, size)]
    total = pick(stacked, here)
    for part in arrived:
        total = total + part
    return total


def after(value, *others):
    return lax.optimization_barrier((value,) + others)[0]


def pack_half(parts, bound):
    power = jnp.clip(jnp.ceil(jnp.log2(bound)) - 14.0, -120.0, 120.0)
    scaled = (parts * jnp.exp2(-power)).astype(half)
    return jnp.concatenate([scaled, jnp.broadcast_to(power.astype(half), parts.shape[:-1] + (LANES,))], axis=-1)


def unpack_half(message):
    width = message.shape[-1] - LANES
    return message[..., :width].astype(jnp.float32) * jnp.exp2(message[..., width : width + 1].astype(jnp.float32))


def near_parts(block, axis):
    size, here = lax.axis_size(axis), lax.axis_index(axis)
    if size != 4:
        return [block] + [shift(block, axis, turn) for turn in range(1, size)]
    below, above = step_to(block, axis, 1), step_to(block, axis, -1)
    across = shift(block, axis, 2)
    far = lax.ppermute(across, axis, [(2, 3), (1, 0)])
    return [block, jnp.where(here == 0, far, below), across, jnp.where(here == size - 1, far, above)]


def send_near(stacked, axis):
    return [shift(stacked[turn], axis, lax.axis_size(axis) - turn) for turn in range(1, lax.axis_size(axis))]


def slots_of(own_blocks, packed, axis):
    size, here = lax.axis_size(axis), lax.axis_index(axis)
    arrived = [shift(pick(packed, (here + turn) % size), axis, turn) for turn in range(1, size)]
    return [pick(own_blocks, here)] + arrived


def gather_direct(block, axis):
    size, here = lax.axis_size(axis), lax.axis_index(axis)
    arrived = [block] + [shift(block, axis, turn) for turn in range(1, size)]
    result = jnp.stack(arrived)
    return jnp.take(result, (here + size - jnp.arange(size)) % size, axis=0)


def sum_near(stacked, axis):
    total = stacked
    for turn in range(1, lax.axis_size(axis)):
        total = total + jnp.roll(shift(stacked, axis, turn), turn, axis=0)
    return total


def gather_bits(block, axis):
    here = lax.axis_index(axis)
    result, bit = block[None], 1
    while bit < lax.axis_size(axis):
        other = swap(result, axis, bit)
        upper = (here & bit) > 0
        result = jnp.concatenate(
            [jnp.where(upper, other, result), jnp.where(upper, result, other)], axis=0
        )
        bit *= 2
    return result


def gather_rows(blocks, axis):
    size, here = lax.axis_size(axis), lax.axis_index(axis)
    bits = [1 << k for k in range(size.bit_length() - 1)]
    upper = bits[1:]
    turned = upper[len(upper) // 2 :] + upper[: len(upper) // 2]
    parts, paths = [], []
    for block in blocks:
        rows = block.shape[0] // 2
        parts += [p.reshape((1,) * len(bits) + p.shape) for p in (block[:rows], block[rows:])]
        paths += [upper + bits[:1], turned + bits[:1]]
    for step in range(len(bits)):
        arrived = [swap(p, axis, path[step]) for p, path in zip(parts, paths)]
        for k, path in enumerate(paths):
            place = bits[::-1].index(path[step])
            up = (here & path[step]) > 0
            parts[k] = jnp.concatenate(
                [jnp.where(up, arrived[k], parts[k]), jnp.where(up, parts[k], arrived[k])], axis=place
            )
    return [
        jnp.concatenate(parts[2 * k : 2 * k + 2], axis=len(bits)).reshape(-1, block.shape[1])
        for k, block in enumerate(blocks)
    ]


def halves(value):
    high = value.astype(low)
    return high, (value - high.astype(jnp.float32)).astype(low)


def product(left, right, right_dim=0):
    joined_left = jnp.concatenate([left[0], left[0], left[1]], axis=1)
    joined_right = jnp.concatenate([right[0], right[1], right[0]], axis=right_dim)
    dims = (((1,), (right_dim,)), ((), ()))
    return lax.dot_general(joined_left, joined_right, dims, preferred_element_type=jnp.float32)


def thirds(value):
    high, rest = value.astype(low), value
    rest = value - high.astype(jnp.float32)
    middle = rest.astype(low)
    return high, middle, (rest - middle.astype(jnp.float32)).astype(low)


def spread(parts, chosen):
    return jnp.dot(
        jnp.concatenate(parts, axis=1), jnp.concatenate([chosen] * len(parts), axis=0), preferred_element_type=jnp.float32
    )


def exact_dot(left, right):
    return jnp.dot(left, right, precision=highest, preferred_element_type=jnp.float32)


def softplus(value):
    small = jnp.exp(-jnp.abs(value))
    ratio = small / (2.0 + small)
    square = ratio * ratio
    series = jnp.full_like(square, 1.0 / 17.0)
    for power in (15, 13, 11, 9, 7, 5, 3, 1):
        series = series * square + 1.0 / power
    return jnp.maximum(value, 0.0) + 2.0 * ratio * series


def lane_of_head(pair, base, transposed=False):
    shape = (LANES, LANES)
    head = lax.broadcasted_iota(jnp.int32, shape, 1 if transposed else 0)
    lane = lax.broadcasted_iota(jnp.int32, shape, 0 if transposed else 1)
    return jnp.where(head == base + 2 * pair + lane // HDIM, 1.0, 0.0).astype(low)


def own_lanes(parts, side):
    lane = lax.broadcasted_iota(jnp.int32, parts[0].shape, 1)
    return tuple(jnp.where(lane // HDIM == side, p, jnp.zeros_like(p)) for p in parts)


def decays(column, row, after_row):
    mid = column.shape[0] // 2
    shape = (mid, mid)
    down = lax.broadcasted_iota(jnp.int32, shape, 0)
    across = lax.broadcasted_iota(jnp.int32, shape, 1)
    keep = (down <= across) if after_row else (down >= across)

    def block(rows, cols, masked):
        gap = column[rows] - row[:, cols]
        gap = -gap if after_row else gap
        return jnp.exp(jnp.where(keep, gap, -1e30)) if masked else jnp.exp(gap)

    early, late = slice(0, mid), slice(mid, 2 * mid)
    side = block(early, late, False) if after_row else block(late, early, False)
    return block(early, early, True), side, block(late, late, True)


def taps_of(extended, size, kernel, offset):
    total = offset + kernel[0:1] * extended[pl.ds(8 - CONVW + 1, size), :]
    for index in range(1, CONVW):
        total = total + kernel[index : index + 1] * extended[pl.ds(8 - CONVW + 1 + index, size), :]
    return total


def step_sizes(raw, heads):
    delta = softplus(raw + heads[0:1])
    change = -delta * jnp.exp(heads[1:2])
    size = raw.shape[0]
    below = lax.broadcasted_iota(jnp.int32, (size, size), 0) >= lax.broadcasted_iota(jnp.int32, (size, size), 1)
    return delta, change, exact_dot(below.astype(jnp.float32), change)


def forward_kernel(
    table_ref, z_ref, x_ref, shared_ref, step_ref, chan_ref, shared_chan_ref, head_ref,
    gated_ref, mixed_ref, state_ref, square_ref,
    tails, shared_tail, states,
    extended, shared_extended, meet, read_high, read_low, keys_high, keys_low,
    delta_all, run_all, run_rows,
):
    chunk, pair = pl.program_id(0), pl.program_id(1)
    size = x_ref.shape[0]
    base = table_ref[pl.num_programs(0)]

    @pl.when(pair == 0)
    def _():
        @pl.when(chunk == 0)
        def _():
            shared_tail[...] = jnp.zeros_like(shared_tail)
            tails[...] = jnp.zeros_like(tails)
            states[...] = jnp.zeros_like(states)

        shared_extended[0:8, :] = shared_tail[...]
        shared_extended[8:, :] = shared_ref[...]
        shared_tail[...] = shared_ref[size - 8 :, :]
        pre = taps_of(shared_extended, size, shared_chan_ref[...], shared_chan_ref[4:5, :])
        active = pre * jax.nn.sigmoid(pre)
        keys, read = halves(active[:, :NST]), halves(active[:, NST:])
        meet[...] = product(read, keys, 1)
        read_high[...], read_low[...] = read
        keys_high[...], keys_low[...] = halves(active[:, :NST].T)
        delta, _, running = step_sizes(step_ref[...], head_ref[...])
        for k, (d, r) in enumerate(zip(thirds(delta), thirds(running))):
            delta_all[k] = d
            run_all[k] = r
        run_rows[...] = running.T
        square_ref[...] = jnp.zeros_like(square_ref)

    chan = chan_ref[...]
    extended[0:8, :] = tails[pair]
    extended[8:, :] = x_ref[...]
    tails[pair] = x_ref[size - 8 :, :]
    pre = taps_of(extended, size, chan, chan[4:5])
    values = pre * jax.nn.sigmoid(pre)
    lanes = lane_of_head(pair, base)
    delta = spread([delta_all[k] for k in range(3)], lanes)
    running = spread([run_all[k] for k in range(3)], lanes)
    stepped = delta * values
    stepped_halves = halves(stepped)
    mid = size // 2
    top, bottom, sources = [], [], []
    for side in range(2):
        column = running[:, side * HDIM : side * HDIM + 1]
        row = run_rows[pl.ds(base + 2 * pair + side, 1), :]
        first, below, second = decays(column, row, False)
        top.append(halves(first * meet[:mid, :mid]))
        bottom.append(
            (halves(below * meet[mid:, :mid]), halves(second * meet[mid:, mid:]))
        )
        sources.append(own_lanes(stepped_halves, side))
    joined = lambda parts, axis: tuple(jnp.concatenate(p, axis=axis) for p in zip(*parts))
    upper = product(joined(top, 1), joined([tuple(p[:mid] for p in x) for x in sources], 0))
    lower = product(joined([joined(b, 1) for b in bottom], 1), joined(sources, 0))
    local = jnp.concatenate([upper, lower], axis=0)
    state = states[pair]
    state_ref[0, 0] = state
    carried = product((read_high[...], read_low[...]), halves(state))
    scanned = local + jnp.exp(running) * carried
    last = running[size - 1 :, :]
    tail = halves(stepped * jnp.exp(last - running))
    states[pair] = jnp.exp(last) * state + product((keys_high[...], keys_low[...]), tail)
    mixed = scanned + chan[5:6] * values
    z = z_ref[...]
    gated = mixed * (z * jax.nn.sigmoid(z))
    mixed_ref[...] = mixed
    gated_ref[...] = gated
    square_ref[...] += gated * gated


def gate_kernel(
    z_ref, gated_ref, mixed_ref, up_ref, chan_ref, stats_ref,
    z_grad_ref, mix_grad_ref, square_ref, gain_grad_ref,
):
    @pl.when(pl.program_id(0) == 0)
    def _():
        gain_grad_ref[...] = jnp.zeros_like(gain_grad_ref)

    stats = stats_ref[...].T
    scale, pull = stats[:, 0:1], stats[:, 1:2]
    z, gated = z_ref[...], gated_ref[...]
    scaled = up_ref[...] * scale
    z_gain = jax.nn.sigmoid(z)
    gated_grad = scaled * chan_ref[6:7, :] - gated * pull
    z_gate = gated_grad * z_gain
    mix_grad_ref[...] = z_gate * z
    z_grad = (z_gate * mixed_ref[...] * (1.0 + z * (1.0 - z_gain))).astype(z_grad_ref.dtype)
    z_grad_ref[...] = z_grad
    wide_grad = z_grad.astype(jnp.float32)
    square_ref[...] = jnp.sum(wide_grad * wide_grad, axis=1, keepdims=True)
    gain_grad_ref[0:1, :] += jnp.sum(scaled * gated, axis=0, keepdims=True)


def backward_kernel(
    start, chunks, table_ref, x_ref, x_before_ref, shared_ref, shared_before_ref, step_ref, chan_ref, shared_chan_ref, head_ref,
    mixed_ref, mix_grad_ref, state_ref, state_after_ref, carried_in, *refs
):
    carried_in = (carried_in,) + refs[:5]
    (
        x_grad_ref, square_ref, shared_grad_ref,
        state_grads, heads_after, shared_after, chan_grad_ref, shared_chan_grad_ref, head_grad_ref,
        extended, shared_extended, later, shared_later, shared_pre,
        meet, read_high, read_low, keys_high, keys_low, read_rows_high, read_rows_low,
        delta_all, change_all, run_all, run_rows, meet_grad, keys_grad, read_grad, run_grad, delta_grad, last_grad,
    ) = refs[-31:]
    carried_out = (state_grads, heads_after, shared_after, chan_grad_ref, shared_chan_grad_ref, head_grad_ref)
    turn, pair, pairs = pl.program_id(0), pl.program_id(1), pl.num_programs(1)
    first = turn == start
    size = x_ref.shape[0]
    base = table_ref[chunks]

    @pl.when(pair == 0)
    def _():
        @pl.when(turn == 0)
        def _():
            for new, old in zip(carried_out, carried_in):
                new[...] = old[...]

        shared_extended[0:8, :] = jnp.where(first, 0.0, shared_before_ref[...])
        shared_extended[8:, :] = shared_ref[...]
        pre = taps_of(shared_extended, size, shared_chan_ref[...], shared_chan_ref[4:5, :])
        shared_pre[...] = pre
        active = pre * jax.nn.sigmoid(pre)
        keys, read = halves(active[:, :NST]), halves(active[:, NST:])
        meet[...] = product(keys, read, 1)
        read_high[...], read_low[...] = read
        keys_high[...], keys_low[...] = keys
        read_rows_high[...], read_rows_low[...] = halves(active[:, NST:].T)
        delta, change, running = step_sizes(step_ref[...], head_ref[...])
        for k, (d, r) in enumerate(zip(thirds(delta), thirds(running))):
            delta_all[k] = d
            run_all[k] = r
        change_all[...] = change
        run_rows[...] = running.T
        meet_grad[...] = jnp.zeros_like(meet_grad)
        keys_grad[...] = jnp.zeros_like(keys_grad)
        read_grad[...] = jnp.zeros_like(read_grad)
        run_grad[...] = jnp.zeros_like(run_grad)
        delta_grad[...] = jnp.zeros_like(delta_grad)
        last_grad[...] = jnp.zeros_like(last_grad)
        square_ref[...] = jnp.zeros_like(square_ref)

    chan = chan_ref[...]
    extended[0:8, :] = jnp.where(first, 0.0, x_before_ref[...])
    extended[8:, :] = x_ref[...]
    pre = taps_of(extended, size, chan, chan[4:5])
    gain = jax.nn.sigmoid(pre)
    values = pre * gain
    lanes = lane_of_head(pair, base)
    delta = spread([delta_all[k] for k in range(3)], lanes)
    running = spread([run_all[k] for k in range(3)], lanes)
    stepped = delta * values

    mixed, mix_grad = mixed_ref[...], mix_grad_ref[...]
    last = running[size - 1 :, :]
    fall = jnp.exp(last - running)
    rise = jnp.exp(running)
    state, state_grad = state_ref[0, 0], state_grads[pair]
    state_halves, state_grad_halves = halves(state), halves(state_grad)
    keys = (keys_high[...], keys_low[...])
    stepped_grad = fall * product(keys, state_grad_halves)
    keys_grad[...] += product(halves(stepped * fall), state_grad_halves, 1)
    risen = halves(mix_grad * rise)
    read_grad[...] += product(risen, state_halves, 1)
    ended = jnp.sum(state_grad * state_after_ref[0, 0], axis=0, keepdims=True)
    state_grads[pair] = jnp.exp(last) * state_grad + product((read_rows_high[...], read_rows_low[...]), risen)

    mid = size // 2
    grad_halves, stepped_halves = halves(mix_grad), halves(stepped)
    early, late = slice(0, mid), slice(mid, size)
    joined = lambda parts, axis: tuple(jnp.concatenate(p, axis=axis) for p in zip(*parts))
    top, bottom, sources = [], [], []
    first_grad = side_grad = second_grad = 0.0
    for side in range(2):
        column = running[:, side * HDIM : side * HDIM + 1]
        row = run_rows[pl.ds(base + 2 * pair + side, 1), :]
        first, beside, second = decays(column, row, True)
        top.append((halves(first * meet[early, early]), halves(beside * meet[early, late])))
        bottom.append(halves(second * meet[late, late]))
        sources.append(own_lanes(grad_halves, side))
        mine = own_lanes(stepped_halves, side)
        wide_grad = product(tuple(p[early] for p in mine), grad_halves, 1)
        first_grad += first * wide_grad[:, early]
        side_grad += beside * wide_grad[:, late]
        second_grad += second * product(tuple(p[late] for p in mine), tuple(p[late] for p in grad_halves), 1)
    meet_grad[early, early] += first_grad
    meet_grad[early, late] += side_grad
    meet_grad[late, late] += second_grad
    upper = product(joined([joined(t, 1) for t in top], 1), joined(sources, 0))
    lower = product(joined(bottom, 1), joined([tuple(p[late] for p in x) for x in sources], 0))
    stepped_grad = stepped_grad + jnp.concatenate([upper, lower], axis=0)
    to_head = lane_of_head(pair, base, transposed=True)
    scanned = mixed - chan[5:6] * values
    run_grad[...] += spread(halves(mix_grad * scanned - stepped * stepped_grad), to_head)
    delta_grad[...] += spread(halves(values * stepped_grad), to_head)
    last_grad[...] += spread(thirds(jnp.broadcast_to(ended, (8, LANES))), to_head)

    values_grad = chan[5:6] * mix_grad + delta * stepped_grad
    pre_grad = values_grad * (gain * (1.0 + pre * (1.0 - gain)))
    later[0:size, :] = pre_grad
    later[size:, :] = heads_after[pair]
    heads_after[pair] = pre_grad[0:8]
    x_grad = chan[0:1] * later[pl.ds(CONVW - 1, size), :]
    for index in range(1, CONVW):
        x_grad = x_grad + chan[index : index + 1] * later[pl.ds(CONVW - 1 - index, size), :]
    x_grad = x_grad.astype(x_grad_ref.dtype)
    x_grad_ref[:, pl.ds(pl.multiple_of(pair * LANES, LANES), LANES)] = x_grad
    wide_grad = x_grad.astype(jnp.float32)
    square_ref[...] += wide_grad * wide_grad
    for index in range(CONVW):
        seen = extended[pl.ds(8 - CONVW + 1 + index, size), :]
        chan_grad_ref[pair, index : index + 1, :] += jnp.sum(pre_grad * seen, axis=0, keepdims=True)
    chan_grad_ref[pair, 4:5, :] += jnp.sum(pre_grad, axis=0, keepdims=True)
    chan_grad_ref[pair, 5:6, :] += jnp.sum(mix_grad * values, axis=0, keepdims=True)

    @pl.when(pair == pairs - 1)
    def _():
        meet_halves = halves(meet_grad[...])
        keys_all = keys_grad[...] + product(meet_halves, (read_high[...], read_low[...]))
        read_all = read_grad[...] + product(halves(meet_grad[...].T), (keys_high[...], keys_low[...]))
        pre_s = shared_pre[...]
        gain_s = jax.nn.sigmoid(pre_s)
        chan_s = shared_chan_ref[...]
        grad_s = jnp.concatenate([keys_all, read_all], axis=1) * (gain_s * (1.0 + pre_s * (1.0 - gain_s)))
        shared_later[0:size, :] = grad_s
        shared_later[size:, :] = shared_after[...]
        shared_after[...] = grad_s[0:8]
        out = chan_s[0:1] * shared_later[pl.ds(CONVW - 1, size), :]
        for index in range(1, CONVW):
            out = out + chan_s[index : index + 1] * shared_later[pl.ds(CONVW - 1 - index, size), :]
        shared_grad_ref[...] = out
        for index in range(CONVW):
            seen = shared_extended[pl.ds(8 - CONVW + 1 + index, size), :]
            shared_chan_grad_ref[index : index + 1, :] += jnp.sum(grad_s * seen, axis=0, keepdims=True)
        shared_chan_grad_ref[4:5, :] += jnp.sum(grad_s, axis=0, keepdims=True)

        above = lax.broadcasted_iota(jnp.int32, (size, size), 0) <= lax.broadcasted_iota(jnp.int32, (size, size), 1)
        change_grad = exact_dot(above.astype(jnp.float32), run_grad[...]) + last_grad[0:1, :]
        rate = jnp.exp(head_ref[1:2, :])
        raw = step_ref[...] + head_ref[0:1, :]
        raw_grad = (delta_grad[...] - change_grad * rate) * jax.nn.sigmoid(raw)
        raw_low = raw_grad.astype(x_grad_ref.dtype)
        x_grad_ref[:, x_grad_ref.shape[1] - LANES :] = raw_low
        wide_raw = raw_low.astype(jnp.float32)
        square_ref[...] += wide_raw * wide_raw
        head_grad_ref[0:1, :] += jnp.sum(raw_grad, axis=0, keepdims=True)
        head_grad_ref[1:2, :] += jnp.sum(change_grad * change_all[...], axis=0, keepdims=True)


def run_forward(table, projected, chan, shared_chan, head_rows):
    length, wide = projected.shape[0], chan.shape[1]
    chunks, pairs = length // SPAN, wide // LANES
    f32 = jnp.float32
    block = pl.BlockSpec((SPAN, LANES), lambda c, p, t: (t[c], p))
    return pl.pallas_call(
        forward_kernel,
        grid_spec=pltpu.PrefetchScalarGridSpec(
            num_scalar_prefetch=1,
            grid=(chunks, pairs),
            in_specs=[
                block,
                pl.BlockSpec((SPAN, LANES), lambda c, p, t: (t[c], pairs + 2 + p)),
                pl.BlockSpec((SPAN, 2 * NST), lambda c, p, t: (t[c], pairs // 2)),
                pl.BlockSpec((SPAN, LANES), lambda c, p, t: (t[c], 2 * pairs + 2)),
                pl.BlockSpec((8, LANES), lambda c, p, t: (0, p)),
                pl.BlockSpec((8, 2 * NST), lambda c, p, t: (0, 0)),
                pl.BlockSpec((8, LANES), lambda c, p, t: (0, 0)),
            ],
            out_specs=[
                block,
                block,
                pl.BlockSpec((1, 1, NST, LANES), lambda c, p, t: (c, p, 0, 0)),
                pl.BlockSpec((SPAN, LANES), lambda c, p, t: (t[c], 0)),
            ],
            scratch_shapes=[
                pltpu.VMEM((pairs, 8, LANES), f32),
                pltpu.VMEM((8, 2 * NST), f32),
                pltpu.VMEM((pairs, NST, LANES), f32),
                pltpu.VMEM((SPAN + 8, LANES), f32),
                pltpu.VMEM((SPAN + 8, 2 * NST), f32),
                pltpu.VMEM((SPAN, SPAN), f32),
                pltpu.VMEM((SPAN, NST), low),
                pltpu.VMEM((SPAN, NST), low),
                pltpu.VMEM((NST, SPAN), low),
                pltpu.VMEM((NST, SPAN), low),
                pltpu.VMEM((3, SPAN, LANES), low),
                pltpu.VMEM((3, SPAN, LANES), low),
                pltpu.VMEM((LANES, SPAN), f32),
            ],
        ),
        out_shape=[
            jax.ShapeDtypeStruct((length, wide), f32),
            jax.ShapeDtypeStruct((length, wide), f32),
            jax.ShapeDtypeStruct((chunks, pairs, NST, LANES), f32),
            jax.ShapeDtypeStruct((length, LANES), f32),
        ],
        compiler_params=pltpu.CompilerParams(vmem_limit_bytes=20 * MIB),
        name="mixer_forward",
    )(table, projected, projected, projected, projected, chan, shared_chan, head_rows)


def run_gate(projected, gated, mixed, up, chan, stats):
    length, wide = gated.shape
    f32 = jnp.float32
    size = SPAN
    block = pl.BlockSpec((size, wide), lambda c: (c, 0))
    whole = pl.BlockSpec((8, wide), lambda c: (0, 0))
    return pl.pallas_call(
        gate_kernel,
        grid=(length // size,),
        in_specs=[block, block, block, block, whole, pl.BlockSpec((8, size), lambda c: (0, c))],
        out_specs=[block, block, pl.BlockSpec((size, 1), lambda c: (c, 0)), whole],
        out_shape=[
            jax.ShapeDtypeStruct((length, wide), low),
            jax.ShapeDtypeStruct((length, wide), f32),
            jax.ShapeDtypeStruct((length, 1), f32),
            jax.ShapeDtypeStruct((8, wide), f32),
        ],
        compiler_params=pltpu.CompilerParams(vmem_limit_bytes=20 * MIB),
        name="gate_backward",
    )(projected, gated, mixed, up, chan, stats)


def run_backward(start, count, table, projected, chan, shared_chan, head_rows, mixed, mix_grad, states, carried, before):
    length, wide = projected.shape[0], chan.shape[1]
    chunks, pairs = length // SPAN, wide // LANES
    f32 = jnp.float32
    lines = SPAN // 8
    earlier = lambda c: jnp.maximum(start - c - 1, 0)
    following = lambda c: jnp.minimum(start - c + 1, chunks - 1)
    block = pl.BlockSpec((SPAN, LANES), lambda c, p, t: (t[start - c], p))
    flat = pl.BlockSpec((8, 2 * NST), lambda c, p, t: (0, 0))
    head = pl.BlockSpec((8, LANES), lambda c, p, t: (0, 0))
    carries = [
        pl.BlockSpec((pairs, NST, LANES), lambda c, p, t: (0, 0, 0)),
        pl.BlockSpec((pairs, 8, LANES), lambda c, p, t: (0, 0, 0)),
        flat,
        pl.BlockSpec((pairs, 8, LANES), lambda c, p, t: (0, 0, 0)),
        flat,
        head,
    ]
    carried_shapes = [jax.ShapeDtypeStruct(c.shape, f32) for c in carried]
    return pl.pallas_call(
        functools.partial(backward_kernel, start, chunks),
        grid_spec=pltpu.PrefetchScalarGridSpec(
            num_scalar_prefetch=1,
            grid=(count, pairs),
            in_specs=[
                pl.BlockSpec((SPAN, LANES), lambda c, p, t: (t[start - c], pairs + 2 + p)),
                pl.BlockSpec((8, LANES), lambda c, p, t: (t[earlier(c)] * lines + lines - 1, pairs + 2 + p)),
                pl.BlockSpec((SPAN, 2 * NST), lambda c, p, t: (t[start - c], pairs // 2)),
                pl.BlockSpec((8, 2 * NST), lambda c, p, t: (t[earlier(c)] * lines + lines - 1, pairs // 2)),
                pl.BlockSpec((SPAN, LANES), lambda c, p, t: (t[start - c], 2 * pairs + 2)),
                pl.BlockSpec((8, LANES), lambda c, p, t: (0, p)),
                flat,
                head,
                block,
                block,
                pl.BlockSpec((1, 1, NST, LANES), lambda c, p, t: (start - c, p, 0, 0)),
                pl.BlockSpec((1, 1, NST, LANES), lambda c, p, t: (following(c), p, 0, 0)),
            ]
            + carries
            + [pl.BlockSpec(memory_space=pl.ANY)] * len(before),
            out_specs=[
                pl.BlockSpec((SPAN, wide + LANES), lambda c, p, t: (t[start - c], 0)),
                pl.BlockSpec((SPAN, LANES), lambda c, p, t: (t[start - c], 0)),
                pl.BlockSpec((SPAN, 2 * NST), lambda c, p, t: (t[start - c], 0)),
            ]
            + carries,
            scratch_shapes=[
                pltpu.VMEM((SPAN + 8, LANES), f32),
                pltpu.VMEM((SPAN + 8, 2 * NST), f32),
                pltpu.VMEM((SPAN + 8, LANES), f32),
                pltpu.VMEM((SPAN + 8, 2 * NST), f32),
                pltpu.VMEM((SPAN, 2 * NST), f32),
                pltpu.VMEM((SPAN, SPAN), f32),
                pltpu.VMEM((SPAN, NST), low),
                pltpu.VMEM((SPAN, NST), low),
                pltpu.VMEM((SPAN, NST), low),
                pltpu.VMEM((SPAN, NST), low),
                pltpu.VMEM((NST, SPAN), low),
                pltpu.VMEM((NST, SPAN), low),
                pltpu.VMEM((3, SPAN, LANES), low),
                pltpu.VMEM((SPAN, LANES), f32),
                pltpu.VMEM((3, SPAN, LANES), low),
                pltpu.VMEM((LANES, SPAN), f32),
                pltpu.VMEM((SPAN, SPAN), f32),
                pltpu.VMEM((SPAN, NST), f32),
                pltpu.VMEM((SPAN, NST), f32),
                pltpu.VMEM((SPAN, LANES), f32),
                pltpu.VMEM((SPAN, LANES), f32),
                pltpu.VMEM((8, LANES), f32),
            ],
        ),
        out_shape=[
            jax.ShapeDtypeStruct((length, wide + LANES), low),
            jax.ShapeDtypeStruct((length, LANES), f32),
            jax.ShapeDtypeStruct((length, 2 * NST), f32),
        ]
        + carried_shapes,
        input_output_aliases={19 + k: k for k in range(len(before))},
        compiler_params=pltpu.CompilerParams(vmem_limit_bytes=50 * MIB),
        name="mixer_backward",
    )(
        table, projected, projected, projected, projected, projected, chan, shared_chan, head_rows,
        mixed, mix_grad, states, states, *carried, *before,
    )


def halve(block, left, bit, axis):
    place = left.index(bit)
    own = (lax.axis_index(axis) & bit) // bit
    keep = lax.dynamic_index_in_dim(block, own, place, keepdims=False)
    send = lax.dynamic_index_in_dim(block, 1 - own, place, keepdims=False)
    return keep + swap(send, axis, bit), [b for b in left if b != bit]


class Scatter:
    def __init__(self, arrays, axis, phase=0):
        self.axis = axis
        size = lax.axis_size(axis)
        bits = [1 << k for k in range(size.bit_length() - 1)]
        upper = bits[1:]
        turned = upper[len(upper) // 2 :] + upper[: len(upper) // 2]
        self.orders = [bits[:1] + (upper if (k + phase) % 2 == 0 else turned) for k in range(len(arrays))]
        self.left = [bits[::-1] for _ in arrays]
        self.blocks = [
            a.reshape((2,) * len(bits) + (a.shape[0] // size,) + a.shape[1:]) for a in arrays
        ]
        self.steps = len(bits)
        self.done = 0

    def step(self):
        for k in range(len(self.blocks)):
            self.blocks[k], self.left[k] = halve(
                self.blocks[k], self.left[k], self.orders[k][self.done], self.axis
            )
        self.done += 1

    def finish(self):
        while self.done < self.steps:
            self.step()
        return self.blocks


def update_kernel(
    pieces, widths, rate, decay, slot_ref, source_ref, param_ref, first_ref, second_ref,
    grad_ref, param_out, first_out, second_out,
):
    for piece, width in zip(range(pieces), widths):
        at = sum(widths[:piece])
        own = slice(at, at + width)
        grad = source_ref[slot_ref[piece], :, :width]
        new = adamw_update(param_ref[:, own], grad, first_ref[:, own], second_ref[:, own], rate, decay)
        grad_ref[:, own] = grad
        param_out[:, own], first_out[:, own], second_out[:, own] = new


def run_update(slots, sources, widths, param, first, second, rate, decay):
    rows, total = param.shape
    size = 16 if rows % 16 == 0 else rows
    block = pl.BlockSpec((size, total), lambda r, t: (r, 0))
    return pl.pallas_call(
        functools.partial(update_kernel, len(widths), widths, rate, decay),
        grid_spec=pltpu.PrefetchScalarGridSpec(
            num_scalar_prefetch=1,
            grid=(rows // size,),
            in_specs=[pl.BlockSpec((sources.shape[0], size, sources.shape[2]), lambda r, t: (0, r, 0))] + [block] * 3,
            out_specs=[block] * 4,
        ),
        out_shape=[jax.ShapeDtypeStruct(param.shape, jnp.float32)] * 4,
        compiler_params=pltpu.CompilerParams(vmem_limit_bytes=20 * MIB),
        name="weight_update",
    )(slots, sources, param, first, second)


def adamw_update(param, grad, first, second, rate, decay):
    first_new = beta_one * first + (1.0 - beta_one) * grad
    second_new = beta_two * second + (1.0 - beta_two) * grad * grad
    corrected_first = first_new * (1.0 / (1.0 - beta_one**adam_step))
    corrected_second = second_new * (1.0 / (1.0 - beta_two**adam_step))
    param_new = param - rate * (
        corrected_first / (jnp.sqrt(corrected_second) + adam_eps) + decay * param
    )
    return (param_new, first_new, second_new)


def dot(left, right):
    return jnp.dot(left, right, preferred_element_type=jnp.float32)


def body(
    block_input,
    cotangent,
    norm_gain,
    in_weight,
    conv_weight,
    conv_bias,
    step_bias,
    decay_log,
    skip_gain,
    gated_gain,
    out_weight,
    first_norm_gain,
    second_norm_gain,
    first_in_weight,
    second_in_weight,
    first_conv_weight,
    second_conv_weight,
    first_conv_bias,
    second_conv_bias,
    first_step_bias,
    second_step_bias,
    first_decay_log,
    second_decay_log,
    first_skip_gain,
    second_skip_gain,
    first_gated_gain,
    second_gated_gain,
    first_out_weight,
    second_out_weight,
):
    ranks, rank = lax.axis_size(SEQ), lax.axis_index(SEQ)
    groups = lax.axis_size(DP)
    devices = ranks * groups
    wide, heads = E // ranks, NHEADS // ranks
    rows = in_weight.shape[0]
    width = rows * devices
    taps = conv_bias.shape[0]
    channels = taps * devices
    step_at = 2 * E + 2 * NST
    spare = LANES - (in_weight.shape[1] - step_at)

    packed = jnp.concatenate(
        [norm_gain, conv_weight.reshape(-1), conv_bias, gated_gain]
    ).astype(low).astype(jnp.float32)
    gains = gated_gain.shape[0]
    filled = packed.shape[0]
    lines = -(-filled // LANES)
    packed = jnp.pad(packed, (0, lines * LANES - filled)).reshape(lines, LANES)
    small_line = gather_direct(packed, SEQ)
    small = gather_bits(small_line, DP)
    small = small.reshape(devices, lines * LANES)
    norm_float = small[:, :rows].reshape(-1)
    kernel_float = small[:, rows : rows + CONVW * taps].reshape(devices, CONVW, taps)
    kernel_float = kernel_float.transpose(1, 0, 2).reshape(CONVW, channels)
    offset_float = small[:, rows + CONVW * taps : rows + (CONVW + 1) * taps].reshape(-1)
    gated_float = small[:, rows + (CONVW + 1) * taps : filled].reshape(-1)
    kernel_own = lax.dynamic_slice_in_dim(kernel_float, rank * wide, wide, 1)
    offset_own = lax.dynamic_slice_in_dim(offset_float, rank * wide, wide, 0)
    gated_own = lax.dynamic_slice_in_dim(gated_float, rank * wide, wide, 0)
    skip_own = lax.dynamic_slice_in_dim(skip_gain, rank * heads, heads, 0)

    in_low = in_weight.astype(low)
    out_low = out_weight.astype(low)

    def for_rank(j):
        return jnp.concatenate(
            [
                lax.dynamic_slice_in_dim(in_low, j * wide, wide, 1),
                in_low[:, 2 * E : step_at],
                lax.dynamic_slice_in_dim(in_low, E + j * wide, wide, 1),
                jnp.pad(in_low[:, step_at:], ((0, 0), (0, spare))),
                lax.dynamic_slice_in_dim(out_low, j * wide, wide, 1),
            ],
            axis=1,
        )

    columns = 2 * NST + 2 * wide + LANES
    weights_arrived = []
    for turn in range(1, ranks):
        weights_arrived.append(shift(for_rank((rank + turn) % ranks), SEQ, turn))

    tokens, upstream = block_input[0], cotangent[0]
    span = tokens.shape[0]
    length = span * ranks
    inverse = lax.rsqrt(jnp.mean(tokens * tokens, axis=-1, keepdims=True) + norm_eps)
    hidden_own = (tokens * inverse * norm_float).astype(low)
    weights_arrived = [after(part, hidden_own) for part in weights_arrived]
    weight_rows = jnp.zeros((ranks, rows, columns + wide), low)
    weight_rows = lax.dynamic_update_index_in_dim(weight_rows, for_rank(rank), rank, 0)
    for turn in range(1, ranks):
        weight_rows = lax.dynamic_update_index_in_dim(
            weight_rows, weights_arrived[turn - 1], (rank + ranks - turn) % ranks, 0
        )
    weight_rows = weight_rows.reshape(ranks * rows, columns + wide)
    in_full, out_full = gather_rows([weight_rows[:, :columns], weight_rows[:, columns:]], DP)

    line_parts = near_parts(hidden_own, SEQ)
    line_parts = [after(part, in_full, out_full) for part in line_parts]
    up_parts = near_parts(after(upstream.astype(low), *line_parts), SEQ)
    hidden = jnp.stack(line_parts).reshape(length, width)

    projected = dot(hidden, in_full)
    none = jnp.zeros((1, wide), jnp.float32)
    chan = jnp.concatenate(
        [kernel_own, offset_own[None], jnp.repeat(skip_own, HDIM)[None], gated_own[None], none], axis=0
    )
    shared_chan = jnp.concatenate(
        [kernel_float[:, E:], offset_float[None, E:], jnp.zeros((3, 2 * NST), jnp.float32)], axis=0
    )
    head_rows = jnp.pad(jnp.stack([step_bias, decay_log]), ((0, 6), (0, LANES - NHEADS)))
    pairs, chunks = wide // LANES, length // SPAN
    per_rank = span // SPAN
    order = jnp.arange(chunks, dtype=jnp.int32)
    order = (rank + ranks - order // per_rank) % ranks * per_rank + order % per_rank
    table = jnp.concatenate([order, jnp.reshape(rank * heads, (1,))]).astype(jnp.int32)
    zeros = functools.partial(jnp.zeros, dtype=jnp.float32)
    gated, mixed, states, squares = run_forward(table, projected, chan, shared_chan, head_rows)
    packed_length = (ranks, span // LANES, LANES)
    square_sum = sum_near(jnp.sum(squares, axis=1).reshape(packed_length), SEQ).reshape(length)
    scale = lax.rsqrt(square_sum / E + norm_eps)
    normed_low = (gated * scale[:, None] * gated_own).astype(low)
    branch_factor = 2.0 ** (14 - math.ceil(math.log2(0.17 * math.sqrt(E * wide))))
    out_half = (dot(normed_low, out_full.T) * branch_factor).astype(half).reshape(ranks, span, width)

    upstream_low = jnp.stack([after(part, out_half) for part in up_parts]).reshape(length, width)
    normed_grad = dot(upstream_low, out_full)
    pull_sum = jnp.sum(normed_grad * gated_own * gated, axis=1).reshape(packed_length)
    pull_sum = sum_near(pull_sum, SEQ).reshape(length)
    stats = jnp.stack([scale, scale * scale * scale * (pull_sum / E)])
    stats = jnp.pad(stats, ((0, 6), (0, 0)))
    out_grad_part = dot(upstream_low.T, normed_low)
    out_scatter = Scatter([out_grad_part], DP)
    out_scatter.step()
    gate_low, mix_grad, gate_square, gain_rows = run_gate(projected, gated, mixed, normed_grad, chan, stats)
    gated_grad = gain_rows[0]

    branch_parts = send_near(out_half, SEQ)

    gate_scatter = Scatter([dot(hidden.T, gate_low)], DP, 1)
    gate_scatter.step()
    carried = (
        zeros((pairs, NST, LANES)), zeros((pairs, 8, LANES)), zeros((8, 2 * NST)),
        zeros((pairs, 8, LANES)), zeros((8, 2 * NST)), zeros((8, LANES)),
    )
    outputs, early = (), (out_scatter, gate_scatter)
    calls = [(chunks - 1, chunks - 2 * (chunks // 4)), (2 * (chunks // 4) - 1, chunks // 4), (chunks // 4 - 1, chunks // 4)]
    for turn, (start, count) in enumerate(calls):
        ready = tuple(scatter.blocks[0] for scatter in early)
        if turn < len(calls) - 1:
            for scatter in early:
                if scatter.done < scatter.steps:
                    scatter.step()
        else:
            early_sums = jnp.concatenate(
                [block.reshape(ranks, rows, wide) for scatter in early for block in scatter.finish()], axis=2
            )
            early_packed = pack_half(early_sums, jnp.max(jnp.abs(early_sums), axis=-1, keepdims=True))
            early_slots = slots_of(early_sums, early_packed, SEQ)
            ready = (early_packed,)
        mix_grad = after(mix_grad, *ready)
        result = run_backward(
            start, count, table, projected, chan, shared_chan, head_rows, mixed, mix_grad, states, carried, outputs
        )
        outputs, carried = tuple(result[:3]), tuple(result[3:])
    conv_low, conv_square, shared_grad = outputs
    _, _, _, chan_grad, shared_chan_grad, head_grad = carried

    largest = jnp.max(gate_square.reshape(ranks, span) + jnp.sum(conv_square.reshape(ranks, span, LANES), axis=2), axis=1)
    bound = 0.1565 * math.sqrt(2 * wide + NHEADS) * jnp.sqrt(largest)
    power = jnp.clip(jnp.ceil(jnp.log2(bound)) - 14.0, -120.0, 120.0)
    shared_parts = shared_grad.reshape(ranks, span, 2 * NST)
    lines_of_power = jnp.broadcast_to(power[:, None, None], (ranks, 8, 2 * NST))
    shared_sent = send_near(jnp.concatenate([shared_parts, lines_of_power], axis=1), SEQ)

    factors = jnp.exp2(-power)[:, None, None]
    hidden_part = dot(gate_low, in_full[:, :wide].T) + dot(conv_low, in_full[:, wide + 2 * NST :].T)
    hidden_part = hidden_part.reshape(ranks, span, width)
    hidden_half = (hidden_part * factors).astype(half)
    hidden_parts = send_near(hidden_half, SEQ)

    split = 4 * LANES
    conv_parts = [dot(hidden.T, conv_low[:, :split]), dot(hidden.T, conv_low[:, split:])]
    late = Scatter(conv_parts, DP)
    normed_own = normed_low[:span]
    for turn in range(late.steps):
        if turn == 1:
            normed_own = after(normed_own, *late.blocks)
            early_slots = [after(part, *late.blocks) for part in early_slots]
            chan_grad, shared_chan_grad, head_grad = (
                after(part, *late.blocks) for part in (chan_grad, shared_chan_grad, head_grad)
            )
        late.step()
    shared_own = shared_parts[0]
    for part in shared_sent:
        shared_own = shared_own + part[:span]
    shared_own = shared_own.astype(low)
    shared_grad_part = dot(hidden_own.T, shared_own)
    last = Scatter([shared_grad_part], DP, 1)
    for turn in range(last.steps):
        if turn == last.steps - 1:
            hidden_parts = [after(part, *last.blocks) for part in hidden_parts]
            power_parts = [after(part, *last.blocks)[span, 0] for part in shared_sent]
        last.step()
    hidden_grad = hidden_part[0] + dot(shared_own, in_full[:, wide : wide + 2 * NST].T)
    branch = tokens + dot(normed_own, out_full.T)
    for part in branch_parts:
        branch = branch + part.astype(jnp.float32) * (1.0 / branch_factor)
    block_output = branch[None]

    chan_grad = chan_grad.transpose(1, 0, 2).reshape(8, wide)
    kernel_grad, offset_grad = chan_grad[:CONVW], chan_grad[4]
    skip_grad = jnp.sum(chan_grad[5].reshape(heads, HDIM), axis=1)
    kernel_shared_grad, offset_shared_grad = shared_chan_grad[:CONVW], shared_chan_grad[4]

    late_sums = jnp.concatenate([block.reshape(ranks, rows, -1) for block in late.blocks + last.blocks], axis=2)
    late_packed = pack_half(late_sums, jnp.max(jnp.abs(late_sums), axis=-1, keepdims=True))
    late_slots = slots_of(late_sums, late_packed, SEQ)

    for part, exponent in zip(hidden_parts, power_parts):
        hidden_grad = hidden_grad + part.astype(jnp.float32) * jnp.exp2(exponent)
    scaled = tokens * inverse
    gain_grad = jnp.sum(hidden_grad * scaled, axis=0)
    inner = hidden_grad * norm_float
    token_grad = inverse * (inner - scaled * jnp.mean(inner * scaled, axis=-1, keepdims=True))
    input_grad = (upstream + token_grad)[None]

    def placed(own, shared):
        full = jnp.zeros(own.shape[:-1] + (E,), jnp.float32)
        full = lax.dynamic_update_slice_in_dim(full, own, rank * wide, own.ndim - 1)
        return jnp.concatenate([full, shared], axis=-1)

    kernel_all = placed(kernel_grad, kernel_shared_grad).reshape(CONVW, devices, taps)
    kernel_all = kernel_all.transpose(1, 0, 2).reshape(devices, CONVW * taps)
    offset_all = placed(offset_grad, offset_shared_grad).reshape(devices, taps)
    gated_all = lax.dynamic_update_slice_in_dim(jnp.zeros((E,), jnp.float32), gated_grad, rank * wide, 0)
    skip_all = lax.dynamic_update_slice_in_dim(jnp.zeros((NHEADS,), jnp.float32), skip_grad, rank * heads, 0)
    head_all = jnp.concatenate([head_grad[0, :NHEADS], head_grad[1, :NHEADS], skip_all])
    terms = jnp.concatenate(
        [
            kernel_all,
            offset_all,
            gated_all.reshape(devices, gains),
            jnp.broadcast_to(head_all[None], (devices, 3 * NHEADS)),
        ],
        axis=1,
    )
    used = terms.shape[1]
    term_lines = -(-used // LANES)
    terms = jnp.pad(terms, ((0, 0), (0, term_lines * LANES - used)))
    terms = terms.reshape(groups, ranks, term_lines, LANES)
    norm_lines = -(-rows // LANES)
    norm_terms = jnp.pad(gain_grad.reshape(devices, rows), ((0, 0), (0, norm_lines * LANES - rows)))
    norm_terms = norm_terms.reshape(groups, ranks, norm_lines, LANES)
    term_lines += norm_lines
    terms = jnp.concatenate([norm_terms, terms], axis=2).reshape(groups, ranks * term_lines, LANES)
    small_scatter = Scatter([terms], DP)
    for _ in range(small_scatter.steps):
        small_scatter.step()
    summed = small_scatter.blocks[0].reshape(ranks, term_lines, LANES)
    summed = exchange_sum(summed, SEQ).reshape(-1)
    grad_norm_gain = summed[:rows]
    at = norm_lines * LANES
    grad_conv_weight = summed[at : at + CONVW * taps].reshape(CONVW, taps)
    at += CONVW * taps
    grad_conv_bias = summed[at : at + taps]
    at += taps
    grad_gated_gain = summed[at : at + gains]
    at += gains
    grad_step_bias, grad_decay_log, grad_skip_gain = (
        summed[at + k * NHEADS : at + (k + 1) * NHEADS] for k in range(3)
    )
    new_norm_gain, new_first_norm_gain, new_second_norm_gain = adamw_update(
        norm_gain, grad_norm_gain, first_norm_gain, second_norm_gain, rate_vector, 0.0
    )
    place = (rank + ranks - jnp.arange(ranks, dtype=jnp.int32)) % ranks
    early_f32 = early_slots[:1] + list(unpack_half(jnp.stack(early_slots[1:])))
    late_f32 = late_slots[:1] + list(unpack_half(jnp.stack(late_slots[1:])))
    shared_sum = late_f32[0][:, wide:]
    for part in late_f32[1:]:
        shared_sum = shared_sum + part[:, wide:]
    shared_sum = jnp.concatenate([shared_sum[:, LANES:], shared_sum[:, :LANES]], axis=1)
    sources = jnp.stack(
        [part[:, wide:] for part in early_f32]
        + [part[:, :wide] for part in late_f32]
        + [jnp.pad(shared_sum, ((0, 0), (0, wide - shared_sum.shape[1])))]
    )
    slots = jnp.concatenate([place, place + ranks, jnp.full((1,), 2 * ranks)]).astype(jnp.int32)
    widths = (wide,) * (2 * ranks) + (in_weight.shape[1] - 2 * E,)
    grad_in_weight, new_in_weight, new_first_in_weight, new_second_in_weight = run_update(
        slots, sources, widths, in_weight, first_in_weight, second_in_weight, rate_matrix, weight_decay
    )
    new_conv_weight, new_first_conv_weight, new_second_conv_weight = adamw_update(
        conv_weight, grad_conv_weight, first_conv_weight, second_conv_weight, rate_vector, 0.0
    )
    new_conv_bias, new_first_conv_bias, new_second_conv_bias = adamw_update(
        conv_bias, grad_conv_bias, first_conv_bias, second_conv_bias, rate_vector, 0.0
    )
    new_step_bias, new_first_step_bias, new_second_step_bias = adamw_update(
        step_bias, grad_step_bias, first_step_bias, second_step_bias, rate_vector, 0.0
    )
    new_decay_log, new_first_decay_log, new_second_decay_log = adamw_update(
        decay_log, grad_decay_log, first_decay_log, second_decay_log, rate_vector, 0.0
    )
    new_skip_gain, new_first_skip_gain, new_second_skip_gain = adamw_update(
        skip_gain, grad_skip_gain, first_skip_gain, second_skip_gain, rate_vector, 0.0
    )
    new_gated_gain, new_first_gated_gain, new_second_gated_gain = adamw_update(
        gated_gain, grad_gated_gain, first_gated_gain, second_gated_gain, rate_vector, 0.0
    )
    grad_out_weight, new_out_weight, new_first_out_weight, new_second_out_weight = run_update(
        place,
        jnp.stack([part[:, :wide] for part in early_f32]),
        (wide,) * ranks,
        out_weight,
        first_out_weight,
        second_out_weight,
        rate_matrix,
        weight_decay,
    )

    return (
        block_output,
        input_grad,
        grad_norm_gain,
        grad_in_weight,
        grad_conv_weight,
        grad_conv_bias,
        grad_step_bias,
        grad_decay_log,
        grad_skip_gain,
        grad_gated_gain,
        grad_out_weight,
        new_norm_gain,
        new_first_norm_gain,
        new_second_norm_gain,
        new_in_weight,
        new_first_in_weight,
        new_second_in_weight,
        new_conv_weight,
        new_first_conv_weight,
        new_second_conv_weight,
        new_conv_bias,
        new_first_conv_bias,
        new_second_conv_bias,
        new_step_bias,
        new_first_step_bias,
        new_second_step_bias,
        new_decay_log,
        new_first_decay_log,
        new_second_decay_log,
        new_skip_gain,
        new_first_skip_gain,
        new_second_skip_gain,
        new_gated_gain,
        new_first_gated_gain,
        new_second_gated_gain,
        new_out_weight,
        new_first_out_weight,
        new_second_out_weight,
    )


def solution(mesh):
    in_specs = (
        P(DP, SEQ, None),
        P(DP, SEQ, None),
        P((DP, SEQ)),
        P((DP, SEQ), None),
        P(None, (DP, SEQ)),
        P((DP, SEQ)),
        P(),
        P(),
        P(),
        P((DP, SEQ)),
        P((DP, SEQ), None),
        P((DP, SEQ)),
        P((DP, SEQ)),
        P((DP, SEQ), None),
        P((DP, SEQ), None),
        P(None, (DP, SEQ)),
        P(None, (DP, SEQ)),
        P((DP, SEQ)),
        P((DP, SEQ)),
        P(),
        P(),
        P(),
        P(),
        P(),
        P(),
        P((DP, SEQ)),
        P((DP, SEQ)),
        P((DP, SEQ), None),
        P((DP, SEQ), None),
    )
    out_specs = (
        P(DP, SEQ, None),
        P(DP, SEQ, None),
        P((DP, SEQ)),
        P((DP, SEQ), None),
        P(None, (DP, SEQ)),
        P((DP, SEQ)),
        P(),
        P(),
        P(),
        P((DP, SEQ)),
        P((DP, SEQ), None),
        P((DP, SEQ)),
        P((DP, SEQ)),
        P((DP, SEQ)),
        P((DP, SEQ), None),
        P((DP, SEQ), None),
        P((DP, SEQ), None),
        P(None, (DP, SEQ)),
        P(None, (DP, SEQ)),
        P(None, (DP, SEQ)),
        P((DP, SEQ)),
        P((DP, SEQ)),
        P((DP, SEQ)),
        P(),
        P(),
        P(),
        P(),
        P(),
        P(),
        P(),
        P(),
        P(),
        P((DP, SEQ)),
        P((DP, SEQ)),
        P((DP, SEQ)),
        P((DP, SEQ), None),
        P((DP, SEQ), None),
        P((DP, SEQ), None),
    )

    return jax.shard_map(body, mesh=mesh, in_specs=in_specs, out_specs=out_specs, check_vma=False)
```

```python
import functools
import math

import jax
import jax.numpy as jnp
from jax import lax
from jax.experimental import pallas as pl
from jax.experimental.pallas import tpu as pltpu
from jax.sharding import PartitionSpec as P


E = 3072
NST = 128
NHEADS = 48
HDIM = 64
CONVW = 4
SPAN = 256
LANES = 128
MIB = 2**20
SEQ, DP = "seq", "dp"


low = jnp.bfloat16
half = jnp.float16
beta_one = 0.9
beta_two = 0.95
adam_step = 10.0
adam_eps = 1e-08
rate_matrix = 0.01
rate_vector = 0.3
weight_decay = 0.1
norm_eps = 1e-05


def shift(block, axis, distance):
    size = lax.axis_size(axis)
    return lax.ppermute(block, axis, [(i, (i + distance) % size) for i in range(size)])


def step_to(block, axis, distance):
    size = lax.axis_size(axis)
    route = [(i, i + distance) for i in range(size) if 0 <= i + distance < size]
    return lax.ppermute(block, axis, route)


def swap(block, axis, bit):
    return lax.ppermute(block, axis, [(i, i ^ bit) for i in range(lax.axis_size(axis))])


def pick(stacked, index):
    return lax.dynamic_index_in_dim(stacked, index, 0, keepdims=False)


def exchange_sum(stacked, axis):
    size, here = lax.axis_size(axis), lax.axis_index(axis)
    arrived = [shift(pick(stacked, (here + turn) % size), axis, turn) for turn in range(1, size)]
    total = pick(stacked, here)
    for part in arrived:
        total = total + part
    return total


def after(value, *others):
    return lax.optimization_barrier((value,) + others)[0]


def pack_half(parts, bound):
    power = jnp.clip(jnp.ceil(jnp.log2(bound)) - 14.0, -120.0, 120.0)
    scaled = (parts * jnp.exp2(-power)).astype(half)
    return jnp.concatenate([scaled, jnp.broadcast_to(power.astype(half), parts.shape[:-1] + (LANES,))], axis=-1)


def unpack_half(message):
    width = message.shape[-1] - LANES
    return message[..., :width].astype(jnp.float32) * jnp.exp2(message[..., width : width + 1].astype(jnp.float32))


def near_parts(block, axis):
    size, here = lax.axis_size(axis), lax.axis_index(axis)
    if size != 4:
        return [block] + [shift(block, axis, turn) for turn in range(1, size)]
    below, above = step_to(block, axis, 1), step_to(block, axis, -1)
    across = shift(block, axis, 2)
    far = lax.ppermute(across, axis, [(2, 3), (1, 0)])
    return [block, jnp.where(here == 0, far, below), across, jnp.where(here == size - 1, far, above)]


def send_near(stacked, axis):
    return [shift(stacked[turn], axis, lax.axis_size(axis) - turn) for turn in range(1, lax.axis_size(axis))]


def slots_of(own_blocks, packed, axis):
    size, here = lax.axis_size(axis), lax.axis_index(axis)
    arrived = [shift(pick(packed, (here + turn) % size), axis, turn) for turn in range(1, size)]
    return [pick(own_blocks, here)] + arrived


def gather_direct(block, axis):
    size, here = lax.axis_size(axis), lax.axis_index(axis)
    arrived = [block] + [shift(block, axis, turn) for turn in range(1, size)]
    result = jnp.stack(arrived)
    return jnp.take(result, (here + size - jnp.arange(size)) % size, axis=0)


def sum_near(stacked, axis):
    total = stacked
    for turn in range(1, lax.axis_size(axis)):
        total = total + jnp.roll(shift(stacked, axis, turn), turn, axis=0)
    return total


def gather_bits(block, axis):
    here = lax.axis_index(axis)
    result, bit = block[None], 1
    while bit < lax.axis_size(axis):
        other = swap(result, axis, bit)
        upper = (here & bit) > 0
        result = jnp.concatenate(
            [jnp.where(upper, other, result), jnp.where(upper, result, other)], axis=0
        )
        bit *= 2
    return result


def gather_rows(blocks, axis):
    size, here = lax.axis_size(axis), lax.axis_index(axis)
    bits = [1 << k for k in range(size.bit_length() - 1)]
    upper = bits[1:]
    turned = upper[len(upper) // 2 :] + upper[: len(upper) // 2]
    parts, paths = [], []
    for block in blocks:
        rows = block.shape[0] // 2
        parts += [p.reshape((1,) * len(bits) + p.shape) for p in (block[:rows], block[rows:])]
        paths += [upper + bits[:1], turned + bits[:1]]
    for step in range(len(bits)):
        arrived = [swap(p, axis, path[step]) for p, path in zip(parts, paths)]
        for k, path in enumerate(paths):
            place = bits[::-1].index(path[step])
            up = (here & path[step]) > 0
            parts[k] = jnp.concatenate(
                [jnp.where(up, arrived[k], parts[k]), jnp.where(up, parts[k], arrived[k])], axis=place
            )
    return [
        jnp.concatenate(parts[2 * k : 2 * k + 2], axis=len(bits)).reshape(-1, block.shape[1])
        for k, block in enumerate(blocks)
    ]


def halves(value):
    high = value.astype(low)
    return high, (value - high.astype(jnp.float32)).astype(low)


def product(left, right, right_dim=0):
    joined_left = jnp.concatenate([left[0], left[0], left[1]], axis=1)
    joined_right = jnp.concatenate([right[0], right[1], right[0]], axis=right_dim)
    dims = (((1,), (right_dim,)), ((), ()))
    return lax.dot_general(joined_left, joined_right, dims, preferred_element_type=jnp.float32)


def thirds(value):
    high, rest = value.astype(low), value
    rest = value - high.astype(jnp.float32)
    middle = rest.astype(low)
    return high, middle, (rest - middle.astype(jnp.float32)).astype(low)


def spread(parts, chosen):
    return jnp.dot(
        jnp.concatenate(parts, axis=1), jnp.concatenate([chosen] * len(parts), axis=0), preferred_element_type=jnp.float32
    )


def softplus(value):
    small = jnp.exp(-jnp.abs(value))
    ratio = small / (2.0 + small)
    square = ratio * ratio
    series = jnp.full_like(square, 1.0 / 15.0)
    for power in (13, 11, 9, 7, 5, 3, 1):
        series = series * square + 1.0 / power
    return jnp.maximum(value, 0.0) + 2.0 * ratio * series


def lane_of_head(pair, base, transposed=False):
    shape = (LANES, LANES)
    head = lax.broadcasted_iota(jnp.int32, shape, 1 if transposed else 0)
    lane = lax.broadcasted_iota(jnp.int32, shape, 0 if transposed else 1)
    return jnp.where(head == base + 2 * pair + lane // HDIM, 1.0, 0.0).astype(low)


def own_lanes(parts, side):
    lane = lax.broadcasted_iota(jnp.int32, parts[0].shape, 1)
    return tuple(jnp.where(lane // HDIM == side, p, jnp.zeros_like(p)) for p in parts)


def decays(column, row, after_row):
    mid = column.shape[0] // 2
    shape = (mid, mid)
    down = lax.broadcasted_iota(jnp.int32, shape, 0)
    across = lax.broadcasted_iota(jnp.int32, shape, 1)
    keep = (down <= across) if after_row else (down >= across)

    def block(rows, cols, masked):
        gap = column[rows] - row[:, cols]
        gap = -gap if after_row else gap
        return jnp.exp(jnp.where(keep, gap, -1e30)) if masked else jnp.exp(gap)

    early, late = slice(0, mid), slice(mid, 2 * mid)
    side = block(early, late, False) if after_row else block(late, early, False)
    return block(early, early, True), side, block(late, late, True)


def taps_of(extended, size, kernel, offset):
    total = offset + kernel[0:1] * extended[pl.ds(8 - CONVW + 1, size), :]
    for index in range(1, CONVW):
        total = total + kernel[index : index + 1] * extended[pl.ds(8 - CONVW + 1 + index, size), :]
    return total


def running_sum(chosen, value):
    ones = jnp.where(chosen, 1.0, 0.0).astype(low)
    return jnp.dot(
        jnp.concatenate([ones] * 3, axis=1), jnp.concatenate(thirds(value), axis=0), preferred_element_type=jnp.float32
    )


def step_sizes(raw, heads):
    delta = softplus(raw + heads[0:1])
    change = -delta * jnp.exp(heads[1:2])
    size = raw.shape[0]
    below = lax.broadcasted_iota(jnp.int32, (size, size), 0) >= lax.broadcasted_iota(jnp.int32, (size, size), 1)
    return delta, change, running_sum(below, change)


def forward_kernel(
    table_ref, z_ref, x_ref, shared_ref, step_ref, chan_ref, shared_chan_ref, head_ref,
    gated_ref, mixed_ref, state_ref, square_ref,
    tails, shared_tail, states,
    extended, shared_extended, meet, read_high, read_low, keys_high, keys_low,
    delta_all, run_all, run_rows,
):
    chunk, pair = pl.program_id(0), pl.program_id(1)
    size = x_ref.shape[0]
    base = table_ref[pl.num_programs(0)]

    @pl.when(pair == 0)
    def _():
        @pl.when(chunk == 0)
        def _():
            shared_tail[...] = jnp.zeros_like(shared_tail)
            tails[...] = jnp.zeros_like(tails)
            states[...] = jnp.zeros_like(states)

        shared_extended[0:8, :] = shared_tail[...]
        shared_extended[8:, :] = shared_ref[...]
        shared_tail[...] = shared_ref[size - 8 :, :]
        pre = taps_of(shared_extended, size, shared_chan_ref[...], shared_chan_ref[4:5, :])
        active = pre * jax.nn.sigmoid(pre)
        keys, read = halves(active[:, :NST]), halves(active[:, NST:])
        meet[...] = product(read, keys, 1)
        read_high[...], read_low[...] = read
        keys_high[...], keys_low[...] = halves(active[:, :NST].T)
        delta, _, running = step_sizes(step_ref[...], head_ref[...])
        for k, (d, r) in enumerate(zip(thirds(delta), thirds(running))):
            delta_all[k] = d
            run_all[k] = r
        run_rows[...] = running.T
        square_ref[...] = jnp.zeros_like(square_ref)

    chan = chan_ref[...]
    extended[0:8, :] = tails[pair]
    extended[8:, :] = x_ref[...]
    tails[pair] = x_ref[size - 8 :, :]
    pre = taps_of(extended, size, chan, chan[4:5])
    values = pre * jax.nn.sigmoid(pre)
    lanes = lane_of_head(pair, base)
    delta = spread([delta_all[k] for k in range(3)], lanes)
    running = spread([run_all[k] for k in range(3)], lanes)
    stepped = delta * values
    stepped_halves = halves(stepped)
    mid = size // 2
    top, bottom, sources = [], [], []
    for side in range(2):
        column = running[:, side * HDIM : side * HDIM + 1]
        row = run_rows[pl.ds(base + 2 * pair + side, 1), :]
        first, below, second = decays(column, row, False)
        top.append(halves(first * meet[:mid, :mid]))
        bottom.append(
            (halves(below * meet[mid:, :mid]), halves(second * meet[mid:, mid:]))
        )
        sources.append(own_lanes(stepped_halves, side))
    joined = lambda parts, axis: tuple(jnp.concatenate(p, axis=axis) for p in zip(*parts))
    upper = product(joined(top, 1), joined([tuple(p[:mid] for p in x) for x in sources], 0))
    lower = product(joined([joined(b, 1) for b in bottom], 1), joined(sources, 0))
    local = jnp.concatenate([upper, lower], axis=0)
    state = states[pair]
    state_ref[0, 0] = state
    carried = product((read_high[...], read_low[...]), halves(state))
    scanned = local + jnp.exp(running) * carried
    last = running[size - 1 :, :]
    tail = halves(stepped * jnp.exp(last - running))
    states[pair] = jnp.exp(last) * state + product((keys_high[...], keys_low[...]), tail)
    mixed = scanned + chan[5:6] * values
    z = z_ref[...]
    gated = mixed * (z * jax.nn.sigmoid(z))
    mixed_ref[...] = mixed
    gated_ref[...] = gated
    square_ref[...] += gated * gated


def gate_kernel(
    z_ref, gated_ref, mixed_ref, up_ref, chan_ref, stats_ref,
    z_grad_ref, mix_grad_ref, square_ref, gain_grad_ref,
):
    @pl.when(pl.program_id(0) == 0)
    def _():
        gain_grad_ref[...] = jnp.zeros_like(gain_grad_ref)

    stats = stats_ref[...].T
    scale, pull = stats[:, 0:1], stats[:, 1:2]
    z, gated = z_ref[...], gated_ref[...]
    scaled = up_ref[...] * scale
    z_gain = jax.nn.sigmoid(z)
    gated_grad = scaled * chan_ref[6:7, :] - gated * pull
    z_gate = gated_grad * z_gain
    mix_grad_ref[...] = z_gate * z
    z_grad = (z_gate * mixed_ref[...] * (1.0 + z * (1.0 - z_gain))).astype(z_grad_ref.dtype)
    z_grad_ref[...] = z_grad
    wide_grad = z_grad.astype(jnp.float32)
    square_ref[...] = jnp.sum(wide_grad * wide_grad, axis=1, keepdims=True)
    gain_grad_ref[0:1, :] += jnp.sum(scaled * gated, axis=0, keepdims=True)


def backward_kernel(
    start, chunks, table_ref, x_ref, x_before_ref, shared_ref, shared_before_ref, step_ref, chan_ref, shared_chan_ref, head_ref,
    mixed_ref, mix_grad_ref, state_ref, state_after_ref, carried_in, *refs
):
    carried_in = (carried_in,) + refs[:5]
    (
        x_grad_ref, square_ref, shared_grad_ref,
        state_grads, heads_after, shared_after, chan_grad_ref, shared_chan_grad_ref, head_grad_ref,
        extended, shared_extended, later, shared_later, shared_pre,
        meet, read_high, read_low, keys_high, keys_low, read_rows_high, read_rows_low,
        delta_all, change_all, run_all, run_rows, meet_grad, keys_grad, read_grad, run_grad, delta_grad, last_grad,
    ) = refs[-31:]
    carried_out = (state_grads, heads_after, shared_after, chan_grad_ref, shared_chan_grad_ref, head_grad_ref)
    turn, pair, pairs = pl.program_id(0), pl.program_id(1), pl.num_programs(1)
    first = turn == start
    size = x_ref.shape[0]
    base = table_ref[chunks]

    @pl.when(pair == 0)
    def _():
        @pl.when(turn == 0)
        def _():
            for new, old in zip(carried_out, carried_in):
                new[...] = old[...]

        shared_extended[0:8, :] = jnp.where(first, 0.0, shared_before_ref[...])
        shared_extended[8:, :] = shared_ref[...]
        pre = taps_of(shared_extended, size, shared_chan_ref[...], shared_chan_ref[4:5, :])
        shared_pre[...] = pre
        active = pre * jax.nn.sigmoid(pre)
        keys, read = halves(active[:, :NST]), halves(active[:, NST:])
        meet[...] = product(keys, read, 1)
        read_high[...], read_low[...] = read
        keys_high[...], keys_low[...] = keys
        read_rows_high[...], read_rows_low[...] = halves(active[:, NST:].T)
        delta, change, running = step_sizes(step_ref[...], head_ref[...])
        for k, (d, r) in enumerate(zip(thirds(delta), thirds(running))):
            delta_all[k] = d
            run_all[k] = r
        change_all[...] = change
        run_rows[...] = running.T
        meet_grad[...] = jnp.zeros_like(meet_grad)
        keys_grad[...] = jnp.zeros_like(keys_grad)
        read_grad[...] = jnp.zeros_like(read_grad)
        run_grad[...] = jnp.zeros_like(run_grad)
        delta_grad[...] = jnp.zeros_like(delta_grad)
        last_grad[...] = jnp.zeros_like(last_grad)
        square_ref[...] = jnp.zeros_like(square_ref)

    chan = chan_ref[...]
    extended[0:8, :] = jnp.where(first, 0.0, x_before_ref[...])
    extended[8:, :] = x_ref[...]
    pre = taps_of(extended, size, chan, chan[4:5])
    gain = jax.nn.sigmoid(pre)
    values = pre * gain
    lanes = lane_of_head(pair, base)
    delta = spread([delta_all[k] for k in range(3)], lanes)
    running = spread([run_all[k] for k in range(3)], lanes)
    stepped = delta * values

    mixed, mix_grad = mixed_ref[...], mix_grad_ref[...]
    last = running[size - 1 :, :]
    fall = jnp.exp(last - running)
    rise = jnp.exp(running)
    state, state_grad = state_ref[0, 0], state_grads[pair]
    state_halves, state_grad_halves = halves(state), halves(state_grad)
    keys = (keys_high[...], keys_low[...])
    stepped_grad = fall * product(keys, state_grad_halves)
    keys_grad[...] += product(halves(stepped * fall), state_grad_halves, 1)
    risen = halves(mix_grad * rise)
    read_grad[...] += product(risen, state_halves, 1)
    ended = jnp.sum(state_grad * state_after_ref[0, 0], axis=0, keepdims=True)
    state_grads[pair] = jnp.exp(last) * state_grad + product((read_rows_high[...], read_rows_low[...]), risen)

    mid = size // 2
    grad_halves, stepped_halves = halves(mix_grad), halves(stepped)
    early, late = slice(0, mid), slice(mid, size)
    joined = lambda parts, axis: tuple(jnp.concatenate(p, axis=axis) for p in zip(*parts))
    top, bottom, sources = [], [], []
    first_grad = side_grad = second_grad = 0.0
    for side in range(2):
        column = running[:, side * HDIM : side * HDIM + 1]
        row = run_rows[pl.ds(base + 2 * pair + side, 1), :]
        first, beside, second = decays(column, row, True)
        top.append((halves(first * meet[early, early]), halves(beside * meet[early, late])))
        bottom.append(halves(second * meet[late, late]))
        sources.append(own_lanes(grad_halves, side))
        mine = own_lanes(stepped_halves, side)
        wide_grad = product(tuple(p[early] for p in mine), grad_halves, 1)
        first_grad += first * wide_grad[:, early]
        side_grad += beside * wide_grad[:, late]
        second_grad += second * product(tuple(p[late] for p in mine), tuple(p[late] for p in grad_halves), 1)
    meet_grad[early, early] += first_grad
    meet_grad[early, late] += side_grad
    meet_grad[late, late] += second_grad
    upper = product(joined([joined(t, 1) for t in top], 1), joined(sources, 0))
    lower = product(joined(bottom, 1), joined([tuple(p[late] for p in x) for x in sources], 0))
    stepped_grad = stepped_grad + jnp.concatenate([upper, lower], axis=0)
    to_head = lane_of_head(pair, base, transposed=True)
    scanned = mixed - chan[5:6] * values
    run_grad[...] += spread(halves(mix_grad * scanned - stepped * stepped_grad), to_head)
    delta_grad[...] += spread(halves(values * stepped_grad), to_head)
    last_grad[...] += spread(thirds(jnp.broadcast_to(ended, (8, LANES))), to_head)

    values_grad = chan[5:6] * mix_grad + delta * stepped_grad
    pre_grad = values_grad * (gain * (1.0 + pre * (1.0 - gain)))
    later[0:size, :] = pre_grad
    later[size:, :] = heads_after[pair]
    heads_after[pair] = pre_grad[0:8]
    x_grad = chan[0:1] * later[pl.ds(CONVW - 1, size), :]
    for index in range(1, CONVW):
        x_grad = x_grad + chan[index : index + 1] * later[pl.ds(CONVW - 1 - index, size), :]
    x_grad = x_grad.astype(x_grad_ref.dtype)
    x_grad_ref[:, pl.ds(pl.multiple_of(pair * LANES, LANES), LANES)] = x_grad
    wide_grad = x_grad.astype(jnp.float32)
    square_ref[...] += wide_grad * wide_grad
    for index in range(CONVW):
        seen = extended[pl.ds(8 - CONVW + 1 + index, size), :]
        chan_grad_ref[pair, index : index + 1, :] += jnp.sum(pre_grad * seen, axis=0, keepdims=True)
    chan_grad_ref[pair, 4:5, :] += jnp.sum(pre_grad, axis=0, keepdims=True)
    chan_grad_ref[pair, 5:6, :] += jnp.sum(mix_grad * values, axis=0, keepdims=True)

    @pl.when(pair == pairs - 1)
    def _():
        meet_halves = halves(meet_grad[...])
        keys_all = keys_grad[...] + product(meet_halves, (read_high[...], read_low[...]))
        read_all = read_grad[...] + product(halves(meet_grad[...].T), (keys_high[...], keys_low[...]))
        pre_s = shared_pre[...]
        gain_s = jax.nn.sigmoid(pre_s)
        chan_s = shared_chan_ref[...]
        grad_s = jnp.concatenate([keys_all, read_all], axis=1) * (gain_s * (1.0 + pre_s * (1.0 - gain_s)))
        shared_later[0:size, :] = grad_s
        shared_later[size:, :] = shared_after[...]
        shared_after[...] = grad_s[0:8]
        out = chan_s[0:1] * shared_later[pl.ds(CONVW - 1, size), :]
        for index in range(1, CONVW):
            out = out + chan_s[index : index + 1] * shared_later[pl.ds(CONVW - 1 - index, size), :]
        shared_grad_ref[...] = out
        for index in range(CONVW):
            seen = shared_extended[pl.ds(8 - CONVW + 1 + index, size), :]
            shared_chan_grad_ref[index : index + 1, :] += jnp.sum(grad_s * seen, axis=0, keepdims=True)
        shared_chan_grad_ref[4:5, :] += jnp.sum(grad_s, axis=0, keepdims=True)

        above = lax.broadcasted_iota(jnp.int32, (size, size), 0) <= lax.broadcasted_iota(jnp.int32, (size, size), 1)
        change_grad = running_sum(above, run_grad[...]) + last_grad[0:1, :]
        rate = jnp.exp(head_ref[1:2, :])
        raw = step_ref[...] + head_ref[0:1, :]
        raw_grad = (delta_grad[...] - change_grad * rate) * jax.nn.sigmoid(raw)
        raw_low = raw_grad.astype(x_grad_ref.dtype)
        x_grad_ref[:, x_grad_ref.shape[1] - LANES :] = raw_low
        wide_raw = raw_low.astype(jnp.float32)
        square_ref[...] += wide_raw * wide_raw
        head_grad_ref[0:1, :] += jnp.sum(raw_grad, axis=0, keepdims=True)
        head_grad_ref[1:2, :] += jnp.sum(change_grad * change_all[...], axis=0, keepdims=True)


def run_forward(table, projected, chan, shared_chan, head_rows):
    length, wide = projected.shape[0], chan.shape[1]
    chunks, pairs = length // SPAN, wide // LANES
    f32 = jnp.float32
    block = pl.BlockSpec((SPAN, LANES), lambda c, p, t: (t[c], p))
    return pl.pallas_call(
        forward_kernel,
        grid_spec=pltpu.PrefetchScalarGridSpec(
            num_scalar_prefetch=1,
            grid=(chunks, pairs),
            in_specs=[
                block,
                pl.BlockSpec((SPAN, LANES), lambda c, p, t: (t[c], pairs + 2 + p)),
                pl.BlockSpec((SPAN, 2 * NST), lambda c, p, t: (t[c], pairs // 2)),
                pl.BlockSpec((SPAN, LANES), lambda c, p, t: (t[c], 2 * pairs + 2)),
                pl.BlockSpec((8, LANES), lambda c, p, t: (0, p)),
                pl.BlockSpec((8, 2 * NST), lambda c, p, t: (0, 0)),
                pl.BlockSpec((8, LANES), lambda c, p, t: (0, 0)),
            ],
            out_specs=[
                block,
                block,
                pl.BlockSpec((1, 1, NST, LANES), lambda c, p, t: (c, p, 0, 0)),
                pl.BlockSpec((SPAN, LANES), lambda c, p, t: (t[c], 0)),
            ],
            scratch_shapes=[
                pltpu.VMEM((pairs, 8, LANES), f32),
                pltpu.VMEM((8, 2 * NST), f32),
                pltpu.VMEM((pairs, NST, LANES), f32),
                pltpu.VMEM((SPAN + 8, LANES), f32),
                pltpu.VMEM((SPAN + 8, 2 * NST), f32),
                pltpu.VMEM((SPAN, SPAN), f32),
                pltpu.VMEM((SPAN, NST), low),
                pltpu.VMEM((SPAN, NST), low),
                pltpu.VMEM((NST, SPAN), low),
                pltpu.VMEM((NST, SPAN), low),
                pltpu.VMEM((3, SPAN, LANES), low),
                pltpu.VMEM((3, SPAN, LANES), low),
                pltpu.VMEM((LANES, SPAN), f32),
            ],
        ),
        out_shape=[
            jax.ShapeDtypeStruct((length, wide), f32),
            jax.ShapeDtypeStruct((length, wide), f32),
            jax.ShapeDtypeStruct((chunks, pairs, NST, LANES), f32),
            jax.ShapeDtypeStruct((length, LANES), f32),
        ],
        compiler_params=pltpu.CompilerParams(vmem_limit_bytes=20 * MIB),
        name="mixer_forward",
    )(table, projected, projected, projected, projected, chan, shared_chan, head_rows)


def run_gate(projected, gated, mixed, up, chan, stats):
    length, wide = gated.shape
    f32 = jnp.float32
    size = SPAN
    block = pl.BlockSpec((size, wide), lambda c: (c, 0))
    whole = pl.BlockSpec((8, wide), lambda c: (0, 0))
    return pl.pallas_call(
        gate_kernel,
        grid=(length // size,),
        in_specs=[block, block, block, block, whole, pl.BlockSpec((8, size), lambda c: (0, c))],
        out_specs=[block, block, pl.BlockSpec((size, 1), lambda c: (c, 0)), whole],
        out_shape=[
            jax.ShapeDtypeStruct((length, wide), low),
            jax.ShapeDtypeStruct((length, wide), f32),
            jax.ShapeDtypeStruct((length, 1), f32),
            jax.ShapeDtypeStruct((8, wide), f32),
        ],
        compiler_params=pltpu.CompilerParams(vmem_limit_bytes=20 * MIB),
        name="gate_backward",
    )(projected, gated, mixed, up, chan, stats)


def run_backward(start, count, table, projected, chan, shared_chan, head_rows, mixed, mix_grad, states, carried, before):
    length, wide = projected.shape[0], chan.shape[1]
    chunks, pairs = length // SPAN, wide // LANES
    f32 = jnp.float32
    lines = SPAN // 8
    earlier = lambda c: jnp.maximum(start - c - 1, 0)
    following = lambda c: jnp.minimum(start - c + 1, chunks - 1)
    block = pl.BlockSpec((SPAN, LANES), lambda c, p, t: (t[start - c], p))
    flat = pl.BlockSpec((8, 2 * NST), lambda c, p, t: (0, 0))
    head = pl.BlockSpec((8, LANES), lambda c, p, t: (0, 0))
    carries = [
        pl.BlockSpec((pairs, NST, LANES), lambda c, p, t: (0, 0, 0)),
        pl.BlockSpec((pairs, 8, LANES), lambda c, p, t: (0, 0, 0)),
        flat,
        pl.BlockSpec((pairs, 8, LANES), lambda c, p, t: (0, 0, 0)),
        flat,
        head,
    ]
    carried_shapes = [jax.ShapeDtypeStruct(c.shape, f32) for c in carried]
    return pl.pallas_call(
        functools.partial(backward_kernel, start, chunks),
        grid_spec=pltpu.PrefetchScalarGridSpec(
            num_scalar_prefetch=1,
            grid=(count, pairs),
            in_specs=[
                pl.BlockSpec((SPAN, LANES), lambda c, p, t: (t[start - c], pairs + 2 + p)),
                pl.BlockSpec((8, LANES), lambda c, p, t: (t[earlier(c)] * lines + lines - 1, pairs + 2 + p)),
                pl.BlockSpec((SPAN, 2 * NST), lambda c, p, t: (t[start - c], pairs // 2)),
                pl.BlockSpec((8, 2 * NST), lambda c, p, t: (t[earlier(c)] * lines + lines - 1, pairs // 2)),
                pl.BlockSpec((SPAN, LANES), lambda c, p, t: (t[start - c], 2 * pairs + 2)),
                pl.BlockSpec((8, LANES), lambda c, p, t: (0, p)),
                flat,
                head,
                block,
                block,
                pl.BlockSpec((1, 1, NST, LANES), lambda c, p, t: (start - c, p, 0, 0)),
                pl.BlockSpec((1, 1, NST, LANES), lambda c, p, t: (following(c), p, 0, 0)),
            ]
            + carries
            + [pl.BlockSpec(memory_space=pl.ANY)] * len(before),
            out_specs=[
                pl.BlockSpec((SPAN, wide + LANES), lambda c, p, t: (t[start - c], 0)),
                pl.BlockSpec((SPAN, LANES), lambda c, p, t: (t[start - c], 0)),
                pl.BlockSpec((SPAN, 2 * NST), lambda c, p, t: (t[start - c], 0)),
            ]
            + carries,
            scratch_shapes=[
                pltpu.VMEM((SPAN + 8, LANES), f32),
                pltpu.VMEM((SPAN + 8, 2 * NST), f32),
                pltpu.VMEM((SPAN + 8, LANES), f32),
                pltpu.VMEM((SPAN + 8, 2 * NST), f32),
                pltpu.VMEM((SPAN, 2 * NST), f32),
                pltpu.VMEM((SPAN, SPAN), f32),
                pltpu.VMEM((SPAN, NST), low),
                pltpu.VMEM((SPAN, NST), low),
                pltpu.VMEM((SPAN, NST), low),
                pltpu.VMEM((SPAN, NST), low),
                pltpu.VMEM((NST, SPAN), low),
                pltpu.VMEM((NST, SPAN), low),
                pltpu.VMEM((3, SPAN, LANES), low),
                pltpu.VMEM((SPAN, LANES), f32),
                pltpu.VMEM((3, SPAN, LANES), low),
                pltpu.VMEM((LANES, SPAN), f32),
                pltpu.VMEM((SPAN, SPAN), f32),
                pltpu.VMEM((SPAN, NST), f32),
                pltpu.VMEM((SPAN, NST), f32),
                pltpu.VMEM((SPAN, LANES), f32),
                pltpu.VMEM((SPAN, LANES), f32),
                pltpu.VMEM((8, LANES), f32),
            ],
        ),
        out_shape=[
            jax.ShapeDtypeStruct((length, wide + LANES), low),
            jax.ShapeDtypeStruct((length, LANES), f32),
            jax.ShapeDtypeStruct((length, 2 * NST), f32),
        ]
        + carried_shapes,
        input_output_aliases={19 + k: k for k in range(len(before))},
        compiler_params=pltpu.CompilerParams(vmem_limit_bytes=50 * MIB),
        name="mixer_backward",
    )(
        table, projected, projected, projected, projected, projected, chan, shared_chan, head_rows,
        mixed, mix_grad, states, states, *carried, *before,
    )


def halve(block, left, bit, axis):
    place = left.index(bit)
    own = (lax.axis_index(axis) & bit) // bit
    keep = lax.dynamic_index_in_dim(block, own, place, keepdims=False)
    send = lax.dynamic_index_in_dim(block, 1 - own, place, keepdims=False)
    return keep + swap(send, axis, bit), [b for b in left if b != bit]


class Scatter:
    def __init__(self, arrays, axis, phase=0):
        self.axis = axis
        size = lax.axis_size(axis)
        bits = [1 << k for k in range(size.bit_length() - 1)]
        upper = bits[1:]
        turned = upper[len(upper) // 2 :] + upper[: len(upper) // 2]
        self.orders = [bits[:1] + (upper if (k + phase) % 2 == 0 else turned) for k in range(len(arrays))]
        self.left = [bits[::-1] for _ in arrays]
        self.blocks = [
            a.reshape((2,) * len(bits) + (a.shape[0] // size,) + a.shape[1:]) for a in arrays
        ]
        self.steps = len(bits)
        self.done = 0

    def step(self):
        for k in range(len(self.blocks)):
            self.blocks[k], self.left[k] = halve(
                self.blocks[k], self.left[k], self.orders[k][self.done], self.axis
            )
        self.done += 1

    def finish(self):
        while self.done < self.steps:
            self.step()
        return self.blocks


def update_kernel(
    pieces, widths, rate, decay, slot_ref, source_ref, param_ref, first_ref, second_ref,
    grad_ref, param_out, first_out, second_out,
):
    for piece, width in zip(range(pieces), widths):
        at = sum(widths[:piece])
        own = slice(at, at + width)
        grad = source_ref[slot_ref[piece], :, :width]
        new = adamw_update(param_ref[:, own], grad, first_ref[:, own], second_ref[:, own], rate, decay)
        grad_ref[:, own] = grad
        param_out[:, own], first_out[:, own], second_out[:, own] = new


def run_update(slots, sources, widths, param, first, second, rate, decay):
    rows, total = param.shape
    size = 16 if rows % 16 == 0 else rows
    block = pl.BlockSpec((size, total), lambda r, t: (r, 0))
    return pl.pallas_call(
        functools.partial(update_kernel, len(widths), widths, rate, decay),
        grid_spec=pltpu.PrefetchScalarGridSpec(
            num_scalar_prefetch=1,
            grid=(rows // size,),
            in_specs=[pl.BlockSpec((sources.shape[0], size, sources.shape[2]), lambda r, t: (0, r, 0))] + [block] * 3,
            out_specs=[block] * 4,
        ),
        out_shape=[jax.ShapeDtypeStruct(param.shape, jnp.float32)] * 4,
        compiler_params=pltpu.CompilerParams(vmem_limit_bytes=20 * MIB),
        name="weight_update",
    )(slots, sources, param, first, second)


def adamw_update(param, grad, first, second, rate, decay):
    first_new = beta_one * first + (1.0 - beta_one) * grad
    second_new = beta_two * second + (1.0 - beta_two) * grad * grad
    corrected_first = first_new * (1.0 / (1.0 - beta_one**adam_step))
    corrected_second = second_new * (1.0 / (1.0 - beta_two**adam_step))
    param_new = param - rate * (
        corrected_first / (jnp.sqrt(corrected_second) + adam_eps) + decay * param
    )
    return (param_new, first_new, second_new)


def dot(left, right):
    return jnp.dot(left, right, preferred_element_type=jnp.float32)


def body(
    block_input,
    cotangent,
    norm_gain,
    in_weight,
    conv_weight,
    conv_bias,
    step_bias,
    decay_log,
    skip_gain,
    gated_gain,
    out_weight,
    first_norm_gain,
    second_norm_gain,
    first_in_weight,
    second_in_weight,
    first_conv_weight,
    second_conv_weight,
    first_conv_bias,
    second_conv_bias,
    first_step_bias,
    second_step_bias,
    first_decay_log,
    second_decay_log,
    first_skip_gain,
    second_skip_gain,
    first_gated_gain,
    second_gated_gain,
    first_out_weight,
    second_out_weight,
):
    ranks, rank = lax.axis_size(SEQ), lax.axis_index(SEQ)
    groups = lax.axis_size(DP)
    devices = ranks * groups
    wide, heads = E // ranks, NHEADS // ranks
    rows = in_weight.shape[0]
    width = rows * devices
    taps = conv_bias.shape[0]
    channels = taps * devices
    step_at = 2 * E + 2 * NST
    spare = LANES - (in_weight.shape[1] - step_at)

    packed = jnp.concatenate(
        [norm_gain, conv_weight.reshape(-1), conv_bias, gated_gain]
    ).astype(low).astype(jnp.float32)
    gains = gated_gain.shape[0]
    filled = packed.shape[0]
    lines = -(-filled // LANES)
    packed = jnp.pad(packed, (0, lines * LANES - filled)).reshape(lines, LANES)
    small_line = gather_direct(packed, SEQ)
    small = gather_bits(small_line, DP)
    small = small.reshape(devices, lines * LANES)
    norm_float = small[:, :rows].reshape(-1)
    kernel_float = small[:, rows : rows + CONVW * taps].reshape(devices, CONVW, taps)
    kernel_float = kernel_float.transpose(1, 0, 2).reshape(CONVW, channels)
    offset_float = small[:, rows + CONVW * taps : rows + (CONVW + 1) * taps].reshape(-1)
    gated_float = small[:, rows + (CONVW + 1) * taps : filled].reshape(-1)
    kernel_own = lax.dynamic_slice_in_dim(kernel_float, rank * wide, wide, 1)
    offset_own = lax.dynamic_slice_in_dim(offset_float, rank * wide, wide, 0)
    gated_own = lax.dynamic_slice_in_dim(gated_float, rank * wide, wide, 0)
    skip_own = lax.dynamic_slice_in_dim(skip_gain, rank * heads, heads, 0)

    in_low = in_weight.astype(low)
    out_low = out_weight.astype(low)

    def for_rank(j):
        return jnp.concatenate(
            [
                lax.dynamic_slice_in_dim(in_low, j * wide, wide, 1),
                in_low[:, 2 * E : step_at],
                lax.dynamic_slice_in_dim(in_low, E + j * wide, wide, 1),
                jnp.pad(in_low[:, step_at:], ((0, 0), (0, spare))),
                lax.dynamic_slice_in_dim(out_low, j * wide, wide, 1),
            ],
            axis=1,
        )

    columns = 2 * NST + 2 * wide + LANES
    weights_arrived = []
    for turn in range(1, ranks):
        weights_arrived.append(shift(for_rank((rank + turn) % ranks), SEQ, turn))

    tokens, upstream = block_input[0], cotangent[0]
    span = tokens.shape[0]
    length = span * ranks
    inverse = lax.rsqrt(jnp.mean(tokens * tokens, axis=-1, keepdims=True) + norm_eps)
    hidden_own = (tokens * inverse * norm_float).astype(low)
    weights_arrived = [after(part, hidden_own) for part in weights_arrived]
    weight_rows = jnp.zeros((ranks, rows, columns + wide), low)
    weight_rows = lax.dynamic_update_index_in_dim(weight_rows, for_rank(rank), rank, 0)
    for turn in range(1, ranks):
        weight_rows = lax.dynamic_update_index_in_dim(
            weight_rows, weights_arrived[turn - 1], (rank + ranks - turn) % ranks, 0
        )
    weight_rows = weight_rows.reshape(ranks * rows, columns + wide)
    in_full, out_full = gather_rows([weight_rows[:, :columns], weight_rows[:, columns:]], DP)

    line_parts = near_parts(hidden_own, SEQ)
    line_parts = [after(part, in_full, out_full) for part in line_parts]
    up_parts = near_parts(after(upstream.astype(low), *line_parts), SEQ)
    hidden = jnp.stack(line_parts).reshape(length, width)

    projected = dot(hidden, in_full)
    none = jnp.zeros((1, wide), jnp.float32)
    chan = jnp.concatenate(
        [kernel_own, offset_own[None], jnp.repeat(skip_own, HDIM)[None], gated_own[None], none], axis=0
    )
    shared_chan = jnp.concatenate(
        [kernel_float[:, E:], offset_float[None, E:], jnp.zeros((3, 2 * NST), jnp.float32)], axis=0
    )
    head_rows = jnp.pad(jnp.stack([step_bias, decay_log]), ((0, 6), (0, LANES - NHEADS)))
    pairs, chunks = wide // LANES, length // SPAN
    per_rank = span // SPAN
    order = jnp.arange(chunks, dtype=jnp.int32)
    order = (rank + ranks - order // per_rank) % ranks * per_rank + order % per_rank
    table = jnp.concatenate([order, jnp.reshape(rank * heads, (1,))]).astype(jnp.int32)
    zeros = functools.partial(jnp.zeros, dtype=jnp.float32)
    gated, mixed, states, squares = run_forward(table, projected, chan, shared_chan, head_rows)
    packed_length = (ranks, span // LANES, LANES)
    square_sum = sum_near(jnp.sum(squares, axis=1).reshape(packed_length), SEQ).reshape(length)
    scale = lax.rsqrt(square_sum / E + norm_eps)
    normed_low = (gated * scale[:, None] * gated_own).astype(low)
    branch_factor = 2.0 ** (14 - math.ceil(math.log2(0.17 * math.sqrt(E * wide))))
    out_half = (dot(normed_low, out_full.T) * branch_factor).astype(half).reshape(ranks, span, width)

    upstream_low = jnp.stack([after(part, out_half) for part in up_parts]).reshape(length, width)
    normed_grad = dot(upstream_low, out_full)
    pull_sum = jnp.sum(normed_grad * gated_own * gated, axis=1).reshape(packed_length)
    pull_sum = sum_near(pull_sum, SEQ).reshape(length)
    stats = jnp.stack([scale, scale * scale * scale * (pull_sum / E)])
    stats = jnp.pad(stats, ((0, 6), (0, 0)))
    out_grad_part = dot(upstream_low.T, normed_low)
    out_scatter = Scatter([out_grad_part], DP)
    out_scatter.step()
    gate_low, mix_grad, gate_square, gain_rows = run_gate(projected, gated, mixed, normed_grad, chan, stats)
    gated_grad = gain_rows[0]

    branch_parts = send_near(out_half, SEQ)

    gate_scatter = Scatter([dot(hidden.T, gate_low)], DP, 1)
    gate_scatter.step()
    carried = (
        zeros((pairs, NST, LANES)), zeros((pairs, 8, LANES)), zeros((8, 2 * NST)),
        zeros((pairs, 8, LANES)), zeros((8, 2 * NST)), zeros((8, LANES)),
    )
    outputs, early = (), (out_scatter, gate_scatter)
    calls = [(chunks - 1, chunks - 2 * (chunks // 4)), (2 * (chunks // 4) - 1, chunks // 4), (chunks // 4 - 1, chunks // 4)]
    for turn, (start, count) in enumerate(calls):
        ready = tuple(scatter.blocks[0] for scatter in early)
        if turn < len(calls) - 1:
            for scatter in early:
                if scatter.done < scatter.steps:
                    scatter.step()
        else:
            early_sums = jnp.concatenate(
                [block.reshape(ranks, rows, wide) for scatter in early for block in scatter.finish()], axis=2
            )
            early_packed = pack_half(early_sums, jnp.max(jnp.abs(early_sums), axis=-1, keepdims=True))
            early_slots = slots_of(early_sums, early_packed, SEQ)
            ready = (early_packed,)
        mix_grad = after(mix_grad, *ready)
        result = run_backward(
            start, count, table, projected, chan, shared_chan, head_rows, mixed, mix_grad, states, carried, outputs
        )
        outputs, carried = tuple(result[:3]), tuple(result[3:])
    conv_low, conv_square, shared_grad = outputs
    _, _, _, chan_grad, shared_chan_grad, head_grad = carried

    largest = jnp.max(gate_square.reshape(ranks, span) + jnp.sum(conv_square.reshape(ranks, span, LANES), axis=2), axis=1)
    bound = 0.1565 * math.sqrt(2 * wide + NHEADS) * jnp.sqrt(largest)
    power = jnp.clip(jnp.ceil(jnp.log2(bound)) - 14.0, -120.0, 120.0)
    shared_parts = shared_grad.reshape(ranks, span, 2 * NST)
    lines_of_power = jnp.broadcast_to(power[:, None, None], (ranks, 8, 2 * NST))
    shared_sent = send_near(jnp.concatenate([shared_parts, lines_of_power], axis=1), SEQ)

    factors = jnp.exp2(-power)[:, None, None]
    hidden_part = dot(gate_low, in_full[:, :wide].T) + dot(conv_low, in_full[:, wide + 2 * NST :].T)
    hidden_part = hidden_part.reshape(ranks, span, width)
    hidden_half = (hidden_part * factors).astype(half)
    hidden_parts = send_near(hidden_half, SEQ)

    split = 4 * LANES
    conv_parts = [dot(hidden.T, conv_low[:, :split]), dot(hidden.T, conv_low[:, split:])]
    late = Scatter(conv_parts, DP)
    normed_own = normed_low[:span]
    for turn in range(late.steps):
        if turn == 1:
            normed_own = after(normed_own, *late.blocks)
            early_slots = [after(part, *late.blocks) for part in early_slots]
            chan_grad, shared_chan_grad, head_grad = (
                after(part, *late.blocks) for part in (chan_grad, shared_chan_grad, head_grad)
            )
        late.step()
    shared_own = shared_parts[0]
    for part in shared_sent:
        shared_own = shared_own + part[:span]
    shared_own = shared_own.astype(low)
    shared_grad_part = dot(hidden_own.T, shared_own)
    last = Scatter([shared_grad_part], DP, 1)
    for turn in range(last.steps):
        if turn == last.steps - 1:
            hidden_parts = [after(part, *last.blocks) for part in hidden_parts]
            power_parts = [after(part, *last.blocks)[span, 0] for part in shared_sent]
        last.step()
    hidden_grad = hidden_part[0] + dot(shared_own, in_full[:, wide : wide + 2 * NST].T)
    branch = tokens + dot(normed_own, out_full.T)
    for part in branch_parts:
        branch = branch + part.astype(jnp.float32) * (1.0 / branch_factor)
    block_output = branch[None]

    chan_grad = chan_grad.transpose(1, 0, 2).reshape(8, wide)
    kernel_grad, offset_grad = chan_grad[:CONVW], chan_grad[4]
    skip_grad = jnp.sum(chan_grad[5].reshape(heads, HDIM), axis=1)
    kernel_shared_grad, offset_shared_grad = shared_chan_grad[:CONVW], shared_chan_grad[4]

    late_sums = jnp.concatenate([block.reshape(ranks, rows, -1) for block in late.blocks + last.blocks], axis=2)
    late_packed = pack_half(late_sums, jnp.max(jnp.abs(late_sums), axis=-1, keepdims=True))
    late_slots = slots_of(late_sums, late_packed, SEQ)

    for part, exponent in zip(hidden_parts, power_parts):
        hidden_grad = hidden_grad + part.astype(jnp.float32) * jnp.exp2(exponent)
    scaled = tokens * inverse
    gain_grad = jnp.sum(hidden_grad * scaled, axis=0)
    inner = hidden_grad * norm_float
    token_grad = inverse * (inner - scaled * jnp.mean(inner * scaled, axis=-1, keepdims=True))
    input_grad = (upstream + token_grad)[None]

    def placed(own, shared):
        full = jnp.zeros(own.shape[:-1] + (E,), jnp.float32)
        full = lax.dynamic_update_slice_in_dim(full, own, rank * wide, own.ndim - 1)
        return jnp.concatenate([full, shared], axis=-1)

    kernel_all = placed(kernel_grad, kernel_shared_grad).reshape(CONVW, devices, taps)
    kernel_all = kernel_all.transpose(1, 0, 2).reshape(devices, CONVW * taps)
    offset_all = placed(offset_grad, offset_shared_grad).reshape(devices, taps)
    gated_all = lax.dynamic_update_slice_in_dim(jnp.zeros((E,), jnp.float32), gated_grad, rank * wide, 0)
    skip_all = lax.dynamic_update_slice_in_dim(jnp.zeros((NHEADS,), jnp.float32), skip_grad, rank * heads, 0)
    head_all = jnp.concatenate([head_grad[0, :NHEADS], head_grad[1, :NHEADS], skip_all])
    terms = jnp.concatenate(
        [
            kernel_all,
            offset_all,
            gated_all.reshape(devices, gains),
            jnp.broadcast_to(head_all[None], (devices, 3 * NHEADS)),
        ],
        axis=1,
    )
    used = terms.shape[1]
    term_lines = -(-used // LANES)
    terms = jnp.pad(terms, ((0, 0), (0, term_lines * LANES - used)))
    terms = terms.reshape(groups, ranks, term_lines, LANES)
    norm_lines = -(-rows // LANES)
    norm_terms = jnp.pad(gain_grad.reshape(devices, rows), ((0, 0), (0, norm_lines * LANES - rows)))
    norm_terms = norm_terms.reshape(groups, ranks, norm_lines, LANES)
    term_lines += norm_lines
    terms = jnp.concatenate([norm_terms, terms], axis=2).reshape(groups, ranks * term_lines, LANES)
    small_scatter = Scatter([terms], DP)
    for _ in range(small_scatter.steps):
        small_scatter.step()
    summed = small_scatter.blocks[0].reshape(ranks, term_lines, LANES)
    summed = exchange_sum(summed, SEQ).reshape(-1)
    grad_norm_gain = summed[:rows]
    at = norm_lines * LANES
    grad_conv_weight = summed[at : at + CONVW * taps].reshape(CONVW, taps)
    at += CONVW * taps
    grad_conv_bias = summed[at : at + taps]
    at += taps
    grad_gated_gain = summed[at : at + gains]
    at += gains
    grad_step_bias, grad_decay_log, grad_skip_gain = (
        summed[at + k * NHEADS : at + (k + 1) * NHEADS] for k in range(3)
    )
    new_norm_gain, new_first_norm_gain, new_second_norm_gain = adamw_update(
        norm_gain, grad_norm_gain, first_norm_gain, second_norm_gain, rate_vector, 0.0
    )
    place = (rank + ranks - jnp.arange(ranks, dtype=jnp.int32)) % ranks
    early_f32 = early_slots[:1] + list(unpack_half(jnp.stack(early_slots[1:])))
    late_f32 = late_slots[:1] + list(unpack_half(jnp.stack(late_slots[1:])))
    shared_sum = late_f32[0][:, wide:]
    for part in late_f32[1:]:
        shared_sum = shared_sum + part[:, wide:]
    shared_sum = jnp.concatenate([shared_sum[:, LANES:], shared_sum[:, :LANES]], axis=1)
    sources = jnp.stack(
        [part[:, wide:] for part in early_f32]
        + [part[:, :wide] for part in late_f32]
        + [jnp.pad(shared_sum, ((0, 0), (0, wide - shared_sum.shape[1])))]
    )
    slots = jnp.concatenate([place, place + ranks, jnp.full((1,), 2 * ranks)]).astype(jnp.int32)
    widths = (wide,) * (2 * ranks) + (in_weight.shape[1] - 2 * E,)
    grad_in_weight, new_in_weight, new_first_in_weight, new_second_in_weight = run_update(
        slots, sources, widths, in_weight, first_in_weight, second_in_weight, rate_matrix, weight_decay
    )
    new_conv_weight, new_first_conv_weight, new_second_conv_weight = adamw_update(
        conv_weight, grad_conv_weight, first_conv_weight, second_conv_weight, rate_vector, 0.0
    )
    new_conv_bias, new_first_conv_bias, new_second_conv_bias = adamw_update(
        conv_bias, grad_conv_bias, first_conv_bias, second_conv_bias, rate_vector, 0.0
    )
    new_step_bias, new_first_step_bias, new_second_step_bias = adamw_update(
        step_bias, grad_step_bias, first_step_bias, second_step_bias, rate_vector, 0.0
    )
    new_decay_log, new_first_decay_log, new_second_decay_log = adamw_update(
        decay_log, grad_decay_log, first_decay_log, second_decay_log, rate_vector, 0.0
    )
    new_skip_gain, new_first_skip_gain, new_second_skip_gain = adamw_update(
        skip_gain, grad_skip_gain, first_skip_gain, second_skip_gain, rate_vector, 0.0
    )
    new_gated_gain, new_first_gated_gain, new_second_gated_gain = adamw_update(
        gated_gain, grad_gated_gain, first_gated_gain, second_gated_gain, rate_vector, 0.0
    )
    grad_out_weight, new_out_weight, new_first_out_weight, new_second_out_weight = run_update(
        place,
        jnp.stack([part[:, :wide] for part in early_f32]),
        (wide,) * ranks,
        out_weight,
        first_out_weight,
        second_out_weight,
        rate_matrix,
        weight_decay,
    )

    return (
        block_output,
        input_grad,
        grad_norm_gain,
        grad_in_weight,
        grad_conv_weight,
        grad_conv_bias,
        grad_step_bias,
        grad_decay_log,
        grad_skip_gain,
        grad_gated_gain,
        grad_out_weight,
        new_norm_gain,
        new_first_norm_gain,
        new_second_norm_gain,
        new_in_weight,
        new_first_in_weight,
        new_second_in_weight,
        new_conv_weight,
        new_first_conv_weight,
        new_second_conv_weight,
        new_conv_bias,
        new_first_conv_bias,
        new_second_conv_bias,
        new_step_bias,
        new_first_step_bias,
        new_second_step_bias,
        new_decay_log,
        new_first_decay_log,
        new_second_decay_log,
        new_skip_gain,
        new_first_skip_gain,
        new_second_skip_gain,
        new_gated_gain,
        new_first_gated_gain,
        new_second_gated_gain,
        new_out_weight,
        new_first_out_weight,
        new_second_out_weight,
    )


def solution(mesh):
    in_specs = (
        P(DP, SEQ, None),
        P(DP, SEQ, None),
        P((DP, SEQ)),
        P((DP, SEQ), None),
        P(None, (DP, SEQ)),
        P((DP, SEQ)),
        P(),
        P(),
        P(),
        P((DP, SEQ)),
        P((DP, SEQ), None),
        P((DP, SEQ)),
        P((DP, SEQ)),
        P((DP, SEQ), None),
        P((DP, SEQ), None),
        P(None, (DP, SEQ)),
        P(None, (DP, SEQ)),
        P((DP, SEQ)),
        P((DP, SEQ)),
        P(),
        P(),
        P(),
        P(),
        P(),
        P(),
        P((DP, SEQ)),
        P((DP, SEQ)),
        P((DP, SEQ), None),
        P((DP, SEQ), None),
    )
    out_specs = (
        P(DP, SEQ, None),
        P(DP, SEQ, None),
        P((DP, SEQ)),
        P((DP, SEQ), None),
        P(None, (DP, SEQ)),
        P((DP, SEQ)),
        P(),
        P(),
        P(),
        P((DP, SEQ)),
        P((DP, SEQ), None),
        P((DP, SEQ)),
        P((DP, SEQ)),
        P((DP, SEQ)),
        P((DP, SEQ), None),
        P((DP, SEQ), None),
        P((DP, SEQ), None),
        P(None, (DP, SEQ)),
        P(None, (DP, SEQ)),
        P(None, (DP, SEQ)),
        P((DP, SEQ)),
        P((DP, SEQ)),
        P((DP, SEQ)),
        P(),
        P(),
        P(),
        P(),
        P(),
        P(),
        P(),
        P(),
        P(),
        P((DP, SEQ)),
        P((DP, SEQ)),
        P((DP, SEQ)),
        P((DP, SEQ), None),
        P((DP, SEQ), None),
        P((DP, SEQ), None),
    )

    return jax.shard_map(body, mesh=mesh, in_specs=in_specs, out_specs=out_specs, check_vma=False)
```
